256 devices in a mesh: head: 8 (over x_hi, y), key: 8 (over z), hid: 4 (over x_lo, core).
Axes of the slice: x: 4 (x_hi: 2, x_lo: 2; x = x_hi * 2 + x_lo), y: 4, z: 8, core: 2. Of those that a mesh axis runs over, the one named last changes fastest.
Arguments:
- tokens: bfloat16 [2048, 8192], P('key', 'hid'), may hold values from -6 to 6
- query_weight: bfloat16 [8192, 8192], P('hid', 'head'), may hold values from -0.0625 to 0.0625
- key_weight: bfloat16 [8192, 1024], P('hid', 'head'), may hold values from -0.0625 to 0.0625
- value_weight: bfloat16 [8192, 1024], P('hid', 'head'), may hold values from -0.0625 to 0.0625
- output_weight: bfloat16 [8192, 8192], P(('head', 'hid')), may hold values from -0.125 to 0.125
- key_cache: bfloat16 [16384, 8, 128], P('key', 'head'), may hold values from -2000 to 2000
- value_cache: bfloat16 [16384, 8, 128], P('key', 'head'), may hold values from -6 to 6
- cache_places: int32 [64], P('key'), may hold values from 1 to 510, as said below
- slab_places: int32 [8], replicated, may hold values from 0 to 511, as said below
Outputs:
- attended: bfloat16 [2048, 8192], P('key', ('head', 'hid'))
The draws below stay inside these ranges and needn't reach their ends.
Inputs may be any that keep to these rules, and one draw needn't show every extreme that they name: The 64 entries of cache_places and the 8 entries of slab_places are all different from one another. `slab_places`: see cache_places: no slab shares a block number with another slab or with a resident block.
All inputs are finite; a program needn't handle non-finite values.
Results may differ from the reference program's by a relative error of at most 0.039.
Values may be sent and summed in bfloat16 or wider, within the bound.
No kernel may reach another device: no remote copies, remote signals or barrier semaphores. Data moves between devices by JAX's collectives and lax.ppermute only.
A program may use at most 128 MiB of HBM per device.

```python
import math
import jax
import jax.numpy as jnp
from jax import lax

D = 8192
H = 64
KVH = 8
HD = 128
SEQ = 131072
TOK_DEV = 256
NSLAB = 8
NQ = 2048
NKB = 64
NK = 16384


def block_spots(key):
    blocks = SEQ // TOK_DEV
    middle = 2 + jax.random.permutation(jax.random.fold_in(key, 11), blocks - 4).astype(jnp.int32)
    cache_part = jnp.concatenate([jnp.array([1, blocks - 2], jnp.int32), middle[:NKB - 2]])
    slab_part = jnp.concatenate([jnp.array([0, blocks - 1], jnp.int32), middle[NKB - 2:NKB - 4 + NSLAB]])
    cache_order = jax.random.permutation(jax.random.fold_in(key, 13), NKB)
    slab_order = jax.random.permutation(jax.random.fold_in(key, 17), NSLAB)
    return (cache_part[cache_order].astype(jnp.int32), slab_part[slab_order].astype(jnp.int32))


def draw_cache_places(key, part):
    return block_spots(key)[0]


def draw_slab_places(key, part):
    return block_spots(key)[1]


def draw_key_cache(key, part):
    normal_base = jnp.clip(jax.random.normal(jax.random.fold_in(key, 3), (NK, KVH, HD), jnp.float32), -6.0, 6.0)
    result = 2.0 * normal_base
    return result.astype(jnp.bfloat16)


def raised(values, rng, source, target, shards_of, factor):
    def block_of(dim):
        return (jnp.arange(values.shape[dim]) // (values.shape[dim] // shards_of)).reshape((-1,) + (1,) * (values.ndim - 1 - dim))

    one_side = jax.random.permutation(rng, shards_of)[block_of(target)]
    second = (block_of(target) + shards_of // 2) % shards_of
    return jnp.where((block_of(source) == one_side) | (block_of(source) == second), factor * values, values)


def steps_of(own_key, extent, shards, low, largest):
    def one(dim, shards_of):
        steps = jax.random.uniform(jax.random.fold_in(jax.random.fold_in(own_key, 6), dim), (shards_of,), jnp.float32, low / len(shards), largest / len(shards))
        return jnp.repeat(jnp.exp(steps), extent[dim] // shards_of).reshape((-1,) + (1,) * (len(extent) - dim - 1))

    factor_of = one(*shards[0])
    for cut in shards[1:]:
        factor_of = factor_of * one(*cut)
    return factor_of


def gaussian(rng, dims, width, reach, split=(), kind=jnp.bfloat16):
    values = jax.random.normal(rng, dims, jnp.float32) * width
    if len(split) > 0:
        values = steps_of(rng, dims, split, -0.22, 0.18) * values
    return jnp.clip(values, min=-reach, max=reach).astype(kind)


def heavy_noise(own_key, dims, scale, most, cuts, heavy, kind=jnp.bfloat16):
    values = scale * jax.random.normal(own_key, dims, jnp.float32)
    if cuts:
        values = values * steps_of(own_key, dims, cuts, -0.22, 0.18)
    return jnp.clip(raised(values, jax.random.fold_in(own_key, 3), *heavy), -most, most).astype(kind)


def setup_inputs(seed: int = 0) -> dict:
    seeds = jax.random.split(jax.random.key(seed), 10)
    return {
        "tokens": gaussian(seeds[0], (NQ, D), 1.0, 6.0, ((0, 8), (1, 4))),
        "query_weight": gaussian(seeds[1], (D, H * HD), D ** -0.5, 0.0625, ((0, 4), (1, 8))),
        "key_weight": gaussian(seeds[2], (D, KVH * HD), D ** -0.5, 0.0625, ((0, 4), (1, 8))),
        "value_weight": gaussian(seeds[3], (D, KVH * HD), D ** -0.5, 0.0625, ((0, 4), (1, 8))),
        "output_weight": heavy_noise(seeds[4], (H * HD, D), (H * HD) ** -0.5, 0.125, ((0, 32),), (0, 1, 32, 2.75)),
        "key_cache": draw_key_cache(jax.random.fold_in(seeds[9], 71), 0),
        "value_cache": gaussian(seeds[6], (NK, KVH, HD), 1.0, 6.0, ((0, 8), (1, 8))),
        "cache_places": draw_cache_places(jax.random.fold_in(seeds[9], 71), 0),
        "slab_places": draw_slab_places(jax.random.fold_in(seeds[9], 71), 0),
    }


THETA = 500000.0
NEGATIVE = -1e+30

def rotate(vectors, spots):
    middle = vectors.shape[-1] // 2
    freq_index = jnp.arange(middle, dtype=jnp.float32)
    frequency = jnp.exp(freq_index * (-2.0 * math.log(THETA) / vectors.shape[-1]))
    angles = spots.astype(jnp.float32)[:, None] * frequency[None, :]
    cosine_part = jnp.cos(angles)[:, None, :]
    sine_part = jnp.sin(angles)[:, None, :]
    leading = vectors[..., :middle]
    trailing = vectors[..., middle:]
    return jnp.concatenate([leading * cosine_part - trailing * sine_part, trailing * cosine_part + leading * sine_part], axis=-1)

def reference(tokens, query_weight, key_weight, value_weight, output_weight, key_cache, value_cache, cache_places, slab_places):
    offsets = jnp.arange(TOK_DEV, dtype=jnp.int32)
    query_spots = (slab_places[:, None] * TOK_DEV + offsets[None, :]).reshape(NQ).astype(jnp.int32)
    cache_spots = (cache_places[:, None] * TOK_DEV + offsets[None, :]).reshape(NK).astype(jnp.int32)
    query_raw = jnp.dot(tokens, query_weight, preferred_element_type=jnp.float32).reshape(NQ, H, HD)
    key_raw = jnp.dot(tokens, key_weight, preferred_element_type=jnp.float32).reshape(NQ, KVH, HD)
    value_raw = jnp.dot(tokens, value_weight, preferred_element_type=jnp.float32).reshape(NQ, KVH, HD)
    group_heads = H // KVH
    queries = rotate(query_raw, query_spots).astype(jnp.bfloat16).reshape(NQ, KVH, group_heads, HD)
    keys_new = rotate(key_raw, query_spots).astype(jnp.bfloat16)
    values_new = value_raw.astype(jnp.bfloat16)
    key_rows = jnp.concatenate([key_cache, keys_new], axis=0)
    value_rows = jnp.concatenate([value_cache, values_new], axis=0)
    key_spots = jnp.concatenate([cache_spots, query_spots], axis=0).astype(jnp.int32)
    block_rows = math.gcd(NQ, 512)
    score_scale = 1.0 / math.sqrt(HD)
    query_blocks = jnp.transpose(queries, (1, 0, 2, 3)).reshape(KVH, NQ // block_rows, block_rows, group_heads, HD)
    spot_blocks = query_spots.reshape(NQ // block_rows, block_rows)
    key_heads = jnp.transpose(key_rows, (1, 0, 2))
    value_heads = jnp.transpose(value_rows, (1, 0, 2))

    def head_fn(inputs):
        query_head, key_head, value_head = inputs
        key_float = key_head.astype(jnp.float32)
        value_float = value_head.astype(jnp.float32)

        def block_fn(block_pair):
            query_block, spot_block = block_pair
            scores = jnp.einsum('rgd,cd->rgc', query_block.astype(jnp.float32), key_float) * score_scale
            visible = key_spots[None, None, :] <= spot_block[:, None, None]
            peaks = lax.optimization_barrier(jnp.max(jnp.where(visible, scores, NEGATIVE), axis=-1))
            weights = jnp.where(visible, jnp.exp(scores - peaks[..., None]), 0.0)
            totals = lax.optimization_barrier(jnp.sum(weights, axis=-1))
            rounded = lax.optimization_barrier(weights.astype(jnp.bfloat16)).astype(jnp.float32)
            summed = jnp.einsum('rgc,cd->rgd', rounded, value_float)
            return (summed / totals[..., None]).astype(jnp.bfloat16)
        return lax.map(block_fn, (query_head, spot_blocks))
    heads_all = lax.map(head_fn, (query_blocks, key_heads, value_heads))
    heads_out = jnp.transpose(heads_all, (1, 2, 0, 3, 4)).reshape(NQ, H * HD)
    return jnp.dot(heads_out, output_weight, preferred_element_type=jnp.float32).astype(jnp.bfloat16)
```

```python
import functools
import math

import jax
import jax.numpy as jnp
from jax import lax
from jax.experimental import pallas as pl
from jax.experimental.pallas import tpu as pltpu
from jax.sharding import Mesh
from jax.sharding import PartitionSpec as P

HID = ("hid_0", "hid_1")
HEAD = ("head_0", "head_1")
HEAD_HID = ("head_0", "head_1", "hid_0", "hid_1")
ALONG_X = ("head_0", "hid_0")

THETA = 500000.0
NEGATIVE = -1e30
BF16 = jnp.bfloat16
F32 = jnp.float32

ROWS = 256
HD = 128
NEW = 64
CHUNK = 512
QUARTER = 512
KEYS = 8 * QUARTER + 8 * NEW
NMSG = NEW + 16
MSG = ROWS + 16
EXPONENT = math.log2(math.e) / math.sqrt(HD)


def shift(n, by):
    return [(i, (i + by) % n) for i in range(n)]


def swap(array, axis):
    return lax.ppermute(array, axis, shift(2, 1))


def rotate(vectors, spots, heads):
    middle = HD // 2
    lane = jnp.arange(heads * HD, dtype=jnp.int32) % HD
    frequency = jnp.exp((lane % middle).astype(F32) * (-2.0 * math.log(THETA) / HD))
    angles = spots.astype(F32)[:, None] * frequency[None, :]
    sign = jnp.where(lane < middle, -1.0, 1.0)[None, :]
    by_head = vectors.reshape(vectors.shape[0], heads, 2, middle)
    other = jnp.concatenate([by_head[:, :, 1:], by_head[:, :, :1]], axis=2)
    other = other.reshape(vectors.shape)
    return vectors * jnp.cos(angles) + other * (sign * jnp.sin(angles))


def attention_kernel(
    places, slabs, meta, q_ref, *refs
):
    kv_refs = refs[:8]
    new_ref = refs[8]
    outs = refs[9:13]
    keys, values, scores, peak_ref, acc_ref, count = refs[13:]
    step = pl.program_id(0)
    me = meta[0]
    mine = slabs[me]

    @pl.when(step == 0)
    def _():
        values[:, HD:] = jnp.ones((KEYS, HD), BF16)
        n = jnp.int32(0)
        for i in range(8):
            source = lax.rem(me + 8 - i, 8) if i <= 4 else lax.rem(me + (8 - i), 8)
            for b in range(2):
                seen = places[source * 2 + b] < mine

                @pl.when(seen)
                def _(i=i, b=b, n=n):
                    at = pl.ds(pl.multiple_of(n * NEW, NEW), ROWS)
                    part = slice(b * ROWS, (b + 1) * ROWS)
                    keys[at, :] = kv_refs[i][part, :HD]
                    values[at, :HD] = kv_refs[i][part, HD:]

                n = n + jnp.where(seen, 4, 0)
        for z in range(8):
            seen = slabs[z] < mine

            @pl.when(seen)
            def _(z=z, n=n):
                at = pl.ds(pl.multiple_of(n * NEW, NEW), NEW)
                keys[at, :] = new_ref[z, :NEW, :HD]
                values[at, :HD] = new_ref[z, :NEW, HD:]

            n = n + jnp.where(seen, 1, 0)
        chunks = (n + 7) // 8
        for t in range(7):

            @pl.when(n + t < chunks * 8)
            def _(t=t, n=n):
                at = pl.ds(pl.multiple_of((n + t) * NEW, NEW), NEW)
                keys[at, :] = keys[:NEW, :]
                values[at, :] = jnp.zeros((NEW, 2 * HD), BF16)

        count[0] = chunks

    chunks = count[0]
    q = jnp.concatenate([q_ref[:, :HD], q_ref[:, HD:]], axis=0)
    height = 2 * ROWS
    own = new_ref[me, :NEW, :]
    own = jnp.concatenate([own, jnp.zeros((NEW, 2 * HD), BF16)], axis=0)
    contract = (((1,), (1,)), ((), ()))
    s_own = lax.dot_general(q, own[:, :HD], contract, preferred_element_type=F32)
    row = lax.rem(lax.broadcasted_iota(jnp.int32, (height, HD), 0), ROWS)
    lane = lax.broadcasted_iota(jnp.int32, (height, HD), 1)
    visible = jnp.logical_and(lane < NEW, lane + meta[1] <= row)
    s_own = jnp.where(visible, s_own, NEGATIVE)
    peak_ref[...] = s_own

    def first(i, carry):
        at = pl.ds(pl.multiple_of(i * CHUNK, CHUNK), CHUNK)
        s = lax.dot_general(q, keys[at, :], contract, preferred_element_type=F32)
        scores[i] = s
        best = peak_ref[...]
        for t in range(CHUNK // HD):
            best = jnp.maximum(best, s[:, t * HD : (t + 1) * HD])
        peak_ref[...] = best
        return carry

    lax.fori_loop(0, chunks, first, 0)
    peak = jnp.max(peak_ref[...], axis=1, keepdims=True)
    p_own = jnp.where(visible, jnp.exp2((s_own - peak) * EXPONENT), 0.0)
    v_own = jnp.concatenate([own[:, HD:], jnp.ones((HD, HD), BF16)], axis=1)
    acc_ref[...] = jnp.dot(p_own.astype(BF16), v_own, preferred_element_type=F32)

    def second(i, carry):
        at = pl.ds(pl.multiple_of(i * CHUNK, CHUNK), CHUNK)
        p = jnp.exp2((scores[i] - peak) * EXPONENT).astype(BF16)
        acc_ref[...] += jnp.dot(p, values[at, :], preferred_element_type=F32)
        return carry

    lax.fori_loop(0, chunks, second, 0)
    total = acc_ref[:, HD:]
    some = total > 0.0
    safe = jnp.where(some, total, 1.0)
    heads = (acc_ref[:, :HD] / safe).astype(BF16)
    level = jnp.where(some, peak * EXPONENT + jnp.log2(safe), NEGATIVE)
    level = jnp.transpose(level)[:1, :]
    parts = []
    for half in range(2):
        rest = level[:, half * ROWS : (half + 1) * ROWS]
        for _ in range(3):
            coded = rest.astype(BF16).astype(F32)
            parts.append(coded)
            rest = rest - coded
    where = lax.broadcasted_iota(jnp.int32, (16, ROWS), 0)
    table = jnp.zeros((16, ROWS), F32)
    for t, part in enumerate(parts):
        table = jnp.where(where == t, part, table)
    table = table.astype(BF16)
    for t in range(4):

        @pl.when(step == t)
        def _(t=t):
            outs[t][:ROWS, :HD] = heads[:ROWS]
            outs[t][:ROWS, HD:] = heads[ROWS:]
            outs[t][ROWS:, :] = table


def attention(places, slabs, meta, queries, kvs, new):
    whole = lambda shape: pl.BlockSpec(shape, lambda j, *_: (0,) * len(shape))
    grid_spec = pltpu.PrefetchScalarGridSpec(
        num_scalar_prefetch=3,
        grid=(4,),
        in_specs=[
            pl.BlockSpec((ROWS, 2 * HD), lambda j, places, slabs, meta: (0, meta[2 + j])),
            *[whole((QUARTER, 2 * HD))] * 8,
            whole((8, NMSG, 2 * HD)),
        ],
        out_specs=[whole((MSG, 2 * HD))] * 4,
        scratch_shapes=[
            pltpu.VMEM((KEYS, HD), BF16),
            pltpu.VMEM((KEYS, 2 * HD), BF16),
            pltpu.VMEM((KEYS // CHUNK, 2 * ROWS, CHUNK), F32),
            pltpu.VMEM((2 * ROWS, HD), F32),
            pltpu.VMEM((2 * ROWS, 2 * HD), F32),
            pltpu.SMEM((1,), jnp.int32),
        ],
    )
    return pl.pallas_call(
        attention_kernel,
        out_shape=[jax.ShapeDtypeStruct((MSG, 2 * HD), BF16)] * 4,
        grid_spec=grid_spec,
        compiler_params=pltpu.CompilerParams(vmem_limit_bytes=44 * 2**20),
        cost_estimate=pl.CostEstimate(
            flops=8 * ROWS * KEYS * HD * 4,
            bytes_accessed=8 * QUARTER * 2 * HD * 2,
            transcendentals=8 * ROWS * KEYS,
        ),
        name="attention",
    )(places, slabs, meta, queries, *kvs, new)


def merge_kernel(*refs):
    parts, out = refs[:4], refs[4]
    levels = []
    for ref in parts:
        t = ref[ROWS:, :].astype(F32)
        levels.append([t[0:1] + t[1:2] + t[2:3], t[3:4] + t[4:5] + t[5:6]])
    rows = []
    for half in range(2):
        top = functools.reduce(jnp.maximum, [lv[half] for lv in levels])
        w = [jnp.exp2(lv[half] - top) for lv in levels]
        total = w[0] + w[1] + w[2] + w[3]
        rows.extend([x / total for x in w])
    table = jnp.concatenate(rows, axis=0)
    table = jnp.transpose(jnp.concatenate([table, jnp.zeros((HD - 8, ROWS), F32)], axis=0))
    for half in range(2):
        cols = slice(half * HD, (half + 1) * HD)
        so_far = None
        for t, ref in enumerate(parts):
            w = table[:, half * 4 + t : half * 4 + t + 1]
            term = ref[:ROWS, cols].astype(F32) * w
            so_far = term if so_far is None else so_far + term
        out[:, cols] = so_far.astype(BF16)


def merge(parts):
    return pl.pallas_call(
        merge_kernel,
        out_shape=jax.ShapeDtypeStruct((ROWS, 2 * HD), BF16),
        cost_estimate=pl.CostEstimate(flops=10**6, bytes_accessed=10**6, transcendentals=4096),
        name="merge",
    )(*parts)


def project_kernel(meta, *refs):
    heads, weights, send, keep = refs[:4], refs[4:8], refs[8], refs[9]
    total = None
    for h, w in zip(heads, weights):
        term = jnp.dot(h[...], w[...], preferred_element_type=F32)
        total = term if total is None else total + term

    @pl.when(pl.program_id(0) < 4)
    def _():
        send[...] = total.astype(BF16)

    @pl.when(pl.program_id(0) >= 4)
    def _():
        keep[...] = total


def project(core, heads, weights):
    width = weights[0].shape[1]
    tile = width // 8

    def column(j, meta):
        return (0, (j % 4) * 2 + jnp.where(j < 4, 1 - meta[0], meta[0]))

    grid_spec = pltpu.PrefetchScalarGridSpec(
        num_scalar_prefetch=1,
        grid=(8,),
        in_specs=[
            *[pl.BlockSpec((ROWS, 2 * HD), lambda j, meta: (0, 0))] * 4,
            *[pl.BlockSpec((2 * HD, tile), column)] * 4,
        ],
        out_specs=[
            pl.BlockSpec((ROWS, tile), lambda j, meta: (0, jnp.minimum(j, 3))),
            pl.BlockSpec((ROWS, tile), lambda j, meta: (0, jnp.maximum(j - 4, 0))),
        ],
    )
    return pl.pallas_call(
        project_kernel,
        out_shape=[
            jax.ShapeDtypeStruct((ROWS, width // 2), BF16),
            jax.ShapeDtypeStruct((ROWS, width // 2), F32),
        ],
        grid_spec=grid_spec,
        cost_estimate=pl.CostEstimate(
            flops=2 * ROWS * 8 * HD * width, bytes_accessed=6 * 2**20, transcendentals=0
        ),
        name="project",
    )(core, *heads, *weights)


def body(
    tokens,
    query_weight,
    key_weight,
    value_weight,
    output_weight,
    key_cache,
    value_cache,
    cache_places,
    slab_places,
):
    key_index = lax.axis_index("key")
    x_hi = lax.axis_index("head_0")
    y = lax.axis_index("head_1")
    x = lax.axis_index("hid_0")
    core = lax.axis_index("hid_1")
    quarter = 2 * x + core

    kv = jnp.concatenate(
        [
            lax.dynamic_slice_in_dim(key_cache.reshape(-1, HD), quarter * QUARTER, QUARTER, 0),
            lax.dynamic_slice_in_dim(value_cache.reshape(-1, HD), quarter * QUARTER, QUARTER, 0),
        ],
        axis=1,
    )
    up = [kv]
    for _ in range(4):
        up.append(lax.ppermute(up[-1], "key", shift(8, 1)))
    down = [kv]
    for _ in range(3):
        down.append(lax.ppermute(down[-1], "key", shift(8, -1)))
    kvs = up + [down[3], down[2], down[1]]

    def columns(at):
        return jnp.concatenate(
            [
                lax.dynamic_slice_in_dim(output_weight, hi * 4096 + at * 1024, 1024, 1)
                for hi in range(2)
            ],
            axis=1,
        )

    weights = [columns(y)]
    for by in (1, 3, 2):
        weights.append(lax.ppermute(columns((y + by) % 4), "head_1", shift(4, by)))

    query_part = jnp.dot(tokens, query_weight, preferred_element_type=F32)
    key_part = jnp.dot(tokens, key_weight, preferred_element_type=F32)
    value_part = jnp.dot(tokens, value_weight, preferred_element_type=F32)

    def core_half(at):
        q = lax.dynamic_slice_in_dim(query_part, at * 512, 512, 1)
        k = lax.dynamic_slice_in_dim(key_part, at * 128, 128, 0)
        v = lax.dynamic_slice_in_dim(value_part, at * 128, 128, 0)
        return q, k, v

    def packed(q, k, v):
        half = k.shape[0] // 2
        low = jnp.concatenate([k[:half], v[:half], k[half:], v[half:]], axis=1)
        return jnp.concatenate([q, low], axis=0).astype(BF16)

    def unpacked(message):
        q = message[:ROWS].astype(F32)
        low = message[ROWS:].astype(F32)
        k = jnp.concatenate([low[:, :128], low[:, 256:384]], axis=0)
        v = jnp.concatenate([low[:, 128:256], low[:, 384:]], axis=0)
        return q, k, v

    got = unpacked(swap(packed(*core_half(1 - core)), "hid_1"))
    q, k, v = [a + b for a, b in zip(core_half(core), got)]
    k_pair = [lax.dynamic_slice_in_dim(k, at * NEW, NEW, 0) for at in (x, 1 - x)]
    v_pair = [lax.dynamic_slice_in_dim(v, at * NEW, NEW, 0) for at in (x, 1 - x)]
    got = unpacked(swap(packed(q, k_pair[1], v_pair[1]), "hid_0"))
    q = q + got[0]
    k = k_pair[0] + got[1]
    v = v_pair[0] + got[2]

    first = slab_places[key_index] * ROWS
    first_new = core * 128 + x * NEW
    q = rotate(q, first + jnp.arange(ROWS, dtype=jnp.int32), 4).astype(BF16)
    k = rotate(k, first + first_new + jnp.arange(NEW, dtype=jnp.int32), 1).astype(BF16)
    far = swap(q, "hid_1")
    queries = jnp.where(
        core == 0, jnp.concatenate([q, far], axis=1), jnp.concatenate([far, q], axis=1)
    )

    place = lax.dynamic_slice_in_dim(cache_places, quarter * 2, 2, 0)
    coded = jnp.concatenate([place // 2, place % 2]).astype(BF16)
    extra = jnp.zeros((16, 2 * HD), BF16).at[0, :4].set(coded)
    note = jnp.concatenate([jnp.concatenate([k, v.astype(BF16)], axis=1), extra], axis=0)
    new = lax.all_to_all(
        jnp.broadcast_to(note, (8, *note.shape)), "key", split_axis=0, concat_axis=0, tiled=True
    )
    coded = new[:, NEW, :4].astype(F32).astype(jnp.int32)
    places = (coded[:, :2] * 2 + coded[:, 2:]).reshape(16)

    mates = jnp.stack([quarter, quarter ^ 1, quarter ^ 2, quarter ^ 3])
    meta = jnp.concatenate([jnp.stack([key_index, first_new]), mates]).astype(jnp.int32)
    parts = attention(places, slab_places, meta, queries, kvs, new)
    flip = [(0, 3), (1, 2), (2, 1), (3, 0)]
    merged = merge(
        [
            parts[0],
            swap(parts[1], "hid_1"),
            swap(parts[2], "hid_0"),
            lax.ppermute(parts[3], HID, flip),
        ]
    )

    heads = [merged] + [lax.ppermute(merged, "head_1", shift(4, by)) for by in (1, 3, 2)]
    send, keep = project(core.astype(jnp.int32).reshape(1), heads, weights)
    total = keep + swap(send, "hid_1").astype(F32)
    spot = 2 * x_hi + x
    out = lax.dynamic_slice_in_dim(total, spot * ROWS, ROWS, 1)
    for by in (1, 3, 2):
        block = lax.dynamic_slice_in_dim(total, ((spot + by) % 4) * ROWS, ROWS, 1)
        out = out + lax.ppermute(block.astype(BF16), ALONG_X, shift(4, by)).astype(F32)
    return out.astype(BF16)


def solution(mesh):
    finer = Mesh(
        mesh.devices.reshape(2, 4, mesh.shape["key"], 2, 2),
        ("head_0", "head_1", "key", "hid_0", "hid_1"),
    )
    return jax.shard_map(
        body,
        mesh=finer,
        in_specs=(
            P("key", HID),
            P(HID, HEAD),
            P(HID, HEAD),
            P(HID, HEAD),
            P(HEAD_HID, None),
            P("key", HEAD, None),
            P("key", HEAD, None),
            P("key"),
            P(),
        ),
        out_specs=P("key", HEAD_HID),
        check_vma=False,
    )
```

```python
import functools
import math

import jax
import jax.numpy as jnp
import numpy as np
from jax import lax
from jax.experimental import pallas as pl
from jax.experimental.pallas import tpu as pltpu
from jax.sharding import Mesh
from jax.sharding import PartitionSpec as P

HID = ("hid_0", "hid_1")
HEAD = ("head_0", "head_1")
HEAD_HID = ("head_0", "head_1", "hid_0", "hid_1")
ALONG_X = ("head_0", "hid_0")

THETA = 500000.0
NEGATIVE = -1e30
BF16 = jnp.bfloat16
F32 = jnp.float32

ROWS = 256
HD = 128
PAIR = 2 * HD
NEW = 64
QUARTER = 512
LOAD = QUARTER + 16
MSG = ROWS + 16
TALL = 1024
EXPONENT = math.log2(math.e) / math.sqrt(HD)
CONTRACT = (((1,), (1,)), ((), ()))

VMEM = pl.BlockSpec(memory_space=pltpu.VMEM)
SMEM = pl.BlockSpec(memory_space=pltpu.SMEM)
ANY = pl.BlockSpec(memory_space=pl.ANY)


def shaped(shape, dtype):
    return jax.ShapeDtypeStruct(shape, dtype)


def params(mib):
    return pltpu.CompilerParams(vmem_limit_bytes=mib * 2**20)


def cost(flops=0, moved=0, exps=0):
    return pl.CostEstimate(flops=flops, bytes_accessed=moved, transcendentals=exps)


def shift(n, by):
    return [(i, (i + by) % n) for i in range(n)]


def swap(array, axis):
    return lax.ppermute(array, axis, shift(2, 1))


def hid_index():
    return 2 * lax.axis_index("hid_0") + lax.axis_index("hid_1")


def pack_kernel(places, keys, values, out, codes, sems):
    quarter = hid_index()
    rows = pl.ds(pl.multiple_of(quarter * QUARTER, QUARTER), QUARTER)
    copies = [
        pltpu.make_async_copy(keys.at[rows, :], out.at[:QUARTER, :HD], sems.at[0]),
        pltpu.make_async_copy(values.at[rows, :], out.at[:QUARTER, HD:], sems.at[1]),
        pltpu.make_async_copy(codes, out.at[QUARTER:, :], sems.at[2]),
    ]
    copies[0].start()
    copies[1].start()
    lane = lax.broadcasted_iota(jnp.int32, (16, PAIR), 1)
    table = jnp.zeros((16, PAIR), jnp.int32)
    for b in range(2):
        place = places[quarter * 2 + b]
        table = jnp.where(lane == 2 * b, place >> 1, table)
        table = jnp.where(lane == 2 * b + 1, place & 1, table)
    codes[...] = table.astype(F32).astype(BF16)
    copies[2].start()
    for copy in copies:
        copy.wait()


def pack(places, keys, values):
    return pl.pallas_call(
        pack_kernel,
        out_shape=shaped((LOAD, PAIR), BF16),
        in_specs=[SMEM, ANY, ANY],
        out_specs=ANY,
        scratch_shapes=[pltpu.VMEM((16, PAIR), BF16), pltpu.SemaphoreType.DMA((3,))],
        compiler_params=params(4),
        cost_estimate=cost(moved=2**19),
        name="pack",
    )(places, keys, values)


def columns_kernel(weight, *refs):
    outs, sems = refs[:4], refs[4]
    y = lax.axis_index("head_1")
    copies = []
    for t, by in enumerate((2, 1, 3, 0)):
        at = lax.rem(y + by, 4) * 1024
        for hi in range(2):
            source = pl.ds(pl.multiple_of(hi * 4096 + at, 1024), 1024)
            copies.append(
                pltpu.make_async_copy(
                    weight.at[:, source],
                    outs[t].at[:, hi * 1024 : (hi + 1) * 1024],
                    sems.at[2 * t + hi],
                )
            )
    for copy in copies:
        copy.start()
    for copy in copies:
        copy.wait()


def columns(weight):
    return pl.pallas_call(
        columns_kernel,
        out_shape=[shaped((ROWS, 2048), BF16)] * 4,
        in_specs=[ANY],
        out_specs=[ANY] * 4,
        scratch_shapes=[pltpu.SemaphoreType.DMA((8,))],
        compiler_params=params(4),
        cost_estimate=cost(moved=2**23),
        name="columns",
    )(weight)


def first_kernel(core_ref, tokens, query, key, value, send, keep, fresh):
    j = pl.program_id(0)
    core = core_ref[0]
    part = jnp.dot(tokens[...], query[...], preferred_element_type=F32)
    for t in range(2):
        cols = slice(t * ROWS, (t + 1) * ROWS)

        @pl.when(j == t)
        def _(cols=cols):
            send[:ROWS, cols] = part.astype(BF16)

        @pl.when(j == 2 + t)
        def _(cols=cols):
            keep[:ROWS, cols] = part

    @pl.when(j == 0)
    def _():
        fresh[:, :HD] = jnp.dot(tokens[...], key[...], preferred_element_type=F32)
        fresh[:, HD:] = jnp.dot(tokens[...], value[...], preferred_element_type=F32)
        for t in range(2):
            cols = slice(t * PAIR, (t + 1) * PAIR)
            far = pl.ds(pl.multiple_of((1 - core) * 128 + t * NEW, NEW), NEW)
            near = pl.ds(pl.multiple_of(core * 128 + t * NEW, NEW), NEW)
            send[ROWS:, cols] = fresh[far, :].astype(BF16)
            keep[ROWS:, cols] = fresh[near, :]


def first(core, tokens, query, key, value):
    def tile(j, core):
        return (0, jnp.where(j < 2, (1 - core[0]) * 2 + j, core[0] * 2 + j - 2))

    whole = lambda a: pl.BlockSpec(a.shape, lambda j, core: (0, 0))
    grid_spec = pltpu.PrefetchScalarGridSpec(
        num_scalar_prefetch=1,
        grid=(4,),
        in_specs=[
            whole(tokens),
            pl.BlockSpec((query.shape[0], ROWS), tile),
            whole(key),
            whole(value),
        ],
        out_specs=[pl.BlockSpec((320, 512), lambda j, core: (0, 0))] * 2,
        scratch_shapes=[pltpu.VMEM((ROWS, PAIR), F32)],
    )
    return pl.pallas_call(
        first_kernel,
        out_shape=[shaped((320, 512), BF16), shaped((320, 512), F32)],
        grid_spec=grid_spec,
        compiler_params=params(20),
        cost_estimate=cost(flops=2 * 256 * 2048 * 1280, moved=6 * 2**20),
        name="first",
    )(core, tokens, query, key, value)


def second_kernel(keep, got, send, onward):
    x = lax.axis_index("hid_0")
    q = keep[:ROWS, :] + got[:ROWS, :].astype(F32)
    send[:ROWS, :] = q.astype(BF16)
    onward[:ROWS, :] = q
    low = keep[ROWS:, :] + got[ROWS:, :].astype(F32)
    sides = [low[:, :PAIR], low[:, PAIR:]]
    sides = [jnp.concatenate([s[:32], s[32:]], axis=1) for s in sides]
    mine = jnp.where(x == 0, sides[0], sides[1])
    other = jnp.where(x == 0, sides[1], sides[0])
    send[ROWS:, :] = other.astype(BF16)
    onward[ROWS:, :] = mine


def second(keep, got):
    return pl.pallas_call(
        second_kernel,
        out_shape=[shaped((288, 512), BF16), shaped((288, 512), F32)],
        in_specs=[VMEM] * 2,
        out_specs=[VMEM] * 2,
        compiler_params=params(8),
        cost_estimate=cost(flops=2**18, moved=2**20),
        name="second",
    )(keep, got)


def new_offset():
    return lax.axis_index("hid_1") * 128 + lax.axis_index("hid_0") * NEW


def rotate_kernel(keep, got, cosine, sine, queries, notes):
    for h in range(4):
        cols = slice(h * HD, (h + 1) * HD)
        u = keep[:ROWS, cols] + got[:ROWS, cols].astype(F32)
        turned = u * cosine[...] + pltpu.roll(u, HD // 2, 1) * sine[...]
        queries[:, cols] = turned.astype(BF16)
    low = keep[ROWS:, :] + got[ROWS:, :].astype(F32)
    low = jnp.concatenate([low[:, :PAIR], low[:, PAIR:]], axis=0)
    rows = pl.ds(pl.multiple_of(new_offset(), NEW), NEW)
    u = low[:, :HD]
    turned = u * cosine[rows, :] + pltpu.roll(u, HD // 2, 1) * sine[rows, :]
    for z in range(8):
        notes[z, :, :HD] = turned.astype(BF16)
        notes[z, :, HD:] = low[:, HD:].astype(BF16)


def rotated(keep, got, cosine, sine):
    return pl.pallas_call(
        rotate_kernel,
        out_shape=[shaped((ROWS, 512), BF16), shaped((8, NEW, PAIR), BF16)],
        in_specs=[VMEM] * 4,
        out_specs=[VMEM] * 2,
        compiler_params=params(8),
        cost_estimate=cost(flops=2**20, moved=2**20),
        name="rotated",
    )(keep, got, cosine, sine)


def gather_visible(mine, slabs, loads, new, keys, values, chunk):
    height = keys.shape[0]
    values[:, HD:] = jnp.ones((height, HD), BF16)
    n = jnp.int32(0)
    lane = lax.broadcasted_iota(jnp.int32, (16, HD), 1)
    for load in loads:
        codes = load[QUARTER:, :HD].astype(F32)
        codes = jnp.where(lane % 2 == 0, 2.0, 1.0) * codes
        for b in range(2):
            part = jnp.where(lane // 2 == b, codes, 0.0)
            place = jnp.max(part[:1] + pltpu.roll(part, HD - 1, 1)[:1]).astype(jnp.int32)
            seen = place < mine

            @pl.when(seen)
            def _(load=load, b=b, n=n):
                at = pl.ds(pl.multiple_of(n * NEW, NEW), ROWS)
                rows = slice(b * ROWS, (b + 1) * ROWS)
                keys[at, :] = load[rows, :HD]
                values[at, :HD] = load[rows, HD:]

            n = n + jnp.where(seen, ROWS // NEW, 0)
    if new is not None:
        for z in range(8):
            seen = slabs[z] < mine

            @pl.when(seen)
            def _(z=z, n=n):
                at = pl.ds(pl.multiple_of(n * NEW, NEW), NEW)
                keys[at, :] = new[z, :, :HD]
                values[at, :HD] = new[z, :, HD:]

            n = n + jnp.where(seen, 1, 0)
    per = chunk // NEW
    chunks = (n + per - 1) // per

    def pad(t, carry):
        at = pl.ds(pl.multiple_of(t * NEW, NEW), NEW)
        keys[at, :] = keys[:NEW, :]
        values[at, :] = jnp.zeros((NEW, PAIR), BF16)
        return carry

    lax.fori_loop(n, chunks * per, pad, 0)
    return chunks


def attend(q, peak_ref, chunks, keys, values, scores, chunk, acc_at, before):
    def peaks(i, carry):
        at = pl.ds(pl.multiple_of(i * chunk, chunk), chunk)
        s = lax.dot_general(q, keys[at, :], CONTRACT, preferred_element_type=F32)
        scores[i] = s
        best = peak_ref[...]
        for t in range(chunk // HD):
            best = jnp.maximum(best, s[:, t * HD : (t + 1) * HD])
        peak_ref[...] = best
        return carry

    lax.fori_loop(0, chunks, peaks, 0)
    peak = jnp.max(peak_ref[...], axis=1, keepdims=True)
    acc_at[...] = before(peak)

    def weigh(i, carry):
        at = pl.ds(pl.multiple_of(i * chunk, chunk), chunk)
        p = jnp.exp2((scores[i] - peak) * EXPONENT).astype(BF16)
        acc_at[...] += jnp.dot(p, values[at, :], preferred_element_type=F32)
        return carry

    lax.fori_loop(0, chunks, weigh, 0)
    return peak


def near_kernel(
    slabs, near, far, own, *refs, chunk, count
):
    loads, (q_out, acc_out, peak_out) = refs[:count], refs[count : count + 3]
    keys, values, scores, peak_ref = refs[count + 3 :]
    mine = slabs[lax.axis_index("key")]
    core = lax.axis_index("hid_1")
    x = lax.axis_index("hid_0")
    for j in range(4):
        half = x if j < 2 else 1 - x
        parity = core if j % 2 == 0 else 1 - core
        cols = pl.ds(pl.multiple_of(parity * PAIR, PAIR), PAIR)
        rows = [slice((2 * j + t) * ROWS, (2 * j + t + 1) * ROWS) for t in range(2)]

        @pl.when(half == core)
        def _(cols=cols, rows=rows):
            both = near[:, cols]
            q_out[rows[0], :] = both[:, :HD]
            q_out[rows[1], :] = both[:, HD:]

        @pl.when(half != core)
        def _(cols=cols, rows=rows):
            both = far[:, cols]
            q_out[rows[0], :] = both[:, :HD]
            q_out[rows[1], :] = both[:, HD:]

    chunks = gather_visible(mine, None, loads, None, keys, values, chunk)
    zeros = jnp.zeros((NEW, HD), BF16)
    own_keys = jnp.concatenate([own[0, :, :HD], zeros], axis=0)
    own_values = jnp.concatenate([own[0, :, HD:], zeros], axis=0)
    own_values = jnp.concatenate([own_values, jnp.ones((HD, HD), BF16)], axis=1)
    row = lax.broadcasted_iota(jnp.int32, (TALL, HD), 0) % ROWS
    lane = lax.broadcasted_iota(jnp.int32, (TALL, HD), 1)
    visible = jnp.logical_and(lane < NEW, lane + new_offset() <= row)

    def tall(step, carry):
        at = pl.ds(pl.multiple_of(step * TALL, TALL), TALL)
        q = q_out[at, :]
        s = lax.dot_general(q, own_keys, CONTRACT, preferred_element_type=F32)
        s = jnp.where(visible, s, NEGATIVE)
        peak_ref[...] = s

        def before(peak):
            p = jnp.where(visible, jnp.exp2((s - peak) * EXPONENT), 0.0)
            return jnp.dot(p.astype(BF16), own_values, preferred_element_type=F32)

        peak = attend(
            q, peak_ref, chunks, keys, values, scores, chunk, acc_out.at[at, :], before
        )
        peak_out[at, :] = jnp.broadcast_to(peak, (TALL, HD))
        return carry

    lax.fori_loop(0, 8 * ROWS // TALL, tall, 0)


def attend_near(slabs, near, far, own, loads):
    count, chunk = len(loads), 1280
    height = count * QUARTER
    return pl.pallas_call(
        functools.partial(near_kernel, chunk=chunk, count=count),
        out_shape=[
            shaped((8 * ROWS, HD), BF16),
            shaped((8 * ROWS, PAIR), F32),
            shaped((8 * ROWS, HD), F32),
        ],
        in_specs=[SMEM] + [VMEM] * (3 + count),
        out_specs=[VMEM] * 3,
        scratch_shapes=[
            pltpu.VMEM((height, HD), BF16),
            pltpu.VMEM((height, PAIR), BF16),
            pltpu.VMEM((height // chunk, TALL, chunk), F32),
            pltpu.VMEM((TALL, HD), F32),
        ],
        compiler_params=params(30),
        cost_estimate=cost(8 * ROWS * height * HD * 6, 2**23, 8 * ROWS * height),
        name="near",
    )(slabs, near, far, own, *loads)


def far_kernel(slabs, queries, acc_in, peak_in, new, *refs, chunk, count):
    loads, outs = refs[:count], refs[count : count + 4]
    keys, values, scores, peak_ref, acc = refs[count + 4 :]
    mine = slabs[lax.axis_index("key")]
    chunks = gather_visible(mine, slabs, loads, new, keys, values, chunk)
    where = lax.broadcasted_iota(jnp.int32, (16, ROWS), 0)
    for step in range(8 * ROWS // TALL):
        at = slice(step * TALL, (step + 1) * TALL)
        peak_ref[...] = peak_in[at, :]

        def before(peak, at=at):
            factor = jnp.exp2((peak_in[at, :1] - peak) * EXPONENT)
            return acc_in[at, :] * factor

        peak = attend(
            queries[at, :], peak_ref, chunks, keys, values, scores, chunk, acc, before
        )
        total = acc[:, HD:]
        some = total > 0.0
        safe = jnp.where(some, total, 1.0)
        heads = (acc[:, :HD] / safe).astype(BF16)
        level = jnp.where(some, peak * EXPONENT + jnp.log2(safe), NEGATIVE)
        level = jnp.transpose(level)[:1, :]
        for t in range(TALL // (2 * ROWS)):
            out = outs[step * (TALL // (2 * ROWS)) + t]
            table = jnp.zeros((16, ROWS), F32)
            for half in range(2):
                rows = slice((2 * t + half) * ROWS, (2 * t + half + 1) * ROWS)
                out[:ROWS, half * HD : (half + 1) * HD] = heads[rows]
                rest = level[:, rows]
                for k in range(3):
                    coded = rest.astype(BF16).astype(F32)
                    table = jnp.where(where == 3 * half + k, coded, table)
                    rest = rest - coded
            out[ROWS:, :] = table.astype(BF16)


def attend_far(slabs, queries, acc, peak, new, loads):
    count, chunk = len(loads), 1024
    height = -(-(count * QUARTER + 8 * NEW) // chunk) * chunk
    return pl.pallas_call(
        functools.partial(far_kernel, chunk=chunk, count=count),
        out_shape=[shaped((MSG, PAIR), BF16)] * 4,
        in_specs=[SMEM] + [VMEM] * (4 + count),
        out_specs=[VMEM] * 4,
        scratch_shapes=[
            pltpu.VMEM((height, HD), BF16),
            pltpu.VMEM((height, PAIR), BF16),
            pltpu.VMEM((height // chunk, TALL, chunk), F32),
            pltpu.VMEM((TALL, HD), F32),
            pltpu.VMEM((TALL, PAIR), F32),
        ],
        compiler_params=params(30),
        cost_estimate=cost(8 * ROWS * height * HD * 6, 2**23, 8 * ROWS * height),
        name="far",
    )(slabs, queries, acc, peak, new, *loads)


def merge_kernel(*refs):
    parts, out = refs[:4], refs[4]
    levels = []
    for ref in parts:
        t = ref[ROWS:, :].astype(F32)
        levels.append([t[0:1] + t[1:2] + t[2:3], t[3:4] + t[4:5] + t[5:6]])
    rows = []
    for half in range(2):
        top = functools.reduce(jnp.maximum, [lv[half] for lv in levels])
        w = [jnp.exp2(lv[half] - top) for lv in levels]
        total = w[0] + w[1] + w[2] + w[3]
        rows.extend([x / total for x in w])
    table = jnp.concatenate(rows, axis=0)
    table = jnp.transpose(jnp.concatenate([table, jnp.zeros((HD - 8, ROWS), F32)], axis=0))
    for half in range(2):
        cols = slice(half * HD, (half + 1) * HD)
        so_far = None
        for t, ref in enumerate(parts):
            w = table[:, half * 4 + t : half * 4 + t + 1]
            term = ref[:ROWS, cols].astype(F32) * w
            so_far = term if so_far is None else so_far + term
        out[:, cols] = so_far.astype(BF16)


def merge(parts):
    return pl.pallas_call(
        merge_kernel,
        out_shape=shaped((ROWS, PAIR), BF16),
        in_specs=[VMEM] * 4,
        out_specs=VMEM,
        compiler_params=params(8),
        cost_estimate=cost(10**6, 10**6, 4096),
        name="merge",
    )(*parts)


def project_kernel(*refs):
    heads, weights, send, keep = refs[:4], refs[4:8], refs[8], refs[9]
    core = lax.axis_index("hid_1")
    h = jnp.concatenate([ref[...] for ref in heads], axis=1)
    for out, side in ((send, 1 - core), (keep, core)):
        for t in range(4):
            cols = pl.ds(pl.multiple_of(t * 512 + side * ROWS, ROWS), ROWS)
            w = jnp.concatenate([ref[:, cols] for ref in weights], axis=0)
            total = jnp.dot(h, w, preferred_element_type=F32)
            out[:, t * ROWS : (t + 1) * ROWS] = total.astype(out.dtype)


def project(heads, weights):
    width = weights[0].shape[1]
    return pl.pallas_call(
        project_kernel,
        out_shape=[shaped((ROWS, width // 2), BF16), shaped((ROWS, width // 2), F32)],
        in_specs=[VMEM] * 8,
        out_specs=[VMEM] * 2,
        compiler_params=params(16),
        cost_estimate=cost(flops=2 * ROWS * 8 * HD * width, moved=6 * 2**20),
        name="project",
    )(*heads, *weights)


def split_kernel(keep, got, own, *sends):
    spot = 2 * lax.axis_index("head_0") + lax.axis_index("hid_0")
    for by in range(4):
        cols = pl.ds(pl.multiple_of(lax.rem(spot + by, 4) * ROWS, ROWS), ROWS)
        total = keep[:, cols] + got[:, cols].astype(F32)
        if by == 0:
            own[...] = total
        else:
            sends[by - 1][...] = total.astype(BF16)


def split(keep, got):
    return pl.pallas_call(
        split_kernel,
        out_shape=[shaped((ROWS, ROWS), F32)] + [shaped((ROWS, ROWS), BF16)] * 3,
        in_specs=[VMEM] * 2,
        out_specs=[VMEM] * 4,
        compiler_params=params(8),
        cost_estimate=cost(flops=2**18, moved=2**21),
        name="split",
    )(keep, got)


def body(
    tokens,
    query_weight,
    key_weight,
    value_weight,
    output_weight,
    key_cache,
    value_cache,
    cache_places,
    slab_places,
):
    key_index = lax.axis_index("key")
    core = lax.axis_index("hid_1")

    load = pack(cache_places, key_cache.reshape(-1, HD), value_cache.reshape(-1, HD))
    up = [load]
    for _ in range(4):
        up.append(lax.ppermute(up[-1], "key", shift(8, 1)))
    down = [load]
    for _ in range(3):
        down.append(lax.ppermute(down[-1], "key", shift(8, -1)))

    pieces = columns(output_weight)
    weights = [pieces[3]]
    for piece, by in zip(pieces, (2, 1, 3)):
        weights.append(lax.ppermute(piece, "head_1", shift(4, by)))

    send, keep = first(
        core.astype(jnp.int32).reshape(1), tokens, query_weight, key_weight, value_weight
    )
    send, keep = second(keep, swap(send, "hid_1"))
    got = swap(send, "hid_0")

    middle = HD // 2
    index = np.arange(HD) % middle
    frequency = jnp.exp(jnp.asarray(index, F32) * (-2.0 * math.log(THETA) / HD))
    sign = np.where(np.arange(HD) < middle, -1.0, 1.0).astype(np.float32)
    spots = slab_places[key_index] * ROWS + jnp.arange(ROWS, dtype=jnp.int32)
    angles = spots.astype(F32)[:, None] * frequency[None, :]
    queries, notes = rotated(keep, got, jnp.cos(angles), jnp.sin(angles) * sign[None, :])
    far = swap(queries, "hid_1")

    new = lax.all_to_all(notes, "key", split_axis=0, concat_axis=0, tiled=True)

    state = attend_near(slab_places, queries, far, notes, up[:3] + down[1:3])
    parts = attend_far(slab_places, *state, new, [up[3], down[3], up[4]])
    flip = [(0, 3), (1, 2), (2, 1), (3, 0)]
    merged = merge(
        [
            parts[0],
            swap(parts[1], "hid_1"),
            swap(parts[2], "hid_0"),
            lax.ppermute(parts[3], HID, flip),
        ]
    )

    heads = [merged] + [lax.ppermute(merged, "head_1", shift(4, by)) for by in (2, 1, 3)]
    send, keep = project(heads, weights)
    own, *blocks = split(keep, swap(send, "hid_1"))
    out = own
    for by in (2, 1, 3):
        out = out + lax.ppermute(blocks[by - 1], ALONG_X, shift(4, by)).astype(F32)
    return out.astype(BF16)


def solution(mesh):
    finer = Mesh(
        mesh.devices.reshape(2, 4, mesh.shape["key"], 2, 2),
        ("head_0", "head_1", "key", "hid_0", "hid_1"),
    )
    return jax.shard_map(
        body,
        mesh=finer,
        in_specs=(
            P("key", HID),
            P(HID, HEAD),
            P(HID, HEAD),
            P(HID, HEAD),
            P(HEAD_HID, None),
            P("key", HEAD, None),
            P("key", HEAD, None),
            P("key"),
            P(),
        ),
        out_specs=P("key", HEAD_HID),
        check_vma=False,
    )
```

```python
import functools
import math

import jax
import jax.numpy as jnp
import numpy as np
from jax import lax
from jax.experimental import pallas as pl
from jax.experimental.pallas import tpu as pltpu
from jax.sharding import Mesh
from jax.sharding import PartitionSpec as P

HID = ("hid_0", "hid_1")
HEAD = ("head_0", "head_1")
HEAD_HID = ("head_0", "head_1", "hid_0", "hid_1")
ALONG_X = ("head_0", "hid_0")

THETA = 500000.0
NEGATIVE = -1e30
BF16 = jnp.bfloat16
F32 = jnp.float32

ROWS = 256
HD = 128
PAIR = 2 * HD
NEW = 64
QUARTER = 512
HALF = ROWS + 16
LOAD = 2 * HALF
MSG = ROWS + 16
TALL = 1024
EXPONENT = math.log2(math.e) / math.sqrt(HD)
CONTRACT = (((1,), (1,)), ((), ()))

VMEM = pl.BlockSpec(memory_space=pltpu.VMEM)
SMEM = pl.BlockSpec(memory_space=pltpu.SMEM)
HBM = pl.BlockSpec(memory_space=pltpu.HBM)


def shaped(shape, dtype):
    return jax.ShapeDtypeStruct(shape, dtype)


def params(mib=60):
    return pltpu.CompilerParams(vmem_limit_bytes=mib * 2**20)


def cost(flops=0, moved=0, exps=0):
    return pl.CostEstimate(flops=flops, bytes_accessed=moved, transcendentals=exps)


def shift(n, by):
    return [(i, (i + by) % n) for i in range(n)]


def swap(array, axis):
    return lax.ppermute(array, axis, shift(2, 1))


def hid_index():
    return 2 * lax.axis_index("hid_0") + lax.axis_index("hid_1")


def fetch(pairs, sems):
    copies = [
        pltpu.make_async_copy(source, target, sems.at[i])
        for i, (source, target) in enumerate(pairs)
    ]
    for copy in copies:
        copy.start()
    return copies


def pack_kernel(places, keys, values, out, codes, sems):
    quarter = hid_index()
    pairs = []
    for b in range(2):
        rows = pl.ds(pl.multiple_of(quarter * QUARTER + b * ROWS, ROWS), ROWS)
        to = slice(b * HALF, b * HALF + ROWS)
        pairs.append((keys.at[rows, :], out.at[to, :HD]))
        pairs.append((values.at[rows, :], out.at[to, HD:]))
    copies = fetch(pairs, sems.at[:4])
    lane = lax.broadcasted_iota(jnp.int32, (16, PAIR), 1)
    for b in range(2):
        place = places[quarter * 2 + b]
        table = jnp.where(lane == 0, place >> 1, jnp.where(lane == 1, place & 1, 0))
        codes[b] = table.astype(F32).astype(BF16)
    pairs = [(codes.at[b], out.at[b * HALF + ROWS : (b + 1) * HALF, :]) for b in range(2)]
    copies += fetch(pairs, sems.at[4:])
    for copy in copies:
        copy.wait()


def pack(places, keys, values):
    return pl.pallas_call(
        pack_kernel,
        out_shape=shaped((LOAD, PAIR), BF16),
        in_specs=[SMEM, HBM, HBM],
        out_specs=HBM,
        scratch_shapes=[pltpu.VMEM((2, 16, PAIR), BF16), pltpu.SemaphoreType.DMA((6,))],
        compiler_params=params(),
        cost_estimate=cost(moved=2**19),
        name="pack",
    )(places, keys, values)


def columns_kernel(weight, *refs):
    outs, sems = refs[:4], refs[4]
    y = lax.axis_index("head_1")
    copies = []
    for t, by in enumerate((2, 1, 3, 0)):
        at = lax.rem(y + by, 4) * 1024
        for hi in range(2):
            source = pl.ds(pl.multiple_of(hi * 4096 + at, 1024), 1024)
            copies.append(
                pltpu.make_async_copy(
                    weight.at[:, source],
                    outs[t].at[:, hi * 1024 : (hi + 1) * 1024],
                    sems.at[2 * t + hi],
                )
            )
    for copy in copies:
        copy.start()
    for copy in copies:
        copy.wait()


def columns(weight):
    return pl.pallas_call(
        columns_kernel,
        out_shape=[shaped((ROWS, 2048), BF16)] * 4,
        in_specs=[HBM],
        out_specs=[HBM] * 4,
        scratch_shapes=[pltpu.SemaphoreType.DMA((8,))],
        compiler_params=params(),
        cost_estimate=cost(moved=2**23),
        name="columns",
    )(weight)


def first_kernel(
    tokens, query, key, value, send, keep, tok, tiles, kv, fresh, sems
):
    core = lax.axis_index("hid_1")
    pairs = [(tokens, tok)]
    for t in range(4):
        side = 1 - core if t < 2 else core
        cols = pl.ds(pl.multiple_of(side * 512 + (t % 2) * ROWS, ROWS), ROWS)
        pairs.append((query.at[:, cols], tiles.at[t]))
        if t == 1:
            pairs.append((key, kv.at[0]))
            pairs.append((value, kv.at[1]))
    copies = fetch(pairs, sems)
    copies[0].wait()

    def part(t):
        return jnp.dot(tok[...], tiles[t], preferred_element_type=F32)

    for t in range(2):
        copies[1 + t].wait()
        send[:ROWS, t * ROWS : (t + 1) * ROWS] = part(t).astype(BF16)
    copies[3].wait()
    copies[4].wait()
    both = jnp.concatenate([kv[0], kv[1]], axis=1)
    fresh[...] = jnp.dot(tok[...], both, preferred_element_type=F32)
    for t in range(2):
        cols = slice(t * PAIR, (t + 1) * PAIR)
        far = pl.ds(pl.multiple_of((1 - core) * 128 + t * NEW, NEW), NEW)
        near = pl.ds(pl.multiple_of(core * 128 + t * NEW, NEW), NEW)
        send[ROWS:, cols] = fresh[far, :].astype(BF16)
        keep[ROWS:, cols] = fresh[near, :]
    for t in range(2):
        copies[5 + t].wait()
        keep[:ROWS, t * ROWS : (t + 1) * ROWS] = part(2 + t)


def first(tokens, query, key, value):
    deep = tokens.shape[1]
    return pl.pallas_call(
        first_kernel,
        out_shape=[shaped((320, 512), BF16), shaped((320, 512), F32)],
        in_specs=[HBM] * 4,
        out_specs=[VMEM] * 2,
        scratch_shapes=[
            pltpu.VMEM((ROWS, deep), BF16),
            pltpu.VMEM((4, deep, ROWS), BF16),
            pltpu.VMEM((2, deep, HD), BF16),
            pltpu.VMEM((ROWS, PAIR), F32),
            pltpu.SemaphoreType.DMA((7,)),
        ],
        compiler_params=params(),
        cost_estimate=cost(flops=2 * 256 * 2048 * 1280, moved=6 * 2**20),
        name="first",
    )(tokens, query, key, value)


def second_kernel(keep, got, send, onward):
    x = lax.axis_index("hid_0")
    q = keep[:ROWS, :] + got[:ROWS, :].astype(F32)
    send[:ROWS, :] = q.astype(BF16)
    onward[:ROWS, :] = q
    low = keep[ROWS:, :] + got[ROWS:, :].astype(F32)
    sides = [low[:, :PAIR], low[:, PAIR:]]
    sides = [jnp.concatenate([s[:32], s[32:]], axis=1) for s in sides]
    mine = jnp.where(x == 0, sides[0], sides[1])
    other = jnp.where(x == 0, sides[1], sides[0])
    send[ROWS:, :] = other.astype(BF16)
    onward[ROWS:, :] = mine


def second(keep, got):
    return pl.pallas_call(
        second_kernel,
        out_shape=[shaped((288, 512), BF16), shaped((288, 512), F32)],
        in_specs=[VMEM] * 2,
        out_specs=[VMEM] * 2,
        compiler_params=params(8),
        cost_estimate=cost(flops=2**18, moved=2**20),
        name="second",
    )(keep, got)


def new_offset():
    return lax.axis_index("hid_1") * 128 + lax.axis_index("hid_0") * NEW


def rotate_kernel(keep, got, cosine, sine, queries, notes):
    for h in range(4):
        cols = slice(h * HD, (h + 1) * HD)
        u = keep[:ROWS, cols] + got[:ROWS, cols].astype(F32)
        turned = u * cosine[...] + pltpu.roll(u, HD // 2, 1) * sine[...]
        queries[:, cols] = turned.astype(BF16)
    low = keep[ROWS:, :] + got[ROWS:, :].astype(F32)
    low = jnp.concatenate([low[:, :PAIR], low[:, PAIR:]], axis=0)
    rows = pl.ds(pl.multiple_of(new_offset(), NEW), NEW)
    u = low[:, :HD]
    turned = u * cosine[rows, :] + pltpu.roll(u, HD // 2, 1) * sine[rows, :]
    for z in range(8):
        notes[z, :, :HD] = turned.astype(BF16)
        notes[z, :, HD:] = low[:, HD:].astype(BF16)


def rotated(keep, got, cosine, sine):
    return pl.pallas_call(
        rotate_kernel,
        out_shape=[shaped((ROWS, 512), BF16), shaped((8, NEW, PAIR), BF16)],
        in_specs=[VMEM] * 4,
        out_specs=[VMEM] * 2,
        compiler_params=params(8),
        cost_estimate=cost(flops=2**20, moved=2**20),
        name="rotated",
    )(keep, got, cosine, sine)


def gather_visible(mine, slabs, halves, new, keys, values, chunk):
    height = keys.shape[0]
    values[:, HD:] = jnp.ones((height, HD), BF16)
    n = jnp.int32(0)
    lane = lax.broadcasted_iota(jnp.int32, (16, HD), 1)
    for load in halves:
        codes = load[ROWS:, :HD].astype(F32)
        codes = jnp.where(lane == 0, 2.0, 1.0) * codes
        place = jnp.max(codes + pltpu.roll(codes, HD - 1, 1)).astype(jnp.int32)
        seen = place < mine

        @pl.when(seen)
        def _(load=load, n=n):
            at = pl.ds(pl.multiple_of(n * NEW, NEW), ROWS)
            keys[at, :] = load[:ROWS, :HD]
            values[at, :HD] = load[:ROWS, HD:]

        n = n + jnp.where(seen, ROWS // NEW, 0)
    if new is not None:
        for z in range(8):
            seen = slabs[z] < mine

            @pl.when(seen)
            def _(z=z, n=n):
                at = pl.ds(pl.multiple_of(n * NEW, NEW), NEW)
                keys[at, :] = new[z, :, :HD]
                values[at, :HD] = new[z, :, HD:]

            n = n + jnp.where(seen, 1, 0)
    per = chunk // NEW
    chunks = (n + per - 1) // per

    def pad(t, carry):
        at = pl.ds(pl.multiple_of(t * NEW, NEW), NEW)
        keys[at, :] = keys[:NEW, :]
        values[at, :] = jnp.zeros((NEW, PAIR), BF16)
        return carry

    lax.fori_loop(n, chunks * per, pad, 0)
    return chunks


def attend(q, peak_ref, chunks, keys, values, scores, chunk, acc_at, before):
    def peaks(i, carry):
        at = pl.ds(pl.multiple_of(i * chunk, chunk), chunk)
        s = lax.dot_general(q, keys[at, :], CONTRACT, preferred_element_type=F32)
        scores[i] = s
        best = peak_ref[...]
        for t in range(chunk // HD):
            best = jnp.maximum(best, s[:, t * HD : (t + 1) * HD])
        peak_ref[...] = best
        return carry

    lax.fori_loop(0, chunks, peaks, 0)
    peak = jnp.max(peak_ref[...], axis=1, keepdims=True)
    acc_at[...] = before(peak)

    def weigh(i, carry):
        at = pl.ds(pl.multiple_of(i * chunk, chunk), chunk)
        p = jnp.exp2((scores[i] - peak) * EXPONENT).astype(BF16)
        acc_at[...] += jnp.dot(p, values[at, :], preferred_element_type=F32)
        return carry

    lax.fori_loop(0, chunks, weigh, 0)
    return peak


def halves_of(buffers):
    halves = []
    for ref in buffers:
        for b in range(ref.shape[0] // HALF):
            halves.append(ref.at[b * HALF : (b + 1) * HALF, :])
    return halves


def near_kernel(slabs, near, far, notes, *refs, chunk, count):
    sources, (q_out, acc_out, peak_out) = refs[:count], refs[count : count + 3]
    refs = refs[count + 3 :]
    near_in, far_in, own, *loads = refs[: 3 + count]
    q_all, acc_all, peak_all, keys, values, scores, peak_ref, sems = refs[3 + count :]
    pairs = list(zip(sources, loads))
    pairs += [(notes.at[0], own), (near, near_in), (far, far_in)]
    copies = fetch(pairs, sems.at[: count + 3])
    mine = slabs[lax.axis_index("key")]
    core = lax.axis_index("hid_1")
    x = lax.axis_index("hid_0")
    for copy in copies[:count]:
        copy.wait()
    chunks = gather_visible(mine, None, halves_of(loads), None, keys, values, chunk)
    for copy in copies[count:]:
        copy.wait()
    for j in range(4):
        half = x if j < 2 else 1 - x
        parity = core if j % 2 == 0 else 1 - core
        cols = pl.ds(pl.multiple_of(parity * PAIR, PAIR), PAIR)
        rows = [slice((2 * j + t) * ROWS, (2 * j + t + 1) * ROWS) for t in range(2)]

        @pl.when(half == core)
        def _(cols=cols, rows=rows):
            both = near_in[:, cols]
            q_all[rows[0], :] = both[:, :HD]
            q_all[rows[1], :] = both[:, HD:]

        @pl.when(half != core)
        def _(cols=cols, rows=rows):
            both = far_in[:, cols]
            q_all[rows[0], :] = both[:, :HD]
            q_all[rows[1], :] = both[:, HD:]

    out = fetch([(q_all, q_out)], sems.at[count + 3 : count + 4])
    zeros = jnp.zeros((NEW, HD), BF16)
    own_keys = jnp.concatenate([own[:, :HD], zeros], axis=0)
    own_values = jnp.concatenate([own[:, HD:], zeros], axis=0)
    own_values = jnp.concatenate([own_values, jnp.ones((HD, HD), BF16)], axis=1)
    row = lax.broadcasted_iota(jnp.int32, (TALL, HD), 0) % ROWS
    lane = lax.broadcasted_iota(jnp.int32, (TALL, HD), 1)
    visible = jnp.logical_and(lane < NEW, lane + new_offset() <= row)
    for step in range(8 * ROWS // TALL):
        at = pl.ds(step * TALL, TALL)
        q = q_all[at, :]
        s = lax.dot_general(q, own_keys, CONTRACT, preferred_element_type=F32)
        s = jnp.where(visible, s, NEGATIVE)
        peak_ref[...] = s

        def before(peak, s=s):
            p = jnp.where(visible, jnp.exp2((s - peak) * EXPONENT), 0.0)
            return jnp.dot(p.astype(BF16), own_values, preferred_element_type=F32)

        peak = attend(
            q, peak_ref, chunks, keys, values, scores, chunk, acc_all.at[at, :], before
        )
        peak_all[at, :] = jnp.broadcast_to(peak, (TALL, HD))
        first_sem = count + 4 + 2 * step
        out += fetch(
            [
                (acc_all.at[at, :], acc_out.at[at, :]),
                (peak_all.at[at, :], peak_out.at[at, :]),
            ],
            sems.at[first_sem : first_sem + 2],
        )
    for copy in out:
        copy.wait()


def attend_near(slabs, near, far, notes, loads):
    count, chunk = len(loads), 1280
    height = count * QUARTER
    state = [((8 * ROWS, HD), BF16), ((8 * ROWS, PAIR), F32), ((8 * ROWS, HD), F32)]
    return pl.pallas_call(
        functools.partial(near_kernel, chunk=chunk, count=count),
        out_shape=[shaped(*s) for s in state],
        in_specs=[SMEM] + [HBM] * (3 + count),
        out_specs=[HBM] * 3,
        scratch_shapes=[
            pltpu.VMEM((ROWS, 4 * HD), BF16),
            pltpu.VMEM((ROWS, 4 * HD), BF16),
            pltpu.VMEM((NEW, PAIR), BF16),
            *[pltpu.VMEM((LOAD, PAIR), BF16)] * count,
            *[pltpu.VMEM(*s) for s in state],
            pltpu.VMEM((height, HD), BF16),
            pltpu.VMEM((height, PAIR), BF16),
            pltpu.VMEM((height // chunk, TALL, chunk), F32),
            pltpu.VMEM((TALL, HD), F32),
            pltpu.SemaphoreType.DMA((count + 4 + 2 * (8 * ROWS // TALL),)),
        ],
        compiler_params=params(),
        cost_estimate=cost(8 * ROWS * height * HD * 6, 2**23, 8 * ROWS * height),
        name="near",
    )(slabs, near, far, notes, *loads)


def far_kernel(slabs, *refs, chunk, count):
    sources, outs = refs[: 4 + count], refs[4 + count : 8 + count]
    refs = refs[8 + count :]
    buffers = refs[: 4 + count]
    queries, acc_in, peak_in, new, *loads = buffers
    keys, values, scores, peak_ref, acc, sems = refs[4 + count :]
    copies = fetch(list(zip(sources, buffers))[::-1], sems)
    mine = slabs[lax.axis_index("key")]
    for copy in copies[: count + 1]:
        copy.wait()
    chunks = gather_visible(mine, slabs, halves_of(loads), new, keys, values, chunk)
    for copy in copies[count + 1 :]:
        copy.wait()
    where = lax.broadcasted_iota(jnp.int32, (16, ROWS), 0)
    for step in range(8 * ROWS // TALL):
        at = slice(step * TALL, (step + 1) * TALL)
        peak_ref[...] = peak_in[at, :]

        def before(peak, at=at):
            factor = jnp.exp2((peak_in[at, :1] - peak) * EXPONENT)
            return acc_in[at, :] * factor

        peak = attend(
            queries[at, :], peak_ref, chunks, keys, values, scores, chunk, acc, before
        )
        total = acc[:, HD:]
        some = total > 0.0
        safe = jnp.where(some, total, 1.0)
        heads = (acc[:, :HD] / safe).astype(BF16)
        level = jnp.where(some, peak * EXPONENT + jnp.log2(safe), NEGATIVE)
        level = jnp.transpose(level)[:1, :]
        for t in range(TALL // (2 * ROWS)):
            out = outs[step * (TALL // (2 * ROWS)) + t]
            table = jnp.zeros((16, ROWS), F32)
            for half in range(2):
                rows = slice((2 * t + half) * ROWS, (2 * t + half + 1) * ROWS)
                out[:ROWS, half * HD : (half + 1) * HD] = heads[rows]
                rest = level[:, rows]
                for k in range(3):
                    coded = rest.astype(BF16).astype(F32)
                    table = jnp.where(where == 3 * half + k, coded, table)
                    rest = rest - coded
            out[ROWS:, :] = table.astype(BF16)


def attend_far(slabs, queries, acc, peak, new, loads):
    operands = [queries, acc, peak, new, *loads]
    count, chunk = len(loads), 1024
    height = sum(a.shape[0] // HALF * ROWS for a in loads) + 8 * NEW
    height = -(-height // chunk) * chunk
    return pl.pallas_call(
        functools.partial(far_kernel, chunk=chunk, count=count),
        out_shape=[shaped((MSG, PAIR), BF16)] * 4,
        in_specs=[SMEM] + [HBM] * len(operands),
        out_specs=[VMEM] * 4,
        scratch_shapes=[
            *[pltpu.VMEM(a.shape, a.dtype) for a in operands],
            pltpu.VMEM((height, HD), BF16),
            pltpu.VMEM((height, PAIR), BF16),
            pltpu.VMEM((height // chunk, TALL, chunk), F32),
            pltpu.VMEM((TALL, HD), F32),
            pltpu.VMEM((TALL, PAIR), F32),
            pltpu.SemaphoreType.DMA((len(operands),)),
        ],
        compiler_params=params(),
        cost_estimate=cost(8 * ROWS * height * HD * 6, 2**23, 8 * ROWS * height),
        name="far",
    )(slabs, *operands)


def merge_kernel(*refs):
    parts, out = refs[:4], refs[4]
    levels = []
    for ref in parts:
        t = ref[ROWS:, :].astype(F32)
        levels.append([t[0:1] + t[1:2] + t[2:3], t[3:4] + t[4:5] + t[5:6]])
    rows = []
    for half in range(2):
        top = functools.reduce(jnp.maximum, [lv[half] for lv in levels])
        w = [jnp.exp2(lv[half] - top) for lv in levels]
        total = w[0] + w[1] + w[2] + w[3]
        rows.extend([x / total for x in w])
    table = jnp.concatenate(rows, axis=0)
    table = jnp.transpose(jnp.concatenate([table, jnp.zeros((HD - 8, ROWS), F32)], axis=0))
    for half in range(2):
        cols = slice(half * HD, (half + 1) * HD)
        so_far = None
        for t, ref in enumerate(parts):
            w = table[:, half * 4 + t : half * 4 + t + 1]
            term = ref[:ROWS, cols].astype(F32) * w
            so_far = term if so_far is None else so_far + term
        out[:, cols] = so_far.astype(BF16)


def merge(parts):
    return pl.pallas_call(
        merge_kernel,
        out_shape=shaped((ROWS, PAIR), BF16),
        in_specs=[VMEM] * 4,
        out_specs=VMEM,
        compiler_params=params(8),
        cost_estimate=cost(10**6, 10**6, 4096),
        name="merge",
    )(*parts)


def project_kernel(*refs):
    heads, weights, send, keep = refs[:4], refs[4:8], refs[8], refs[9]
    core = lax.axis_index("hid_1")
    h = jnp.concatenate([ref[...] for ref in heads], axis=1)
    for out, side in ((send, 1 - core), (keep, core)):
        for t in range(4):
            cols = pl.ds(pl.multiple_of(t * 512 + side * ROWS, ROWS), ROWS)
            w = jnp.concatenate([ref[:, cols] for ref in weights], axis=0)
            total = jnp.dot(h, w, preferred_element_type=F32)
            out[:, t * ROWS : (t + 1) * ROWS] = total.astype(out.dtype)


def project(heads, weights):
    width = weights[0].shape[1]
    return pl.pallas_call(
        project_kernel,
        out_shape=[shaped((ROWS, width // 2), BF16), shaped((ROWS, width // 2), F32)],
        in_specs=[VMEM] * 8,
        out_specs=[VMEM] * 2,
        compiler_params=params(16),
        cost_estimate=cost(flops=2 * ROWS * 8 * HD * width, moved=6 * 2**20),
        name="project",
    )(*heads, *weights)


def split_kernel(keep, got, own, *sends):
    spot = 2 * lax.axis_index("head_0") + lax.axis_index("hid_0")
    for by in range(4):
        cols = pl.ds(pl.multiple_of(lax.rem(spot + by, 4) * ROWS, ROWS), ROWS)
        total = keep[:, cols] + got[:, cols].astype(F32)
        if by == 0:
            own[...] = total
        else:
            sends[by - 1][...] = total.astype(BF16)


def split(keep, got):
    return pl.pallas_call(
        split_kernel,
        out_shape=[shaped((ROWS, ROWS), F32)] + [shaped((ROWS, ROWS), BF16)] * 3,
        in_specs=[VMEM] * 2,
        out_specs=[VMEM] * 4,
        compiler_params=params(8),
        cost_estimate=cost(flops=2**18, moved=2**21),
        name="split",
    )(keep, got)


def body(
    tokens,
    query_weight,
    key_weight,
    value_weight,
    output_weight,
    key_cache,
    value_cache,
    cache_places,
    slab_places,
):
    key_index = lax.axis_index("key")

    load = pack(cache_places, key_cache.reshape(-1, HD), value_cache.reshape(-1, HD))

    def along(array, by):
        return lax.ppermute(array, "key", shift(8, by))

    near_loads = [load] + [along(load, by) for by in (2, -2, 1, -1)]

    pieces = columns(output_weight)
    weights = [pieces[3]]
    for piece, by in zip(pieces, (2, 1, 3)):
        weights.append(lax.ppermute(piece, "head_1", shift(4, by)))

    send, keep = first(tokens, query_weight, key_weight, value_weight)
    send, keep = second(keep, swap(send, "hid_1"))
    got = swap(send, "hid_0")

    middle = HD // 2
    index = np.arange(HD) % middle
    frequency = jnp.exp(jnp.asarray(index, F32) * (-2.0 * math.log(THETA) / HD))
    sign = np.where(np.arange(HD) < middle, -1.0, 1.0).astype(np.float32)
    spots = slab_places[key_index] * ROWS + jnp.arange(ROWS, dtype=jnp.int32)
    angles = spots.astype(F32)[:, None] * frequency[None, :]
    queries, notes = rotated(keep, got, jnp.cos(angles), jnp.sin(angles) * sign[None, :])
    far = swap(queries, "hid_1")

    new = lax.all_to_all(notes, "key", split_axis=0, concat_axis=0, tiled=True)

    _, up, down, _, _ = near_loads
    far_loads = [along(up[:HALF], 2), along(down[HALF:], -2), along(up, 1), along(down, -1)]
    state = attend_near(slab_places, queries, far, notes, near_loads)
    parts = attend_far(slab_places, *state, new, far_loads)
    flip = [(0, 3), (1, 2), (2, 1), (3, 0)]
    merged = merge(
        [
            parts[0],
            swap(parts[1], "hid_1"),
            swap(parts[2], "hid_0"),
            lax.ppermute(parts[3], HID, flip),
        ]
    )

    heads = [merged] + [lax.ppermute(merged, "head_1", shift(4, by)) for by in (2, 1, 3)]
    send, keep = project(heads, weights)
    own, *blocks = split(keep, swap(send, "hid_1"))
    out = own
    for by in (2, 1, 3):
        out = out + lax.ppermute(blocks[by - 1], ALONG_X, shift(4, by)).astype(F32)
    return out.astype(BF16)


def solution(mesh):
    finer = Mesh(
        mesh.devices.reshape(2, 4, mesh.shape["key"], 2, 2),
        ("head_0", "head_1", "key", "hid_0", "hid_1"),
    )
    return jax.shard_map(
        body,
        mesh=finer,
        in_specs=(
            P("key", HID),
            P(HID, HEAD),
            P(HID, HEAD),
            P(HID, HEAD),
            P(HEAD_HID, None),
            P("key", HEAD, None),
            P("key", HEAD, None),
            P("key"),
            P(),
        ),
        out_specs=P("key", HEAD_HID),
        check_vma=False,
    )
```

```python
import functools
import math

import jax
import jax.numpy as jnp
import numpy as np
from jax import lax
from jax.experimental import pallas as pl
from jax.experimental.pallas import tpu as pltpu
from jax.sharding import Mesh
from jax.sharding import PartitionSpec as P

HID = ("hid_0", "hid_1")
HEAD = ("head_0", "head_1")
HEAD_HID = ("head_0", "head_1", "hid_0", "hid_1")
ALONG_X = ("head_0", "hid_0")

THETA = 500000.0
NEGATIVE = -1e30
BF16 = jnp.bfloat16
F32 = jnp.float32

ROWS = 256
HD = 128
PAIR = 2 * HD
NEW = 64
QUARTER = 512
HALF = ROWS + 16
LOAD = 4 * HALF
MSG = ROWS + 16
TALL = 1024
EXPONENT = math.log2(math.e) / math.sqrt(HD)
CONTRACT = (((1,), (1,)), ((), ()))

VMEM = pl.BlockSpec(memory_space=pltpu.VMEM)
SMEM = pl.BlockSpec(memory_space=pltpu.SMEM)
HBM = pl.BlockSpec(memory_space=pltpu.HBM)


def shaped(shape, dtype):
    return jax.ShapeDtypeStruct(shape, dtype)


def params(mib=60):
    return pltpu.CompilerParams(vmem_limit_bytes=mib * 2**20)


def cost(flops=0, moved=0, exps=0):
    return pl.CostEstimate(flops=flops, bytes_accessed=moved, transcendentals=exps)


def shift(n, by):
    return [(i, (i + by) % n) for i in range(n)]


def swap(array, axis):
    return lax.ppermute(array, axis, shift(2, 1))


def hid_index():
    return 2 * lax.axis_index("hid_0") + lax.axis_index("hid_1")


def fetch(pairs, sems):
    copies = [
        pltpu.make_async_copy(source, target, sems.at[i])
        for i, (source, target) in enumerate(pairs)
    ]
    for copy in copies:
        copy.start()
    return copies


def pack_kernel(places, keys, values, out, load, sems):
    core = lax.axis_index("hid_1")
    lane = lax.broadcasted_iota(jnp.int32, (16, PAIR), 1)
    pairs = []
    for i in range(4):
        block = 4 * lax.axis_index("hid_0") + lax.rem(2 * core + i, 4)
        rows = pl.ds(pl.multiple_of(block * ROWS, ROWS), ROWS)
        to = slice(i * HALF, i * HALF + ROWS)
        pairs.append((keys.at[rows, :], load.at[to, :HD]))
        pairs.append((values.at[rows, :], load.at[to, HD:]))
        place = places[block]
        table = jnp.where(lane == 0, place >> 1, jnp.where(lane == 1, place & 1, 0))
        load[i * HALF + ROWS : (i + 1) * HALF, :] = table.astype(F32).astype(BF16)
    copies = fetch(pairs, sems.at[:8])
    for copy in copies:
        copy.wait()
    for copy in fetch([(load, out)], sems.at[8:]):
        copy.wait()


def pack(places, keys, values):
    return pl.pallas_call(
        pack_kernel,
        out_shape=shaped((LOAD, PAIR), BF16),
        in_specs=[SMEM, HBM, HBM],
        out_specs=HBM,
        scratch_shapes=[pltpu.VMEM((LOAD, PAIR), BF16), pltpu.SemaphoreType.DMA((9,))],
        compiler_params=params(),
        cost_estimate=cost(moved=2**19),
        name="pack",
    )(places, keys, values)


def columns_kernel(weight, *refs):
    outs, pieces, sems, out_sems = refs[:4], refs[4], refs[5], refs[6]
    y = lax.axis_index("head_1")
    pairs = []
    for t, by in enumerate((2, 1, 3, 0)):
        at = lax.rem(y + by, 4) * 1024
        for hi in range(2):
            source = pl.ds(pl.multiple_of(hi * 4096 + at, 1024), 1024)
            pairs.append((weight.at[:, source], pieces.at[t, :, hi * 1024 : (hi + 1) * 1024]))
    copies = fetch(pairs, sems)
    leaving = []
    for t in range(4):
        copies[2 * t].wait()
        copies[2 * t + 1].wait()
        leaving += fetch([(pieces.at[t], outs[t])], out_sems.at[t : t + 1])
    for copy in leaving:
        copy.wait()


def columns(weight):
    return pl.pallas_call(
        columns_kernel,
        out_shape=[shaped((ROWS, 2048), BF16)] * 4,
        in_specs=[HBM],
        out_specs=[HBM] * 4,
        scratch_shapes=[
            pltpu.VMEM((4, ROWS, 2048), BF16),
            pltpu.SemaphoreType.DMA((8,)),
            pltpu.SemaphoreType.DMA((4,)),
        ],
        compiler_params=params(),
        cost_estimate=cost(moved=8 * 2**20),
        name="columns",
    )(weight)


def first_kernel(
    tokens, query, key, value, send, keep, tok, tiles, kv, fresh, sems
):
    core = lax.axis_index("hid_1")
    pairs = [(tokens, tok)]
    for t in range(4):
        side = 1 - core if t < 2 else core
        cols = pl.ds(pl.multiple_of(side * 512 + (t % 2) * ROWS, ROWS), ROWS)
        pairs.append((query.at[:, cols], tiles.at[t]))
        if t == 1:
            pairs.append((key, kv.at[0]))
            pairs.append((value, kv.at[1]))
    copies = fetch(pairs, sems)
    copies[0].wait()

    def part(t):
        return jnp.dot(tok[...], tiles[t], preferred_element_type=F32)

    for t in range(2):
        copies[1 + t].wait()
        send[:ROWS, t * ROWS : (t + 1) * ROWS] = part(t).astype(BF16)
    copies[3].wait()
    copies[4].wait()
    both = jnp.concatenate([kv[0], kv[1]], axis=1)
    fresh[...] = jnp.dot(tok[...], both, preferred_element_type=F32)
    for t in range(2):
        cols = slice(t * PAIR, (t + 1) * PAIR)
        far = pl.ds(pl.multiple_of((1 - core) * 128 + t * NEW, NEW), NEW)
        near = pl.ds(pl.multiple_of(core * 128 + t * NEW, NEW), NEW)
        send[ROWS:, cols] = fresh[far, :].astype(BF16)
        keep[ROWS:, cols] = fresh[near, :]
    for t in range(2):
        copies[5 + t].wait()
        keep[:ROWS, t * ROWS : (t + 1) * ROWS] = part(2 + t)


def first(tokens, query, key, value):
    deep = tokens.shape[1]
    return pl.pallas_call(
        first_kernel,
        out_shape=[shaped((320, 512), BF16), shaped((320, 512), F32)],
        in_specs=[HBM] * 4,
        out_specs=[VMEM] * 2,
        scratch_shapes=[
            pltpu.VMEM((ROWS, deep), BF16),
            pltpu.VMEM((4, deep, ROWS), BF16),
            pltpu.VMEM((2, deep, HD), BF16),
            pltpu.VMEM((ROWS, PAIR), F32),
            pltpu.SemaphoreType.DMA((7,)),
        ],
        compiler_params=params(),
        cost_estimate=cost(flops=2 * 256 * 2048 * 1280, moved=6 * 2**20),
        name="first",
    )(tokens, query, key, value)


def second_kernel(keep, got, send, onward):
    x = lax.axis_index("hid_0")
    q = keep[:ROWS, :] + got[:ROWS, :].astype(F32)
    send[:ROWS, :] = q.astype(BF16)
    onward[:ROWS, :] = q
    low = keep[ROWS:, :] + got[ROWS:, :].astype(F32)
    sides = [low[:, :PAIR], low[:, PAIR:]]
    sides = [jnp.concatenate([s[:32], s[32:]], axis=1) for s in sides]
    mine = jnp.where(x == 0, sides[0], sides[1])
    other = jnp.where(x == 0, sides[1], sides[0])
    send[ROWS:, :] = other.astype(BF16)
    onward[ROWS:, :] = mine


def second(keep, got):
    return pl.pallas_call(
        second_kernel,
        out_shape=[shaped((288, 512), BF16), shaped((288, 512), F32)],
        in_specs=[VMEM] * 2,
        out_specs=[VMEM] * 2,
        compiler_params=params(8),
        cost_estimate=cost(flops=2**18, moved=2**20),
        name="second",
    )(keep, got)


def new_offset():
    return lax.axis_index("hid_1") * 128 + lax.axis_index("hid_0") * NEW


def rotate_kernel(keep, got, cosine, sine, queries, notes):
    for h in range(4):
        cols = slice(h * HD, (h + 1) * HD)
        u = keep[:ROWS, cols] + got[:ROWS, cols].astype(F32)
        turned = u * cosine[...] + pltpu.roll(u, HD // 2, 1) * sine[...]
        queries[:, cols] = turned.astype(BF16)
    low = keep[ROWS:, :] + got[ROWS:, :].astype(F32)
    low = jnp.concatenate([low[:, :PAIR], low[:, PAIR:]], axis=0)
    rows = pl.ds(pl.multiple_of(new_offset(), NEW), NEW)
    u = low[:, :HD]
    turned = u * cosine[rows, :] + pltpu.roll(u, HD // 2, 1) * sine[rows, :]
    for z in range(8):
        notes[z, :, :HD] = turned.astype(BF16)
        notes[z, :, HD:] = low[:, HD:].astype(BF16)


def rotated(keep, got, cosine, sine):
    return pl.pallas_call(
        rotate_kernel,
        out_shape=[shaped((ROWS, 512), BF16), shaped((8, NEW, PAIR), BF16)],
        in_specs=[VMEM] * 4,
        out_specs=[VMEM] * 2,
        compiler_params=params(8),
        cost_estimate=cost(flops=2**20, moved=2**20),
        name="rotated",
    )(keep, got, cosine, sine)


def gather_visible(mine, slabs, halves, new, keys, values, chunk):
    height = keys.shape[0]
    values[:, HD:] = jnp.ones((height, HD), BF16)
    n = jnp.int32(0)
    lane = lax.broadcasted_iota(jnp.int32, (16, HD), 1)
    for load in halves:
        codes = load[ROWS:, :HD].astype(F32)
        codes = jnp.where(lane == 0, 2.0, 1.0) * codes
        place = jnp.max(codes + pltpu.roll(codes, HD - 1, 1)).astype(jnp.int32)
        seen = place < mine

        @pl.when(seen)
        def _(load=load, n=n):
            at = pl.ds(pl.multiple_of(n * NEW, NEW), ROWS)
            keys[at, :] = load[:ROWS, :HD]
            values[at, :HD] = load[:ROWS, HD:]

        n = n + jnp.where(seen, ROWS // NEW, 0)
    if new is not None:
        for z in range(8):
            seen = slabs[z] < mine

            @pl.when(seen)
            def _(z=z, n=n):
                at = pl.ds(pl.multiple_of(n * NEW, NEW), NEW)
                keys[at, :] = new[z, :, :HD]
                values[at, :HD] = new[z, :, HD:]

            n = n + jnp.where(seen, 1, 0)
    per = chunk // NEW
    chunks = (n + per - 1) // per

    def pad(t, carry):
        at = pl.ds(pl.multiple_of(t * NEW, NEW), NEW)
        keys[at, :] = keys[:NEW, :]
        values[at, :] = jnp.zeros((NEW, PAIR), BF16)
        return carry

    lax.fori_loop(n, chunks * per, pad, 0)
    return chunks


def attend(q, peak_ref, chunks, keys, values, scores, chunk, acc_at, before):
    def peaks(i, carry):
        at = pl.ds(pl.multiple_of(i * chunk, chunk), chunk)
        s = lax.dot_general(q, keys[at, :], CONTRACT, preferred_element_type=F32)
        scores[i] = s
        best = peak_ref[...]
        for t in range(chunk // HD):
            best = jnp.maximum(best, s[:, t * HD : (t + 1) * HD])
        peak_ref[...] = best
        return carry

    lax.fori_loop(0, chunks, peaks, 0)
    peak = jnp.max(peak_ref[...], axis=1, keepdims=True)
    acc_at[...] = before(peak)

    def weigh(i, carry):
        at = pl.ds(pl.multiple_of(i * chunk, chunk), chunk)
        p = jnp.exp2((scores[i] - peak) * EXPONENT).astype(BF16)
        acc_at[...] += jnp.dot(p, values[at, :], preferred_element_type=F32)
        return carry

    lax.fori_loop(0, chunks, weigh, 0)
    return peak


def halves_of(buffers):
    halves = []
    for ref in buffers:
        for b in range(ref.shape[0] // HALF):
            halves.append(ref.at[b * HALF : (b + 1) * HALF, :])
    return halves


def near_kernel(slabs, near, far, notes, *refs, chunk, count):
    sources, (q_out, acc_out, peak_out) = refs[:count], refs[count : count + 3]
    refs = refs[count + 3 :]
    near_in, far_in, own, *loads = refs[: 3 + count]
    q_all, acc_all, peak_all, keys, values, scores, peak_ref, sems = refs[3 + count :]
    pairs = [(sources[0].at[: 2 * HALF, :], loads[0])] + list(zip(sources[1:], loads[1:]))
    pairs += [(notes.at[0], own), (near, near_in), (far, far_in)]
    copies = fetch(pairs, sems.at[: count + 3])
    mine = slabs[lax.axis_index("key")]
    core = lax.axis_index("hid_1")
    x = lax.axis_index("hid_0")
    for copy in copies[:count]:
        copy.wait()
    chunks = gather_visible(mine, None, halves_of(loads), None, keys, values, chunk)
    for copy in copies[count:]:
        copy.wait()
    for j in range(4):
        half = x if j < 2 else 1 - x
        parity = core if j % 2 == 0 else 1 - core
        cols = pl.ds(pl.multiple_of(parity * PAIR, PAIR), PAIR)
        rows = [slice((2 * j + t) * ROWS, (2 * j + t + 1) * ROWS) for t in range(2)]

        @pl.when(half == core)
        def _(cols=cols, rows=rows):
            both = near_in[:, cols]
            q_all[rows[0], :] = both[:, :HD]
            q_all[rows[1], :] = both[:, HD:]

        @pl.when(half != core)
        def _(cols=cols, rows=rows):
            both = far_in[:, cols]
            q_all[rows[0], :] = both[:, :HD]
            q_all[rows[1], :] = both[:, HD:]

    out = fetch([(q_all, q_out)], sems.at[count + 3 : count + 4])
    zeros = jnp.zeros((NEW, HD), BF16)
    own_keys = jnp.concatenate([own[:, :HD], zeros], axis=0)
    own_values = jnp.concatenate([own[:, HD:], zeros], axis=0)
    own_values = jnp.concatenate([own_values, jnp.ones((HD, HD), BF16)], axis=1)
    row = lax.broadcasted_iota(jnp.int32, (TALL, HD), 0) % ROWS
    lane = lax.broadcasted_iota(jnp.int32, (TALL, HD), 1)
    visible = jnp.logical_and(lane < NEW, lane + new_offset() <= row)
    for step in range(8 * ROWS // TALL):
        at = pl.ds(step * TALL, TALL)
        q = q_all[at, :]
        s = lax.dot_general(q, own_keys, CONTRACT, preferred_element_type=F32)
        s = jnp.where(visible, s, NEGATIVE)
        peak_ref[...] = s

        def before(peak, s=s):
            p = jnp.where(visible, jnp.exp2((s - peak) * EXPONENT), 0.0)
            return jnp.dot(p.astype(BF16), own_values, preferred_element_type=F32)

        peak = attend(
            q, peak_ref, chunks, keys, values, scores, chunk, acc_all.at[at, :], before
        )
        peak_all[at, :] = jnp.broadcast_to(peak, (TALL, HD))
        first_sem = count + 4 + 2 * step
        out += fetch(
            [
                (acc_all.at[at, :], acc_out.at[at, :]),
                (peak_all.at[at, :], peak_out.at[at, :]),
            ],
            sems.at[first_sem : first_sem + 2],
        )
    for copy in out:
        copy.wait()


def attend_near(slabs, near, far, notes, loads):
    count, chunk = len(loads), 1792
    height = (2 + 4 * (count - 1)) * ROWS
    state = [((8 * ROWS, HD), BF16), ((8 * ROWS, PAIR), F32), ((8 * ROWS, HD), F32)]
    return pl.pallas_call(
        functools.partial(near_kernel, chunk=chunk, count=count),
        out_shape=[shaped(*s) for s in state],
        in_specs=[SMEM] + [HBM] * (3 + count),
        out_specs=[HBM] * 3,
        scratch_shapes=[
            pltpu.VMEM((ROWS, 4 * HD), BF16),
            pltpu.VMEM((ROWS, 4 * HD), BF16),
            pltpu.VMEM((NEW, PAIR), BF16),
            pltpu.VMEM((2 * HALF, PAIR), BF16),
            *[pltpu.VMEM((LOAD, PAIR), BF16)] * (count - 1),
            *[pltpu.VMEM(*s) for s in state],
            pltpu.VMEM((height, HD), BF16),
            pltpu.VMEM((height, PAIR), BF16),
            pltpu.VMEM((height // chunk, TALL, chunk), F32),
            pltpu.VMEM((TALL, HD), F32),
            pltpu.SemaphoreType.DMA((count + 4 + 2 * (8 * ROWS // TALL),)),
        ],
        compiler_params=params(),
        cost_estimate=cost(8 * ROWS * height * HD * 6, 2**23, 8 * ROWS * height),
        name="near",
    )(slabs, near, far, notes, *loads)


def far_kernel(slabs, *refs, chunk, count):
    sources, outs = refs[: 4 + count], refs[4 + count : 8 + count]
    refs = refs[8 + count :]
    buffers = refs[: 4 + count]
    queries, acc_in, peak_in, new, *loads = buffers
    keys, values, scores, peak_ref, acc, sems = refs[4 + count :]
    copies = fetch(list(zip(sources, buffers))[::-1], sems)
    mine = slabs[lax.axis_index("key")]
    for copy in copies[: count + 1]:
        copy.wait()
    chunks = gather_visible(mine, slabs, halves_of(loads), new, keys, values, chunk)
    for copy in copies[count + 1 :]:
        copy.wait()
    where = lax.broadcasted_iota(jnp.int32, (16, ROWS), 0)
    for step in range(8 * ROWS // TALL):
        at = slice(step * TALL, (step + 1) * TALL)
        peak_ref[...] = peak_in[at, :]

        def before(peak, at=at):
            factor = jnp.exp2((peak_in[at, :1] - peak) * EXPONENT)
            return acc_in[at, :] * factor

        peak = attend(
            queries[at, :], peak_ref, chunks, keys, values, scores, chunk, acc, before
        )
        total = acc[:, HD:]
        some = total > 0.0
        safe = jnp.where(some, total, 1.0)
        heads = (acc[:, :HD] / safe).astype(BF16)
        level = jnp.where(some, peak * EXPONENT + jnp.log2(safe), NEGATIVE)
        level = jnp.transpose(level)[:1, :]
        for t in range(TALL // (2 * ROWS)):
            out = outs[step * (TALL // (2 * ROWS)) + t]
            table = jnp.zeros((16, ROWS), F32)
            for half in range(2):
                rows = slice((2 * t + half) * ROWS, (2 * t + half + 1) * ROWS)
                out[:ROWS, half * HD : (half + 1) * HD] = heads[rows]
                rest = level[:, rows]
                for k in range(3):
                    coded = rest.astype(BF16).astype(F32)
                    table = jnp.where(where == 3 * half + k, coded, table)
                    rest = rest - coded
            out[ROWS:, :] = table.astype(BF16)


def attend_far(slabs, queries, acc, peak, new, loads):
    operands = [queries, acc, peak, new, *loads]
    count, chunk = len(loads), 1024
    height = sum(a.shape[0] // HALF * ROWS for a in loads) + 8 * NEW
    height = -(-height // chunk) * chunk
    return pl.pallas_call(
        functools.partial(far_kernel, chunk=chunk, count=count),
        out_shape=[shaped((MSG, PAIR), BF16)] * 4,
        in_specs=[SMEM] + [HBM] * len(operands),
        out_specs=[VMEM] * 4,
        scratch_shapes=[
            *[pltpu.VMEM(a.shape, a.dtype) for a in operands],
            pltpu.VMEM((height, HD), BF16),
            pltpu.VMEM((height, PAIR), BF16),
            pltpu.VMEM((height // chunk, TALL, chunk), F32),
            pltpu.VMEM((TALL, HD), F32),
            pltpu.VMEM((TALL, PAIR), F32),
            pltpu.SemaphoreType.DMA((len(operands),)),
        ],
        compiler_params=params(),
        cost_estimate=cost(8 * ROWS * height * HD * 6, 2**23, 8 * ROWS * height),
        name="far",
    )(slabs, *operands)


def merge_kernel(*refs):
    parts, out = refs[:4], refs[4]
    levels = []
    for ref in parts:
        t = ref[ROWS:, :].astype(F32)
        levels.append([t[0:1] + t[1:2] + t[2:3], t[3:4] + t[4:5] + t[5:6]])
    rows = []
    for half in range(2):
        top = functools.reduce(jnp.maximum, [lv[half] for lv in levels])
        w = [jnp.exp2(lv[half] - top) for lv in levels]
        total = w[0] + w[1] + w[2] + w[3]
        rows.extend([x / total for x in w])
    table = jnp.concatenate(rows, axis=0)
    table = jnp.transpose(jnp.concatenate([table, jnp.zeros((HD - 8, ROWS), F32)], axis=0))
    for half in range(2):
        cols = slice(half * HD, (half + 1) * HD)
        so_far = None
        for t, ref in enumerate(parts):
            w = table[:, half * 4 + t : half * 4 + t + 1]
            term = ref[:ROWS, cols].astype(F32) * w
            so_far = term if so_far is None else so_far + term
        out[:, cols] = so_far.astype(BF16)


def merge(parts):
    return pl.pallas_call(
        merge_kernel,
        out_shape=shaped((ROWS, PAIR), BF16),
        in_specs=[VMEM] * 4,
        out_specs=VMEM,
        compiler_params=params(8),
        cost_estimate=cost(10**6, 10**6, 4096),
        name="merge",
    )(*parts)


def project_kernel(*refs):
    heads, weights, send, keep = refs[:4], refs[4:8], refs[8], refs[9]
    core = lax.axis_index("hid_1")
    h = jnp.concatenate([ref[...] for ref in heads], axis=1)
    for out, side in ((send, 1 - core), (keep, core)):
        for t in range(4):
            cols = pl.ds(pl.multiple_of(t * 512 + side * ROWS, ROWS), ROWS)
            w = jnp.concatenate([ref[:, cols] for ref in weights], axis=0)
            total = jnp.dot(h, w, preferred_element_type=F32)
            out[:, t * ROWS : (t + 1) * ROWS] = total.astype(out.dtype)


def project(heads, weights):
    width = weights[0].shape[1]
    return pl.pallas_call(
        project_kernel,
        out_shape=[shaped((ROWS, width // 2), BF16), shaped((ROWS, width // 2), F32)],
        in_specs=[VMEM] * 8,
        out_specs=[VMEM] * 2,
        compiler_params=params(16),
        cost_estimate=cost(flops=2 * ROWS * 8 * HD * width, moved=6 * 2**20),
        name="project",
    )(*heads, *weights)


def split_kernel(keep, got, own, *sends):
    spot = 2 * lax.axis_index("head_0") + lax.axis_index("hid_0")
    for by in range(4):
        cols = pl.ds(pl.multiple_of(lax.rem(spot + by, 4) * ROWS, ROWS), ROWS)
        total = keep[:, cols] + got[:, cols].astype(F32)
        if by == 0:
            own[...] = total
        else:
            sends[by - 1][...] = total.astype(BF16)


def split(keep, got):
    return pl.pallas_call(
        split_kernel,
        out_shape=[shaped((ROWS, ROWS), F32)] + [shaped((ROWS, ROWS), BF16)] * 3,
        in_specs=[VMEM] * 2,
        out_specs=[VMEM] * 4,
        compiler_params=params(8),
        cost_estimate=cost(flops=2**18, moved=2**21),
        name="split",
    )(keep, got)


def body(
    tokens,
    query_weight,
    key_weight,
    value_weight,
    output_weight,
    key_cache,
    value_cache,
    cache_places,
    slab_places,
):
    key_index = lax.axis_index("key")

    load = pack(cache_places, key_cache.reshape(-1, HD), value_cache.reshape(-1, HD))

    def away(array, by):
        pairs = []
        for k in range(8):
            pairs.append((2 * k, 2 * ((k + by) % 8)))
            pairs.append((2 * k + 1, 2 * ((k - by) % 8) + 1))
        return lax.ppermute(array, ("key", "hid_1"), pairs)

    one = away(load, 1)

    pieces = columns(output_weight)

    send, keep = first(tokens, query_weight, key_weight, value_weight)
    one, keep = lax.optimization_barrier((one, keep))
    two = away(one, 1)
    send, keep = second(keep, swap(send, "hid_1"))
    got = swap(send, "hid_0")
    keep, pieces = lax.optimization_barrier((keep, pieces))
    weights = [pieces[3]]
    for piece, by in zip(pieces, (2, 1, 3)):
        weights.append(lax.ppermute(piece, "head_1", shift(4, by)))

    middle = HD // 2
    index = np.arange(HD) % middle
    frequency = jnp.exp(jnp.asarray(index, F32) * (-2.0 * math.log(THETA) / HD))
    sign = np.where(np.arange(HD) < middle, -1.0, 1.0).astype(np.float32)
    spots = slab_places[key_index] * ROWS + jnp.arange(ROWS, dtype=jnp.int32)
    angles = spots.astype(F32)[:, None] * frequency[None, :]
    queries, notes = rotated(keep, got, jnp.cos(angles), jnp.sin(angles) * sign[None, :])
    two, queries, notes = lax.optimization_barrier((two, queries, notes))
    three = away(two, 1)
    far = swap(queries, "hid_1")

    new = lax.all_to_all(notes, "key", split_axis=0, concat_axis=0, tiled=True)

    four = away(three[: 2 * HALF], 1)
    state = attend_near(slab_places, queries, far, notes, [load, one, two, three])
    parts = attend_far(slab_places, *state, new, [four])
    flip = [(0, 3), (1, 2), (2, 1), (3, 0)]
    merged = merge(
        [
            parts[0],
            swap(parts[1], "hid_1"),
            swap(parts[2], "hid_0"),
            lax.ppermute(parts[3], HID, flip),
        ]
    )

    heads = [merged] + [lax.ppermute(merged, "head_1", shift(4, by)) for by in (2, 1, 3)]
    send, keep = project(heads, weights)
    own, *blocks = split(keep, swap(send, "hid_1"))
    out = own
    for by in (2, 1, 3):
        out = out + lax.ppermute(blocks[by - 1], ALONG_X, shift(4, by)).astype(F32)
    return out.astype(BF16)


def solution(mesh):
    finer = Mesh(
        mesh.devices.reshape(2, 4, mesh.shape["key"], 2, 2),
        ("head_0", "head_1", "key", "hid_0", "hid_1"),
    )
    return jax.shard_map(
        body,
        mesh=finer,
        in_specs=(
            P("key", HID),
            P(HID, HEAD),
            P(HID, HEAD),
            P(HID, HEAD),
            P(HEAD_HID, None),
            P("key", HEAD, None),
            P("key", HEAD, None),
            P("key"),
            P(),
        ),
        out_specs=P("key", HEAD_HID),
        check_vma=False,
    )
```

```python
import functools
import math

import jax
import jax.numpy as jnp
import numpy as np
from jax import lax
from jax.experimental import pallas as pl
from jax.experimental.pallas import tpu as pltpu
from jax.sharding import Mesh
from jax.sharding import PartitionSpec as P

HID = ("hid_0", "hid_1")
HEAD = ("head_0", "head_1")
HEAD_HID = ("head_0", "head_1", "hid_0", "hid_1")
ALONG_X = ("head_0", "hid_0")

THETA = 500000.0
NEGATIVE = -1e30
BF16 = jnp.bfloat16
F32 = jnp.float32

ROWS = 256
HD = 128
PAIR = 2 * HD
NEW = 64
QUARTER = 512
HALF = ROWS + 16
LOAD = 4 * HALF
MSG = ROWS + 16
TALL = 1024
EXPONENT = math.log2(math.e) / math.sqrt(HD)
CONTRACT = (((1,), (1,)), ((), ()))

VMEM = pl.BlockSpec(memory_space=pltpu.VMEM)
SMEM = pl.BlockSpec(memory_space=pltpu.SMEM)
HBM = pl.BlockSpec(memory_space=pltpu.HBM)


def shaped(shape, dtype):
    return jax.ShapeDtypeStruct(shape, dtype)


def params(mib=60):
    return pltpu.CompilerParams(vmem_limit_bytes=mib * 2**20)


SMALL = pl.CostEstimate(flops=1, bytes_accessed=1, transcendentals=0)
MEDIUM = pl.CostEstimate(flops=2**27, bytes_accessed=2**18, transcendentals=2**10)


def shift(n, by):
    return [(i, (i + by) % n) for i in range(n)]


def swap(array, axis):
    return lax.ppermute(array, axis, shift(2, 1))


def hid_index():
    return 2 * lax.axis_index("hid_0") + lax.axis_index("hid_1")


def fetch(pairs, sems):
    copies = [
        pltpu.make_async_copy(source, target, sems.at[i])
        for i, (source, target) in enumerate(pairs)
    ]
    for copy in copies:
        copy.start()
    return copies


def pack_kernel(places, keys, values, out, load, sems):
    core = lax.axis_index("hid_1")
    lane = lax.broadcasted_iota(jnp.int32, (16, PAIR), 1)
    pairs = []
    for i in range(4):
        block = 4 * lax.axis_index("hid_0") + lax.rem(2 * core + i, 4)
        rows = pl.ds(pl.multiple_of(block * ROWS, ROWS), ROWS)
        to = slice(i * HALF, i * HALF + ROWS)
        pairs.append((keys.at[rows, :], load.at[to, :HD]))
        pairs.append((values.at[rows, :], load.at[to, HD:]))
        place = places[block]
        table = jnp.where(lane == 0, place >> 1, jnp.where(lane == 1, place & 1, 0))
        load[i * HALF + ROWS : (i + 1) * HALF, :] = table.astype(F32).astype(BF16)
    copies = fetch(pairs, sems.at[:8])
    leaving = []
    for i in range(4):
        copies[2 * i].wait()
        copies[2 * i + 1].wait()
        to = slice(i * HALF, (i + 1) * HALF)
        leaving += fetch([(load.at[to, :], out.at[to, :])], sems.at[8 + i : 9 + i])
    for copy in leaving:
        copy.wait()


def pack(places, keys, values):
    return pl.pallas_call(
        pack_kernel,
        out_shape=shaped((LOAD, PAIR), BF16),
        in_specs=[SMEM, HBM, HBM],
        out_specs=HBM,
        scratch_shapes=[pltpu.VMEM((LOAD, PAIR), BF16), pltpu.SemaphoreType.DMA((12,))],
        compiler_params=params(),
        cost_estimate=SMALL,
        name="pack",
    )(places, keys, values)


def columns_kernel(weight, *refs):
    outs, pieces, sems, out_sems = refs[:4], refs[4], refs[5], refs[6]
    y = lax.axis_index("head_1")
    pairs = []
    for t, by in enumerate((2, 1, 3, 0)):
        at = lax.rem(y + by, 4) * 1024
        for hi in range(2):
            source = pl.ds(pl.multiple_of(hi * 4096 + at, 1024), 1024)
            pairs.append((weight.at[:, source], pieces.at[t, :, hi * 1024 : (hi + 1) * 1024]))
    copies = fetch(pairs, sems)
    leaving = []
    for t in range(4):
        copies[2 * t].wait()
        copies[2 * t + 1].wait()
        leaving += fetch([(pieces.at[t], outs[t])], out_sems.at[t : t + 1])
    for copy in leaving:
        copy.wait()


def columns(weight):
    return pl.pallas_call(
        columns_kernel,
        out_shape=[shaped((ROWS, 2048), BF16)] * 4,
        in_specs=[HBM],
        out_specs=[HBM] * 4,
        scratch_shapes=[
            pltpu.VMEM((4, ROWS, 2048), BF16),
            pltpu.SemaphoreType.DMA((8,)),
            pltpu.SemaphoreType.DMA((4,)),
        ],
        compiler_params=params(),
        cost_estimate=SMALL,
        name="columns",
    )(weight)


def first_kernel(tokens, query, key, value, send, keep, tok, wide, kv, sent, fresh, sems):
    core = lax.axis_index("hid_1")
    deep = tok.shape[2]
    copies = []
    for t in range(4):
        part = slice(t * deep, (t + 1) * deep)
        pairs = [
            (tokens.at[:, part], tok.at[t]),
            (query.at[part, :], wide.at[t]),
            (key.at[part, :], kv.at[t, :, :HD]),
            (value.at[part, :], kv.at[t, :, HD:]),
        ]
        copies.append(fetch(pairs, sems.at[4 * t : 4 * t + 4]))
    far_cols = pl.ds(pl.multiple_of((1 - core) * 512, 512), 512)
    near_cols = pl.ds(pl.multiple_of(core * 512, 512), 512)
    for t in range(4):
        for copy in copies[t]:
            copy.wait()
        a = tok[t]
        far = jnp.dot(a, wide[t, :, far_cols], preferred_element_type=F32)
        near = jnp.dot(a, wide[t, :, near_cols], preferred_element_type=F32)
        new = jnp.dot(a, kv[t], preferred_element_type=F32)
        if t == 0:
            sent[...] = far
            keep[:ROWS, :] = near
            fresh[...] = new
        else:
            keep[:ROWS, :] += near
            fresh[...] += new
            if t == 3:
                send[:ROWS, :] = (sent[...] + far).astype(BF16)
            else:
                sent[...] += far
    for t in range(2):
        cols = slice(t * PAIR, (t + 1) * PAIR)
        far_rows = pl.ds(pl.multiple_of((1 - core) * 128 + t * NEW, NEW), NEW)
        near_rows = pl.ds(pl.multiple_of(core * 128 + t * NEW, NEW), NEW)
        send[ROWS:, cols] = fresh[far_rows, :].astype(BF16)
        keep[ROWS:, cols] = fresh[near_rows, :]


def first(tokens, query, key, value):
    deep = tokens.shape[1] // 4
    return pl.pallas_call(
        first_kernel,
        out_shape=[shaped((320, 512), BF16), shaped((320, 512), F32)],
        in_specs=[HBM] * 4,
        out_specs=[VMEM] * 2,
        scratch_shapes=[
            pltpu.VMEM((4, ROWS, deep), BF16),
            pltpu.VMEM((4, deep, query.shape[1]), BF16),
            pltpu.VMEM((4, deep, PAIR), BF16),
            pltpu.VMEM((ROWS, 512), F32),
            pltpu.VMEM((ROWS, PAIR), F32),
            pltpu.SemaphoreType.DMA((16,)),
        ],
        compiler_params=params(),
        cost_estimate=SMALL,
        name="first",
    )(tokens, query, key, value)


def second_kernel(keep, got, send, onward):
    x = lax.axis_index("hid_0")
    q = keep[:ROWS, :] + got[:ROWS, :].astype(F32)
    send[:ROWS, :] = q.astype(BF16)
    onward[:ROWS, :] = q
    low = keep[ROWS:, :] + got[ROWS:, :].astype(F32)
    sides = [low[:, :PAIR], low[:, PAIR:]]
    sides = [jnp.concatenate([s[:32], s[32:]], axis=1) for s in sides]
    mine = jnp.where(x == 0, sides[0], sides[1])
    other = jnp.where(x == 0, sides[1], sides[0])
    send[ROWS:, :] = other.astype(BF16)
    onward[ROWS:, :] = mine


def second(keep, got):
    return pl.pallas_call(
        second_kernel,
        out_shape=[shaped((288, 512), BF16), shaped((288, 512), F32)],
        in_specs=[VMEM] * 2,
        out_specs=[VMEM] * 2,
        compiler_params=params(8),
        cost_estimate=SMALL,
        name="second",
    )(keep, got)


def new_offset():
    return lax.axis_index("hid_1") * 128 + lax.axis_index("hid_0") * NEW


def rotate_kernel(keep, got, cosine, sine, queries, notes):
    for h in range(4):
        cols = slice(h * HD, (h + 1) * HD)
        u = keep[:ROWS, cols] + got[:ROWS, cols].astype(F32)
        turned = u * cosine[...] + pltpu.roll(u, HD // 2, 1) * sine[...]
        queries[:, cols] = turned.astype(BF16)
    low = keep[ROWS:, :] + got[ROWS:, :].astype(F32)
    low = jnp.concatenate([low[:, :PAIR], low[:, PAIR:]], axis=0)
    rows = pl.ds(pl.multiple_of(new_offset(), NEW), NEW)
    u = low[:, :HD]
    turned = u * cosine[rows, :] + pltpu.roll(u, HD // 2, 1) * sine[rows, :]
    for z in range(8):
        notes[z, :, :HD] = turned.astype(BF16)
        notes[z, :, HD:] = low[:, HD:].astype(BF16)


def rotated(keep, got, cosine, sine):
    return pl.pallas_call(
        rotate_kernel,
        out_shape=[shaped((ROWS, 512), BF16), shaped((8, NEW, PAIR), BF16)],
        in_specs=[VMEM] * 4,
        out_specs=[VMEM] * 2,
        compiler_params=params(8),
        cost_estimate=SMALL,
        name="rotated",
    )(keep, got, cosine, sine)


def gather_visible(mine, slabs, halves, new, keys, values, chunk):
    height = keys.shape[0]
    values[:, HD:] = jnp.ones((height, HD), BF16)
    n = jnp.int32(0)
    lane = lax.broadcasted_iota(jnp.int32, (16, HD), 1)
    for load in halves:
        codes = load[ROWS:, :HD].astype(F32)
        codes = jnp.where(lane == 0, 2.0, 1.0) * codes
        place = jnp.max(codes + pltpu.roll(codes, HD - 1, 1)).astype(jnp.int32)
        seen = place < mine

        @pl.when(seen)
        def _(load=load, n=n):
            at = pl.ds(pl.multiple_of(n * NEW, NEW), ROWS)
            keys[at, :] = load[:ROWS, :HD]
            values[at, :HD] = load[:ROWS, HD:]

        n = n + jnp.where(seen, ROWS // NEW, 0)
    if new is not None:
        for z in range(8):
            seen = slabs[z] < mine

            @pl.when(seen)
            def _(z=z, n=n):
                at = pl.ds(pl.multiple_of(n * NEW, NEW), NEW)
                keys[at, :] = new[z, :, :HD]
                values[at, :HD] = new[z, :, HD:]

            n = n + jnp.where(seen, 1, 0)
    per = chunk // NEW
    chunks = (n + per - 1) // per

    def pad(t, carry):
        at = pl.ds(pl.multiple_of(t * NEW, NEW), NEW)
        keys[at, :] = keys[:NEW, :]
        values[at, :] = jnp.zeros((NEW, PAIR), BF16)
        return carry

    lax.fori_loop(n, chunks * per, pad, 0)
    return chunks


def attend(q, peak_ref, chunks, keys, values, scores, chunk, acc_at, before):
    def peaks(i, carry):
        at = pl.ds(pl.multiple_of(i * chunk, chunk), chunk)
        s = lax.dot_general(q, keys[at, :], CONTRACT, preferred_element_type=F32)
        scores[i] = s
        best = peak_ref[...]
        for t in range(chunk // HD):
            best = jnp.maximum(best, s[:, t * HD : (t + 1) * HD])
        peak_ref[...] = best
        return carry

    lax.fori_loop(0, chunks, peaks, 0)
    peak = jnp.max(peak_ref[...], axis=1, keepdims=True)
    acc_at[...] = before(peak)

    def weigh(i, carry):
        at = pl.ds(pl.multiple_of(i * chunk, chunk), chunk)
        p = jnp.exp2((scores[i] - peak) * EXPONENT).astype(BF16)
        acc_at[...] += jnp.dot(p, values[at, :], preferred_element_type=F32)
        return carry

    lax.fori_loop(0, chunks, weigh, 0)
    return peak


def halves_of(buffers):
    halves = []
    for ref in buffers:
        for b in range(ref.shape[0] // HALF):
            halves.append(ref.at[b * HALF : (b + 1) * HALF, :])
    return halves


def near_kernel(slabs, near, far, notes, *refs, chunk, count):
    sources, (q_out, acc_out, peak_out) = refs[:count], refs[count : count + 3]
    refs = refs[count + 3 :]
    near_in, far_in, own, *loads = refs[: 3 + count]
    q_all, acc_all, peak_all, keys, values, scores, peak_ref, acc, sems = refs[3 + count :]
    pairs = [(sources[0].at[: 2 * HALF, :], loads[0])] + list(zip(sources[1:], loads[1:]))
    pairs += [(notes.at[0], own), (near, near_in), (far, far_in)]
    copies = fetch(pairs, sems.at[: count + 3])
    mine = slabs[lax.axis_index("key")]
    core = lax.axis_index("hid_1")
    x = lax.axis_index("hid_0")
    for copy in copies[:count]:
        copy.wait()
    chunks = gather_visible(mine, None, halves_of(loads), None, keys, values, chunk)
    for copy in copies[count:]:
        copy.wait()
    for j in range(4):
        half = x if j < 2 else 1 - x
        parity = core if j % 2 == 0 else 1 - core
        cols = pl.ds(pl.multiple_of(parity * PAIR, PAIR), PAIR)
        rows = [slice((2 * j + t) * ROWS, (2 * j + t + 1) * ROWS) for t in range(2)]

        @pl.when(half == core)
        def _(cols=cols, rows=rows):
            both = near_in[:, cols]
            q_all[rows[0], :] = both[:, :HD]
            q_all[rows[1], :] = both[:, HD:]

        @pl.when(half != core)
        def _(cols=cols, rows=rows):
            both = far_in[:, cols]
            q_all[rows[0], :] = both[:, :HD]
            q_all[rows[1], :] = both[:, HD:]

    out = fetch([(q_all, q_out)], sems.at[count + 3 : count + 4])
    zeros = jnp.zeros((NEW, HD), BF16)
    own_keys = jnp.concatenate([own[:, :HD], zeros], axis=0)
    own_values = jnp.concatenate([own[:, HD:], zeros], axis=0)
    own_values = jnp.concatenate([own_values, jnp.ones((HD, HD), BF16)], axis=1)
    row = lax.broadcasted_iota(jnp.int32, (TALL, HD), 0) % ROWS
    lane = lax.broadcasted_iota(jnp.int32, (TALL, HD), 1)
    visible = jnp.logical_and(lane < NEW, lane + new_offset() <= row)
    for step in range(8 * ROWS // TALL):
        at = pl.ds(step * TALL, TALL)
        q = q_all[at, :]
        s = lax.dot_general(q, own_keys, CONTRACT, preferred_element_type=F32)
        s = jnp.where(visible, s, NEGATIVE)
        peak_ref[...] = s

        def before(peak, s=s):
            p = jnp.where(visible, jnp.exp2((s - peak) * EXPONENT), 0.0)
            return jnp.dot(p.astype(BF16), own_values, preferred_element_type=F32)

        peak = attend(
            q, peak_ref, chunks, keys, values, scores, chunk, acc, before
        )
        acc_all[at, :] = acc[:, :HD]
        peak_all[at, :] = jnp.where(lane < HD // 2, peak, acc[:, HD:])
        first_sem = count + 4 + 2 * step
        out += fetch(
            [
                (acc_all.at[at, :], acc_out.at[at, :]),
                (peak_all.at[at, :], peak_out.at[at, :]),
            ],
            sems.at[first_sem : first_sem + 2],
        )
    for copy in out:
        copy.wait()


def attend_near(slabs, near, far, notes, loads):
    count, chunk = len(loads), 1280
    shapes = [(2 * HALF, PAIR)] + [a.shape for a in loads[1:]]
    height = sum(shape[0] // HALF * ROWS for shape in shapes)
    state = [((8 * ROWS, HD), BF16), ((8 * ROWS, HD), F32), ((8 * ROWS, HD), F32)]
    return pl.pallas_call(
        functools.partial(near_kernel, chunk=chunk, count=count),
        out_shape=[shaped(*s) for s in state],
        in_specs=[SMEM] + [HBM] * (3 + count),
        out_specs=[HBM] * 3,
        scratch_shapes=[
            pltpu.VMEM((ROWS, 4 * HD), BF16),
            pltpu.VMEM((ROWS, 4 * HD), BF16),
            pltpu.VMEM((NEW, PAIR), BF16),
            *[pltpu.VMEM(shape, BF16) for shape in shapes],
            *[pltpu.VMEM(*s) for s in state],
            pltpu.VMEM((height, HD), BF16),
            pltpu.VMEM((height, PAIR), BF16),
            pltpu.VMEM((height // chunk, TALL, chunk), F32),
            pltpu.VMEM((TALL, HD), F32),
            pltpu.VMEM((TALL, PAIR), F32),
            pltpu.SemaphoreType.DMA((count + 4 + 2 * (8 * ROWS // TALL),)),
        ],
        compiler_params=params(),
        cost_estimate=SMALL,
        name="near",
    )(slabs, near, far, notes, *loads)


def far_kernel(slabs, *refs, chunk, count, start, tall):
    sources, out = refs[: 4 + count], refs[4 + count]
    refs = refs[5 + count :]
    buffers = refs[: 4 + count]
    queries, acc_in, peak_in, new, *loads = buffers
    keys, values, scores, peak_ref, acc, sems = refs[4 + count :]
    sources = [ref.at[start : start + tall, :] for ref in sources[:3]] + list(sources[3:])
    copies = fetch(list(zip(sources, buffers))[::-1], sems)
    mine = slabs[lax.axis_index("key")]
    for copy in copies[: count + 1]:
        copy.wait()
    chunks = gather_visible(mine, slabs, halves_of(loads), new, keys, values, chunk)
    for copy in copies[count + 1 :]:
        copy.wait()
    peak_ref[...] = jnp.broadcast_to(peak_in[:, :1], (tall, HD))

    def before(peak):
        factor = jnp.exp2((peak_in[:, :1] - peak) * EXPONENT)
        total = jnp.broadcast_to(peak_in[:, HD // 2 : HD // 2 + 1], (tall, HD))
        return jnp.concatenate([acc_in[...], total], axis=1) * factor

    peak = attend(
        queries[...], peak_ref, chunks, keys, values, scores, chunk, acc, before
    )
    total = acc[:, HD:]
    heads = (acc[:, :HD] / jnp.where(total > 0.0, total, 1.0)).astype(BF16)
    lane = lax.broadcasted_iota(jnp.int32, (ROWS, HD), 1)
    totals = jnp.zeros((ROWS, HD), F32)
    peaks = jnp.zeros((ROWS, HD), F32)
    for h in range(tall // ROWS):
        rows = slice(h * ROWS, (h + 1) * ROWS)
        totals = jnp.where(lane == h, total[rows], totals)
        peaks = jnp.where(lane == h, peak[rows], peaks)
    some = totals > 0.0
    level = peaks * EXPONENT + jnp.log2(jnp.where(some, totals, 1.0))
    level = jnp.transpose(jnp.where(some, level, NEGATIVE))
    where = lax.broadcasted_iota(jnp.int32, (16, ROWS), 0)
    if start > 0:
        out[hid_index()] = jnp.zeros((MSG, PAIR), BF16)
    for t in range(tall // (2 * ROWS)):
        slot = jnp.bitwise_xor(hid_index(), start // (2 * ROWS) + t) if start > 0 else 0
        table = jnp.zeros((16, ROWS), F32)
        for half in range(2):
            h = 2 * t + half
            cols = slice(half * HD, (half + 1) * HD)
            out[slot, :ROWS, cols] = heads[h * ROWS : (h + 1) * ROWS]
            rest = level[h : h + 1, :]
            for k in range(3):
                coded = rest.astype(BF16).astype(F32)
                table = jnp.where(where == 3 * half + k, coded, table)
                rest = rest - coded
        out[slot, ROWS:, :] = table.astype(BF16)


def attend_far(start, tall, slabs, queries, acc, peak, new, loads):
    operands = [queries, acc, peak, new, *loads]
    count, chunk = len(loads), 1024
    height = sum(a.shape[0] // HALF * ROWS for a in loads) + 8 * NEW
    height = -(-height // chunk) * chunk
    shapes = [(tall, HD)] * 3 + [a.shape for a in operands[3:]]
    return pl.pallas_call(
        functools.partial(far_kernel, chunk=chunk, count=count, start=start, tall=tall),
        out_shape=shaped((4 if start > 0 else 1, MSG, PAIR), BF16),
        in_specs=[SMEM] + [HBM] * len(operands),
        out_specs=VMEM,
        scratch_shapes=[
            *[pltpu.VMEM(shape, a.dtype) for shape, a in zip(shapes, operands)],
            pltpu.VMEM((height, HD), BF16),
            pltpu.VMEM((height, PAIR), BF16),
            pltpu.VMEM((height // chunk, tall, chunk), F32),
            pltpu.VMEM((tall, HD), F32),
            pltpu.VMEM((tall, PAIR), F32),
            pltpu.SemaphoreType.DMA((len(operands),)),
        ],
        compiler_params=params(),
        cost_estimate=MEDIUM,
        name="far%d" % start,
    )(slabs, *operands)


def merge_kernel(own, got, out):
    quarter = hid_index()
    parts = [own.at[0]] + [got.at[jnp.bitwise_xor(quarter, j)] for j in range(1, 4)]
    levels = []
    for ref in parts:
        t = ref[ROWS:, :].astype(F32)
        levels.append([t[0:1] + t[1:2] + t[2:3], t[3:4] + t[4:5] + t[5:6]])
    rows = []
    for half in range(2):
        top = functools.reduce(jnp.maximum, [lv[half] for lv in levels])
        w = [jnp.exp2(lv[half] - top) for lv in levels]
        total = w[0] + w[1] + w[2] + w[3]
        rows.extend([x / total for x in w])
    table = jnp.concatenate(rows, axis=0)
    table = jnp.transpose(jnp.concatenate([table, jnp.zeros((HD - 8, ROWS), F32)], axis=0))
    for half in range(2):
        cols = slice(half * HD, (half + 1) * HD)
        so_far = None
        for t, ref in enumerate(parts):
            w = table[:, half * 4 + t : half * 4 + t + 1]
            term = ref[:ROWS, cols].astype(F32) * w
            so_far = term if so_far is None else so_far + term
        out[:, cols] = so_far.astype(BF16)


def merge(own, got):
    return pl.pallas_call(
        merge_kernel,
        out_shape=shaped((ROWS, PAIR), BF16),
        in_specs=[VMEM] * 2,
        out_specs=VMEM,
        compiler_params=params(8),
        cost_estimate=SMALL,
        name="merge",
    )(own, got)


def project_kernel(*refs):
    heads, weights, send, keep = refs[:4], refs[4:8], refs[8], refs[9]
    core = lax.axis_index("hid_1")
    h = jnp.concatenate([ref[...] for ref in heads], axis=1)
    for out, side in ((send, 1 - core), (keep, core)):
        for t in range(4):
            cols = pl.ds(pl.multiple_of(t * 512 + side * ROWS, ROWS), ROWS)
            w = jnp.concatenate([ref[:, cols] for ref in weights], axis=0)
            total = jnp.dot(h, w, preferred_element_type=F32)
            out[:, t * ROWS : (t + 1) * ROWS] = total.astype(out.dtype)


def project(heads, weights):
    width = weights[0].shape[1]
    return pl.pallas_call(
        project_kernel,
        out_shape=[shaped((ROWS, width // 2), BF16), shaped((ROWS, width // 2), F32)],
        in_specs=[VMEM] * 8,
        out_specs=[VMEM] * 2,
        compiler_params=params(16),
        cost_estimate=SMALL,
        name="project",
    )(*heads, *weights)


def split_kernel(keep, got, own, *sends):
    spot = 2 * lax.axis_index("head_0") + lax.axis_index("hid_0")
    for by in range(4):
        cols = pl.ds(pl.multiple_of(lax.rem(spot + by, 4) * ROWS, ROWS), ROWS)
        total = keep[:, cols] + got[:, cols].astype(F32)
        if by == 0:
            own[...] = total
        else:
            sends[by - 1][...] = total.astype(BF16)


def split(keep, got):
    return pl.pallas_call(
        split_kernel,
        out_shape=[shaped((ROWS, ROWS), F32)] + [shaped((ROWS, ROWS), BF16)] * 3,
        in_specs=[VMEM] * 2,
        out_specs=[VMEM] * 4,
        compiler_params=params(8),
        cost_estimate=SMALL,
        name="split",
    )(keep, got)


def body(
    tokens,
    query_weight,
    key_weight,
    value_weight,
    output_weight,
    key_cache,
    value_cache,
    cache_places,
    slab_places,
):
    key_index = lax.axis_index("key")

    load = pack(cache_places, key_cache.reshape(-1, HD), value_cache.reshape(-1, HD))

    def away(array, by):
        pairs = []
        for k in range(8):
            pairs.append((2 * k, 2 * ((k + by) % 8)))
            pairs.append((2 * k + 1, 2 * ((k - by) % 8) + 1))
        return lax.ppermute(array, ("key", "hid_1"), pairs)

    one = away(load, 1)

    pieces = columns(output_weight)

    send, keep = first(tokens, query_weight, key_weight, value_weight)
    one, keep = lax.optimization_barrier((one, keep))
    two = away(one, 1)
    send, keep = second(keep, swap(send, "hid_1"))
    got = swap(send, "hid_0")
    keep, pieces = lax.optimization_barrier((keep, pieces))
    weights = [pieces[3]]
    for piece, by in zip(pieces, (2, 1, 3)):
        weights.append(lax.ppermute(piece, "head_1", shift(4, by)))

    middle = HD // 2
    index = np.arange(HD) % middle
    frequency = jnp.exp(jnp.asarray(index, F32) * (-2.0 * math.log(THETA) / HD))
    sign = np.where(np.arange(HD) < middle, -1.0, 1.0).astype(np.float32)
    spots = slab_places[key_index] * ROWS + jnp.arange(ROWS, dtype=jnp.int32)
    angles = spots.astype(F32)[:, None] * frequency[None, :]
    cosine, sine = jnp.cos(angles), jnp.sin(angles) * sign[None, :]
    two, cosine, sine = lax.optimization_barrier((two, cosine, sine))
    three = away(two, 1)
    queries, notes = rotated(keep, got, cosine, sine)
    far = swap(queries, "hid_1")
    far, onward = lax.optimization_barrier((far, two[: 2 * HALF]))
    four = away(onward, 2)

    new = lax.all_to_all(notes, "key", split_axis=0, concat_axis=0, tiled=True)

    state = attend_near(slab_places, queries, far, notes, [load, one, two])
    late = attend_far(2 * ROWS, 6 * ROWS, slab_places, *state, new, [three, four])
    got = lax.all_to_all(late, HID, split_axis=0, concat_axis=0, tiled=True)
    state, late = lax.optimization_barrier((state, late))
    own = attend_far(0, 2 * ROWS, slab_places, *state, new, [three, four])
    got, weights = lax.optimization_barrier((got, weights))
    merged = merge(own, got)

    heads = [merged] + [lax.ppermute(merged, "head_1", shift(4, by)) for by in (2, 1, 3)]
    send, keep = project(heads, weights)
    own, *blocks = split(keep, swap(send, "hid_1"))
    out = own
    for by in (2, 1, 3):
        out = out + lax.ppermute(blocks[by - 1], ALONG_X, shift(4, by)).astype(F32)
    return out.astype(BF16)


def solution(mesh):
    finer = Mesh(
        mesh.devices.reshape(2, 4, mesh.shape["key"], 2, 2),
        ("head_0", "head_1", "key", "hid_0", "hid_1"),
    )
    return jax.shard_map(
        body,
        mesh=finer,
        in_specs=(
            P("key", HID),
            P(HID, HEAD),
            P(HID, HEAD),
            P(HID, HEAD),
            P(HEAD_HID, None),
            P("key", HEAD, None),
            P("key", HEAD, None),
            P("key"),
            P(),
        ),
        out_specs=P("key", HEAD_HID),
        check_vma=False,
    )
```

```python
import functools
import math

import jax
import jax.numpy as jnp
import numpy as np
from jax import lax
from jax.experimental import pallas as pl
from jax.experimental.pallas import tpu as pltpu
from jax.sharding import Mesh
from jax.sharding import PartitionSpec as P

HID = ("hid_0", "hid_1")
HEAD = ("head_0", "head_1")
HEAD_HID = ("head_0", "head_1", "hid_0", "hid_1")
ALONG_X = ("head_0", "hid_0")

THETA = 500000.0
NEGATIVE = -1e30
BF16 = jnp.bfloat16
F32 = jnp.float32

ROWS = 256
HD = 128
PAIR = 2 * HD
NEW = 64
QUARTER = 512
HALF = ROWS + 16
LOAD = 4 * HALF
MSG = ROWS + 16
TALL = 2048
EXPONENT = math.log2(math.e) / math.sqrt(HD)
CONTRACT = (((1,), (1,)), ((), ()))

VMEM = pl.BlockSpec(memory_space=pltpu.VMEM)
SMEM = pl.BlockSpec(memory_space=pltpu.SMEM)
HBM = pl.BlockSpec(memory_space=pltpu.HBM)


def shaped(shape, dtype):
    return jax.ShapeDtypeStruct(shape, dtype)


def params(mib=60):
    return pltpu.CompilerParams(vmem_limit_bytes=mib * 2**20)


SMALL = pl.CostEstimate(flops=1, bytes_accessed=1, transcendentals=0)
MEDIUM = pl.CostEstimate(flops=2**27, bytes_accessed=2**18, transcendentals=2**10)


def shift(n, by):
    return [(i, (i + by) % n) for i in range(n)]


def swap(array, axis):
    return lax.ppermute(array, axis, shift(2, 1))


def hid_index():
    return 2 * lax.axis_index("hid_0") + lax.axis_index("hid_1")


def fetch(pairs, sems):
    copies = [
        pltpu.make_async_copy(source, target, sems.at[i])
        for i, (source, target) in enumerate(pairs)
    ]
    for copy in copies:
        copy.start()
    return copies


def pack_kernel(places, slabs, keys, values, out, spots, load, sems):
    core = lax.axis_index("hid_1")
    lane = lax.broadcasted_iota(jnp.int32, (16, PAIR), 1)
    pairs = []
    for i in range(4):
        block = 4 * lax.axis_index("hid_0") + lax.rem(2 * core + i, 4)
        rows = pl.ds(pl.multiple_of(block * ROWS, ROWS), ROWS)
        to = slice(i * HALF, i * HALF + ROWS)
        pairs.append((keys.at[rows, :], load.at[to, :HD]))
        pairs.append((values.at[rows, :], load.at[to, HD:]))
        place = places[block]
        table = jnp.where(lane == 0, place >> 1, jnp.where(lane == 1, place & 1, 0))
        load[i * HALF + ROWS : (i + 1) * HALF, :] = table.astype(F32).astype(BF16)
    copies = fetch(pairs, sems.at[:8])
    leaving = []
    for i in range(4):
        copies[2 * i].wait()
        copies[2 * i + 1].wait()
        to = slice(i * HALF, (i + 1) * HALF)
        leaving += fetch([(load.at[to, :], out.at[to, :])], sems.at[8 + i : 9 + i])
    row = lax.broadcasted_iota(jnp.int32, (ROWS, HD), 0)
    spots[...] = (slabs[lax.axis_index("key")] * ROWS + row).astype(F32)
    for copy in leaving:
        copy.wait()


def pack(places, slabs, keys, values):
    return pl.pallas_call(
        pack_kernel,
        out_shape=[shaped((LOAD, PAIR), BF16), shaped((ROWS, HD), F32)],
        in_specs=[SMEM, SMEM, HBM, HBM],
        out_specs=[HBM, VMEM],
        scratch_shapes=[pltpu.VMEM((LOAD, PAIR), BF16), pltpu.SemaphoreType.DMA((12,))],
        compiler_params=params(),
        cost_estimate=SMALL,
        name="pack",
    )(places, slabs, keys, values)


def columns_kernel(weight, *refs):
    outs, pieces, sems, out_sems = refs[:4], refs[4], refs[5], refs[6]
    y = lax.axis_index("head_1")
    pairs = []
    for t, by in enumerate((2, 1, 3, 0)):
        at = lax.rem(y + by, 4) * 1024
        for hi in range(2):
            source = pl.ds(pl.multiple_of(hi * 4096 + at, 1024), 1024)
            pairs.append((weight.at[:, source], pieces.at[t, :, hi * 1024 : (hi + 1) * 1024]))
    copies = fetch(pairs, sems)
    leaving = []
    for t in range(4):
        copies[2 * t].wait()
        copies[2 * t + 1].wait()
        leaving += fetch([(pieces.at[t], outs[t])], out_sems.at[t : t + 1])
    for copy in leaving:
        copy.wait()


def columns(weight):
    return pl.pallas_call(
        columns_kernel,
        out_shape=[shaped((ROWS, 2048), BF16)] * 4,
        in_specs=[HBM],
        out_specs=[HBM] * 4,
        scratch_shapes=[
            pltpu.VMEM((4, ROWS, 2048), BF16),
            pltpu.SemaphoreType.DMA((8,)),
            pltpu.SemaphoreType.DMA((4,)),
        ],
        compiler_params=params(),
        cost_estimate=SMALL,
        name="columns",
    )(weight)


def first_kernel(tokens, query, key, value, send, keep, tok, wide, kv, sent, fresh, sems):
    core = lax.axis_index("hid_1")
    deep = tok.shape[2]
    copies = []
    for t in range(4):
        part = slice(t * deep, (t + 1) * deep)
        pairs = [
            (tokens.at[:, part], tok.at[t]),
            (query.at[part, :], wide.at[t]),
            (key.at[part, :], kv.at[t, :, :HD]),
            (value.at[part, :], kv.at[t, :, HD:]),
        ]
        copies.append(fetch(pairs, sems.at[4 * t : 4 * t + 4]))
    far_cols = pl.ds(pl.multiple_of((1 - core) * 512, 512), 512)
    near_cols = pl.ds(pl.multiple_of(core * 512, 512), 512)
    for t in range(4):
        for copy in copies[t]:
            copy.wait()
        a = tok[t]
        far = jnp.dot(a, wide[t, :, far_cols], preferred_element_type=F32)
        near = jnp.dot(a, wide[t, :, near_cols], preferred_element_type=F32)
        new = jnp.dot(a, kv[t], preferred_element_type=F32)
        if t == 0:
            sent[...] = far
            keep[:ROWS, :] = near
            fresh[...] = new
        else:
            keep[:ROWS, :] += near
            fresh[...] += new
            if t == 3:
                send[:ROWS, :] = (sent[...] + far).astype(BF16)
            else:
                sent[...] += far
    for t in range(2):
        cols = slice(t * PAIR, (t + 1) * PAIR)
        far_rows = pl.ds(pl.multiple_of((1 - core) * 128 + t * NEW, NEW), NEW)
        near_rows = pl.ds(pl.multiple_of(core * 128 + t * NEW, NEW), NEW)
        send[ROWS:, cols] = fresh[far_rows, :].astype(BF16)
        keep[ROWS:, cols] = fresh[near_rows, :]


def first(tokens, query, key, value):
    deep = tokens.shape[1] // 4
    return pl.pallas_call(
        first_kernel,
        out_shape=[shaped((320, 512), BF16), shaped((320, 512), F32)],
        in_specs=[HBM] * 4,
        out_specs=[VMEM] * 2,
        scratch_shapes=[
            pltpu.VMEM((4, ROWS, deep), BF16),
            pltpu.VMEM((4, deep, query.shape[1]), BF16),
            pltpu.VMEM((4, deep, PAIR), BF16),
            pltpu.VMEM((ROWS, 512), F32),
            pltpu.VMEM((ROWS, PAIR), F32),
            pltpu.SemaphoreType.DMA((16,)),
        ],
        compiler_params=params(),
        cost_estimate=SMALL,
        name="first",
    )(tokens, query, key, value)


def second_kernel(keep, got, send, onward):
    x = lax.axis_index("hid_0")
    q = keep[:ROWS, :] + got[:ROWS, :].astype(F32)
    send[:ROWS, :] = q.astype(BF16)
    onward[:ROWS, :] = q
    low = keep[ROWS:, :] + got[ROWS:, :].astype(F32)
    sides = [low[:, :PAIR], low[:, PAIR:]]
    sides = [jnp.concatenate([s[:32], s[32:]], axis=1) for s in sides]
    mine = jnp.where(x == 0, sides[0], sides[1])
    other = jnp.where(x == 0, sides[1], sides[0])
    send[ROWS:, :] = other.astype(BF16)
    onward[ROWS:, :] = mine


def second(keep, got):
    return pl.pallas_call(
        second_kernel,
        out_shape=[shaped((288, 512), BF16), shaped((288, 512), F32)],
        in_specs=[VMEM] * 2,
        out_specs=[VMEM] * 2,
        compiler_params=params(8),
        cost_estimate=SMALL,
        name="second",
    )(keep, got)


def new_offset():
    return lax.axis_index("hid_1") * 128 + lax.axis_index("hid_0") * NEW


def rotate_kernel(keep, got, cosine, sine, queries, notes):
    for h in range(4):
        cols = slice(h * HD, (h + 1) * HD)
        u = keep[:ROWS, cols] + got[:ROWS, cols].astype(F32)
        turned = u * cosine[...] + pltpu.roll(u, HD // 2, 1) * sine[...]
        queries[:, cols] = turned.astype(BF16)
    low = keep[ROWS:, :] + got[ROWS:, :].astype(F32)
    low = jnp.concatenate([low[:, :PAIR], low[:, PAIR:]], axis=0)
    rows = pl.ds(pl.multiple_of(new_offset(), NEW), NEW)
    u = low[:, :HD]
    turned = u * cosine[rows, :] + pltpu.roll(u, HD // 2, 1) * sine[rows, :]
    for z in range(8):
        notes[z, :, :HD] = turned.astype(BF16)
        notes[z, :, HD:] = low[:, HD:].astype(BF16)


def rotated(keep, got, cosine, sine):
    return pl.pallas_call(
        rotate_kernel,
        out_shape=[shaped((ROWS, 512), BF16), shaped((8, NEW, PAIR), BF16)],
        in_specs=[VMEM] * 4,
        out_specs=[VMEM] * 2,
        compiler_params=params(8),
        cost_estimate=SMALL,
        name="rotated",
    )(keep, got, cosine, sine)


def gather_visible(mine, slabs, halves, new, keys, values, chunk):
    height = keys.shape[0]
    values[:, HD:] = jnp.ones((height, HD), BF16)
    n = jnp.int32(0)
    lane = lax.broadcasted_iota(jnp.int32, (16, HD), 1)
    marks = jnp.zeros((16, HD), jnp.int32)
    for i, load in enumerate(halves):
        codes = load[ROWS:, :HD].astype(F32)
        codes = jnp.where(lane == 0, 2.0, 1.0) * codes
        place = (codes + pltpu.roll(codes, HD - 1, 1)).astype(jnp.int32)
        marks = marks + jnp.where(place < mine, 1 << i, 0)
    mask = jnp.max(jnp.where(lane == 0, marks, 0))
    bit = 0
    for load in halves:
        seen = ((mask >> bit) & 1) == 1
        bit += 1

        @pl.when(seen)
        def _(load=load, n=n):
            at = pl.ds(pl.multiple_of(n * NEW, NEW), ROWS)
            keys[at, :] = load[:ROWS, :HD]
            values[at, :HD] = load[:ROWS, HD:]

        n = n + jnp.where(seen, ROWS // NEW, 0)
    if new is not None:
        for z in range(8):
            seen = slabs[z] < mine

            @pl.when(seen)
            def _(z=z, n=n):
                at = pl.ds(pl.multiple_of(n * NEW, NEW), NEW)
                keys[at, :] = new[z, :, :HD]
                values[at, :HD] = new[z, :, HD:]

            n = n + jnp.where(seen, 1, 0)
    per = chunk // NEW
    chunks = (n + per - 1) // per

    def pad(t, carry):
        at = pl.ds(pl.multiple_of(t * NEW, NEW), NEW)
        keys[at, :] = keys[:NEW, :]
        values[at, :] = jnp.zeros((NEW, PAIR), BF16)
        return carry

    lax.fori_loop(n, chunks * per, pad, 0)
    return chunks


def attend(q, peak_ref, chunks, keys, values, scores, chunk, acc_at, before):
    def peaks(i, carry):
        at = pl.ds(pl.multiple_of(i * chunk, chunk), chunk)
        s = lax.dot_general(q, keys[at, :], CONTRACT, preferred_element_type=F32)
        scores[i] = s
        best = peak_ref[...]
        for t in range(chunk // HD):
            best = jnp.maximum(best, s[:, t * HD : (t + 1) * HD])
        peak_ref[...] = best
        return carry

    lax.fori_loop(0, chunks, peaks, 0)
    peak = jnp.max(peak_ref[...], axis=1, keepdims=True)
    acc_at[...] = before(peak)

    def weigh(i, carry):
        at = pl.ds(pl.multiple_of(i * chunk, chunk), chunk)
        p = jnp.exp2((scores[i] - peak) * EXPONENT).astype(BF16)
        acc_at[...] += jnp.dot(p, values[at, :], preferred_element_type=F32)
        return carry

    lax.fori_loop(0, chunks, weigh, 0)
    return peak


def halves_of(buffers):
    halves = []
    for ref in buffers:
        for b in range(ref.shape[0] // HALF):
            halves.append(ref.at[b * HALF : (b + 1) * HALF, :])
    return halves


def near_kernel(slabs, near, far, notes, *refs, chunk, count):
    sources, (q_out, acc_out, peak_out) = refs[:count], refs[count : count + 3]
    refs = refs[count + 3 :]
    near_in, far_in, own, *loads = refs[: 3 + count]
    q_all, acc_all, peak_all, keys, values, scores, peak_ref, acc, sems = refs[3 + count :]
    pairs = [(sources[0].at[: 2 * HALF, :], loads[0])] + list(zip(sources[1:], loads[1:]))
    pairs += [(notes.at[0], own), (near, near_in), (far, far_in)]
    copies = fetch(pairs, sems.at[: count + 3])
    mine = slabs[lax.axis_index("key")]
    core = lax.axis_index("hid_1")
    x = lax.axis_index("hid_0")
    for copy in copies[:count]:
        copy.wait()
    chunks = gather_visible(mine, None, halves_of(loads), None, keys, values, chunk)
    for copy in copies[count:]:
        copy.wait()
    for j in range(4):
        half = x if j < 2 else 1 - x
        parity = core if j % 2 == 0 else 1 - core
        cols = pl.ds(pl.multiple_of(parity * PAIR, PAIR), PAIR)
        rows = [slice((2 * j + t) * ROWS, (2 * j + t + 1) * ROWS) for t in range(2)]

        @pl.when(half == core)
        def _(cols=cols, rows=rows):
            both = near_in[:, cols]
            q_all[rows[0], :] = both[:, :HD]
            q_all[rows[1], :] = both[:, HD:]

        @pl.when(half != core)
        def _(cols=cols, rows=rows):
            both = far_in[:, cols]
            q_all[rows[0], :] = both[:, :HD]
            q_all[rows[1], :] = both[:, HD:]

    out = fetch([(q_all, q_out)], sems.at[count + 3 : count + 4])
    zeros = jnp.zeros((NEW, HD), BF16)
    own_keys = jnp.concatenate([own[:, :HD], zeros], axis=0)
    own_values = jnp.concatenate([own[:, HD:], zeros], axis=0)
    own_values = jnp.concatenate([own_values, jnp.ones((HD, HD), BF16)], axis=1)
    row = lax.broadcasted_iota(jnp.int32, (TALL, HD), 0) % ROWS
    lane = lax.broadcasted_iota(jnp.int32, (TALL, HD), 1)
    visible = jnp.logical_and(lane < NEW, lane + new_offset() <= row)
    for step in range(8 * ROWS // TALL):
        at = pl.ds(step * TALL, TALL)
        q = q_all[at, :]
        s = lax.dot_general(q, own_keys, CONTRACT, preferred_element_type=F32)
        s = jnp.where(visible, s, NEGATIVE)
        peak_ref[...] = s

        def before(peak, s=s):
            p = jnp.where(visible, jnp.exp2((s - peak) * EXPONENT), 0.0)
            return jnp.dot(p.astype(BF16), own_values, preferred_element_type=F32)

        peak = attend(
            q, peak_ref, chunks, keys, values, scores, chunk, acc, before
        )
        acc_all[at, :] = acc[:, :HD]
        peak_all[at, :] = jnp.where(lane < HD // 2, peak, acc[:, HD:])
        first_sem = count + 4 + 2 * step
        out += fetch(
            [
                (acc_all.at[at, :], acc_out.at[at, :]),
                (peak_all.at[at, :], peak_out.at[at, :]),
            ],
            sems.at[first_sem : first_sem + 2],
        )
    for copy in out:
        copy.wait()


def attend_near(slabs, near, far, notes, loads):
    count, chunk = len(loads), 1280
    shapes = [(2 * HALF, PAIR)] + [a.shape for a in loads[1:]]
    height = sum(shape[0] // HALF * ROWS for shape in shapes)
    state = [((8 * ROWS, HD), BF16), ((8 * ROWS, HD), F32), ((8 * ROWS, HD), F32)]
    return pl.pallas_call(
        functools.partial(near_kernel, chunk=chunk, count=count),
        out_shape=[shaped(*s) for s in state],
        in_specs=[SMEM] + [HBM] * (3 + count),
        out_specs=[HBM] * 3,
        scratch_shapes=[
            pltpu.VMEM((ROWS, 4 * HD), BF16),
            pltpu.VMEM((ROWS, 4 * HD), BF16),
            pltpu.VMEM((NEW, PAIR), BF16),
            *[pltpu.VMEM(shape, BF16) for shape in shapes],
            *[pltpu.VMEM(*s) for s in state],
            pltpu.VMEM((height, HD), BF16),
            pltpu.VMEM((height, PAIR), BF16),
            pltpu.VMEM((height // chunk, TALL, chunk), F32),
            pltpu.VMEM((TALL, HD), F32),
            pltpu.VMEM((TALL, PAIR), F32),
            pltpu.SemaphoreType.DMA((count + 4 + 2 * (8 * ROWS // TALL),)),
        ],
        compiler_params=params(),
        cost_estimate=SMALL,
        name="near",
    )(slabs, near, far, notes, *loads)


def far_kernel(slabs, *refs, chunk, count):
    sources, out = refs[: 4 + count], refs[4 + count]
    refs = refs[5 + count :]
    buffers = refs[: 4 + count]
    queries, acc_in, peak_in, new, *loads = buffers
    keys, values, scores, peak_ref, acc, sems = refs[4 + count :]
    tall = 8 * ROWS
    copies = fetch(list(zip(sources, buffers))[::-1], sems)
    mine = slabs[lax.axis_index("key")]
    for copy in copies[: count + 1]:
        copy.wait()
    chunks = gather_visible(mine, slabs, halves_of(loads), new, keys, values, chunk)
    for copy in copies[count + 1 :]:
        copy.wait()
    peak_ref[...] = jnp.broadcast_to(peak_in[:, :1], (tall, HD))

    def before(peak):
        factor = jnp.exp2((peak_in[:, :1] - peak) * EXPONENT)
        total = jnp.broadcast_to(peak_in[:, HD // 2 : HD // 2 + 1], (tall, HD))
        return jnp.concatenate([acc_in[...], total], axis=1) * factor

    peak = attend(
        queries[...], peak_ref, chunks, keys, values, scores, chunk, acc, before
    )
    total = acc[:, HD:]
    heads = (acc[:, :HD] / jnp.where(total > 0.0, total, 1.0)).astype(BF16)
    lane = lax.broadcasted_iota(jnp.int32, (ROWS, HD), 1)
    totals = jnp.zeros((ROWS, HD), F32)
    peaks = jnp.zeros((ROWS, HD), F32)
    for h in range(tall // ROWS):
        rows = slice(h * ROWS, (h + 1) * ROWS)
        totals = jnp.where(lane == h, total[rows], totals)
        peaks = jnp.where(lane == h, peak[rows], peaks)
    some = totals > 0.0
    level = peaks * EXPONENT + jnp.log2(jnp.where(some, totals, 1.0))
    level = jnp.transpose(jnp.where(some, level, NEGATIVE))
    where = lax.broadcasted_iota(jnp.int32, (16, ROWS), 0)
    for t in range(tall // (2 * ROWS)):
        slot = jnp.bitwise_xor(hid_index(), t)
        table = jnp.zeros((16, ROWS), F32)
        for half in range(2):
            h = 2 * t + half
            cols = slice(half * HD, (half + 1) * HD)
            out[slot, :ROWS, cols] = heads[h * ROWS : (h + 1) * ROWS]
            rest = level[h : h + 1, :]
            for k in range(3):
                coded = rest.astype(BF16).astype(F32)
                table = jnp.where(where == 3 * half + k, coded, table)
                rest = rest - coded
        out[slot, ROWS:, :] = table.astype(BF16)


def attend_far(slabs, queries, acc, peak, new, loads):
    operands = [queries, acc, peak, new, *loads]
    count, chunk = len(loads), 1024
    height = sum(a.shape[0] // HALF * ROWS for a in loads) + 8 * NEW
    height = -(-height // chunk) * chunk
    tall = 8 * ROWS
    return pl.pallas_call(
        functools.partial(far_kernel, chunk=chunk, count=count),
        out_shape=shaped((4, MSG, PAIR), BF16),
        in_specs=[SMEM] + [HBM] * len(operands),
        out_specs=VMEM,
        scratch_shapes=[
            *[pltpu.VMEM(a.shape, a.dtype) for a in operands],
            pltpu.VMEM((height, HD), BF16),
            pltpu.VMEM((height, PAIR), BF16),
            pltpu.VMEM((height // chunk, tall, chunk), F32),
            pltpu.VMEM((tall, HD), F32),
            pltpu.VMEM((tall, PAIR), F32),
            pltpu.SemaphoreType.DMA((len(operands),)),
        ],
        compiler_params=params(),
        cost_estimate=MEDIUM,
        name="far",
    )(slabs, *operands)


def merge_kernel(got, out):
    parts = [got.at[j] for j in range(4)]
    levels = []
    for ref in parts:
        t = ref[ROWS:, :].astype(F32)
        levels.append([t[0:1] + t[1:2] + t[2:3], t[3:4] + t[4:5] + t[5:6]])
    rows = []
    for half in range(2):
        top = functools.reduce(jnp.maximum, [lv[half] for lv in levels])
        w = [jnp.exp2(lv[half] - top) for lv in levels]
        total = w[0] + w[1] + w[2] + w[3]
        rows.extend([x / total for x in w])
    table = jnp.concatenate(rows, axis=0)
    table = jnp.transpose(jnp.concatenate([table, jnp.zeros((HD - 8, ROWS), F32)], axis=0))
    for half in range(2):
        cols = slice(half * HD, (half + 1) * HD)
        so_far = None
        for t, ref in enumerate(parts):
            w = table[:, half * 4 + t : half * 4 + t + 1]
            term = ref[:ROWS, cols].astype(F32) * w
            so_far = term if so_far is None else so_far + term
        out[:, cols] = so_far.astype(BF16)


def merge(got):
    return pl.pallas_call(
        merge_kernel,
        out_shape=shaped((ROWS, PAIR), BF16),
        in_specs=[VMEM],
        out_specs=VMEM,
        compiler_params=params(8),
        cost_estimate=SMALL,
        name="merge",
    )(got)


def project_kernel(*refs):
    heads, weights, send, keep = refs[:4], refs[4:8], refs[8], refs[9]
    core = lax.axis_index("hid_1")
    h = jnp.concatenate([ref[...] for ref in heads], axis=1)
    for out, side in ((send, 1 - core), (keep, core)):
        for t in range(4):
            cols = pl.ds(pl.multiple_of(t * 512 + side * ROWS, ROWS), ROWS)
            w = jnp.concatenate([ref[:, cols] for ref in weights], axis=0)
            total = jnp.dot(h, w, preferred_element_type=F32)
            out[:, t * ROWS : (t + 1) * ROWS] = total.astype(out.dtype)


def project(heads, weights):
    width = weights[0].shape[1]
    return pl.pallas_call(
        project_kernel,
        out_shape=[shaped((ROWS, width // 2), BF16), shaped((ROWS, width // 2), F32)],
        in_specs=[VMEM] * 8,
        out_specs=[VMEM] * 2,
        compiler_params=params(16),
        cost_estimate=SMALL,
        name="project",
    )(*heads, *weights)


def split_kernel(keep, got, own, *sends):
    spot = 2 * lax.axis_index("head_0") + lax.axis_index("hid_0")
    for by in range(4):
        cols = pl.ds(pl.multiple_of(lax.rem(spot + by, 4) * ROWS, ROWS), ROWS)
        total = keep[:, cols] + got[:, cols].astype(F32)
        if by == 0:
            own[...] = total
        else:
            sends[by - 1][...] = total.astype(BF16)


def split(keep, got):
    return pl.pallas_call(
        split_kernel,
        out_shape=[shaped((ROWS, ROWS), F32)] + [shaped((ROWS, ROWS), BF16)] * 3,
        in_specs=[VMEM] * 2,
        out_specs=[VMEM] * 4,
        compiler_params=params(8),
        cost_estimate=SMALL,
        name="split",
    )(keep, got)


def body(
    tokens,
    query_weight,
    key_weight,
    value_weight,
    output_weight,
    key_cache,
    value_cache,
    cache_places,
    slab_places,
):

    load, spots = pack(
        cache_places, slab_places, key_cache.reshape(-1, HD), value_cache.reshape(-1, HD)
    )

    def away(array, by):
        pairs = []
        for k in range(8):
            pairs.append((2 * k, 2 * ((k + by) % 8)))
            pairs.append((2 * k + 1, 2 * ((k - by) % 8) + 1))
        return lax.ppermute(array, ("key", "hid_1"), pairs)

    one = away(load, 1)

    pieces = columns(output_weight)

    send, keep = first(tokens, query_weight, key_weight, value_weight)
    one, keep, pieces = lax.optimization_barrier((one, keep, pieces))
    two = away(one, 1)
    send, keep = second(keep, swap(send, "hid_1"))
    got = swap(send, "hid_0")
    weights = [pieces[3]]
    for piece, by in zip(pieces, (2, 1, 3)):
        weights.append(lax.ppermute(piece, "head_1", shift(4, by)))

    middle = HD // 2
    index = np.arange(HD) % middle
    frequency = jnp.exp(jnp.asarray(index, F32) * (-2.0 * math.log(THETA) / HD))
    sign = np.where(np.arange(HD) < middle, -1.0, 1.0).astype(np.float32)
    angles = spots * frequency[None, :]
    cosine, sine = jnp.cos(angles), jnp.sin(angles) * sign[None, :]
    two, cosine, sine = lax.optimization_barrier((two, cosine, sine))
    three = away(two, 1)
    queries, notes = rotated(keep, got, cosine, sine)
    far = swap(queries, "hid_1")
    far, onward = lax.optimization_barrier((far, two[: 2 * HALF]))
    four = away(onward, 2)

    new = lax.all_to_all(notes, "key", split_axis=0, concat_axis=0, tiled=True)

    state = attend_near(slab_places, queries, far, notes, [load, one, two])
    parts = attend_far(slab_places, *state, new, [three, four])
    got = lax.all_to_all(parts, HID, split_axis=0, concat_axis=0, tiled=True)
    got, weights = lax.optimization_barrier((got, weights))
    merged = merge(got)

    heads = [merged] + [lax.ppermute(merged, "head_1", shift(4, by)) for by in (2, 1, 3)]
    send, keep = project(heads, weights)
    own, *blocks = split(keep, swap(send, "hid_1"))
    out = own
    for by in (2, 1, 3):
        out = out + lax.ppermute(blocks[by - 1], ALONG_X, shift(4, by)).astype(F32)
    return out.astype(BF16)


def solution(mesh):
    finer = Mesh(
        mesh.devices.reshape(2, 4, mesh.shape["key"], 2, 2),
        ("head_0", "head_1", "key", "hid_0", "hid_1"),
    )
    return jax.shard_map(
        body,
        mesh=finer,
        in_specs=(
            P("key", HID),
            P(HID, HEAD),
            P(HID, HEAD),
            P(HID, HEAD),
            P(HEAD_HID, None),
            P("key", HEAD, None),
            P("key", HEAD, None),
            P("key"),
            P(),
        ),
        out_specs=P("key", HEAD_HID),
        check_vma=False,
    )
```

```python
import functools
import math

import jax
import jax.numpy as jnp
import numpy as np
from jax import lax
from jax.experimental import pallas as pl
from jax.experimental.pallas import tpu as pltpu
from jax.sharding import Mesh
from jax.sharding import PartitionSpec as P

HID = ("hid_0", "hid_1")
HEAD = ("head_0", "head_1")
HEAD_HID = ("head_0", "head_1", "hid_0", "hid_1")
ALONG_X = ("head_0", "hid_0")

THETA = 500000.0
NEGATIVE = -1e30
BF16 = jnp.bfloat16
F32 = jnp.float32

ROWS = 256
HD = 128
PAIR = 2 * HD
NEW = 64
QUARTER = 512
HALF = ROWS + 16
LOAD = 4 * HALF
MSG = ROWS + 16
TALL = 2048
EXPONENT = math.log2(math.e) / math.sqrt(HD)
CONTRACT = (((1,), (1,)), ((), ()))

VMEM = pl.BlockSpec(memory_space=pltpu.VMEM)
SMEM = pl.BlockSpec(memory_space=pltpu.SMEM)
HBM = pl.BlockSpec(memory_space=pltpu.HBM)


def shaped(shape, dtype):
    return jax.ShapeDtypeStruct(shape, dtype)


def params(mib=60):
    return pltpu.CompilerParams(vmem_limit_bytes=mib * 2**20)


SMALL = pl.CostEstimate(flops=1, bytes_accessed=1, transcendentals=0)
MEDIUM = pl.CostEstimate(flops=2**27, bytes_accessed=2**18, transcendentals=2**10)


def shift(n, by):
    return [(i, (i + by) % n) for i in range(n)]


def swap(array, axis):
    return lax.ppermute(array, axis, shift(2, 1))


def hid_index():
    return 2 * lax.axis_index("hid_0") + lax.axis_index("hid_1")


def fetch(pairs, sems):
    copies = [
        pltpu.make_async_copy(source, target, sems.at[i])
        for i, (source, target) in enumerate(pairs)
    ]
    for copy in copies:
        copy.start()
    return copies


def pack_kernel(places, slabs, keys, values, out, spots, load, sems):
    core = lax.axis_index("hid_1")
    lane = lax.broadcasted_iota(jnp.int32, (16, PAIR), 1)
    pairs = []
    for i in range(4):
        block = 4 * lax.axis_index("hid_0") + lax.rem(2 * core + i, 4)
        rows = pl.ds(pl.multiple_of(block * ROWS, ROWS), ROWS)
        to = slice(i * HALF, i * HALF + ROWS)
        pairs.append((keys.at[rows, :], load.at[to, :HD]))
        pairs.append((values.at[rows, :], load.at[to, HD:]))
        place = places[block]
        table = jnp.where(lane == 0, place >> 1, jnp.where(lane == 1, place & 1, 0))
        load[i * HALF + ROWS : (i + 1) * HALF, :] = table.astype(F32).astype(BF16)
    copies = fetch(pairs, sems.at[:8])
    leaving = []
    for i in range(4):
        copies[2 * i].wait()
        copies[2 * i + 1].wait()
        to = slice(i * HALF, (i + 1) * HALF)
        leaving += fetch([(load.at[to, :], out.at[to, :])], sems.at[8 + i : 9 + i])
    row = lax.broadcasted_iota(jnp.int32, (ROWS, HD), 0)
    spots[...] = (slabs[lax.axis_index("key")] * ROWS + row).astype(F32)
    for copy in leaving:
        copy.wait()


def pack(places, slabs, keys, values):
    return pl.pallas_call(
        pack_kernel,
        out_shape=[shaped((LOAD, PAIR), BF16), shaped((ROWS, HD), F32)],
        in_specs=[SMEM, SMEM, HBM, HBM],
        out_specs=[HBM, VMEM],
        scratch_shapes=[pltpu.VMEM((LOAD, PAIR), BF16), pltpu.SemaphoreType.DMA((12,))],
        compiler_params=params(),
        cost_estimate=SMALL,
        name="pack",
    )(places, slabs, keys, values)


def columns_kernel(weight, *refs):
    outs, pieces, sems, out_sems = refs[:4], refs[4], refs[5], refs[6]
    y = lax.axis_index("head_1")
    pairs = []
    for t, by in enumerate((2, 1, 3, 0)):
        at = lax.rem(y + by, 4) * 1024
        for hi in range(2):
            source = pl.ds(pl.multiple_of(hi * 4096 + at, 1024), 1024)
            pairs.append((weight.at[:, source], pieces.at[t, :, hi * 1024 : (hi + 1) * 1024]))
    copies = fetch(pairs, sems)
    leaving = []
    for t in range(4):
        copies[2 * t].wait()
        copies[2 * t + 1].wait()
        leaving += fetch([(pieces.at[t], outs[t])], out_sems.at[t : t + 1])
    for copy in leaving:
        copy.wait()


def columns(weight):
    return pl.pallas_call(
        columns_kernel,
        out_shape=[shaped((ROWS, 2048), BF16)] * 4,
        in_specs=[HBM],
        out_specs=[HBM] * 4,
        scratch_shapes=[
            pltpu.VMEM((4, ROWS, 2048), BF16),
            pltpu.SemaphoreType.DMA((8,)),
            pltpu.SemaphoreType.DMA((4,)),
        ],
        compiler_params=params(),
        cost_estimate=SMALL,
        name="columns",
    )(weight)


def first_kernel(tokens, query, key, value, send, keep, tok, wide, kv, sent, fresh, sems):
    core = lax.axis_index("hid_1")
    deep = tok.shape[2]
    copies = []
    for t in range(4):
        part = slice(t * deep, (t + 1) * deep)
        pairs = [
            (tokens.at[:, part], tok.at[t]),
            (query.at[part, :], wide.at[t]),
            (key.at[part, :], kv.at[t, :, :HD]),
            (value.at[part, :], kv.at[t, :, HD:]),
        ]
        copies.append(fetch(pairs, sems.at[4 * t : 4 * t + 4]))
    far_cols = pl.ds(pl.multiple_of((1 - core) * 512, 512), 512)
    near_cols = pl.ds(pl.multiple_of(core * 512, 512), 512)
    for t in range(4):
        for copy in copies[t]:
            copy.wait()
        a = tok[t]
        far = jnp.dot(a, wide[t, :, far_cols], preferred_element_type=F32)
        near = jnp.dot(a, wide[t, :, near_cols], preferred_element_type=F32)
        new = jnp.dot(a, kv[t], preferred_element_type=F32)
        if t == 0:
            sent[...] = far
            keep[:ROWS, :] = near
            fresh[...] = new
        else:
            keep[:ROWS, :] += near
            fresh[...] += new
            if t == 3:
                send[:ROWS, :] = (sent[...] + far).astype(BF16)
            else:
                sent[...] += far
    for t in range(2):
        cols = slice(t * PAIR, (t + 1) * PAIR)
        far_rows = pl.ds(pl.multiple_of((1 - core) * 128 + t * NEW, NEW), NEW)
        near_rows = pl.ds(pl.multiple_of(core * 128 + t * NEW, NEW), NEW)
        send[ROWS:, cols] = fresh[far_rows, :].astype(BF16)
        keep[ROWS:, cols] = fresh[near_rows, :]


def first(tokens, query, key, value):
    deep = tokens.shape[1] // 4
    return pl.pallas_call(
        first_kernel,
        out_shape=[shaped((320, 512), BF16), shaped((320, 512), F32)],
        in_specs=[HBM] * 4,
        out_specs=[VMEM] * 2,
        scratch_shapes=[
            pltpu.VMEM((4, ROWS, deep), BF16),
            pltpu.VMEM((4, deep, query.shape[1]), BF16),
            pltpu.VMEM((4, deep, PAIR), BF16),
            pltpu.VMEM((ROWS, 512), F32),
            pltpu.VMEM((ROWS, PAIR), F32),
            pltpu.SemaphoreType.DMA((16,)),
        ],
        compiler_params=params(),
        cost_estimate=SMALL,
        name="first",
    )(tokens, query, key, value)


def second_kernel(keep, got, send, onward):
    x = lax.axis_index("hid_0")
    q = keep[:ROWS, :] + got[:ROWS, :].astype(F32)
    send[:ROWS, :] = q.astype(BF16)
    onward[:ROWS, :] = q
    low = keep[ROWS:, :] + got[ROWS:, :].astype(F32)
    sides = [low[:, :PAIR], low[:, PAIR:]]
    sides = [jnp.concatenate([s[:32], s[32:]], axis=1) for s in sides]
    mine = jnp.where(x == 0, sides[0], sides[1])
    other = jnp.where(x == 0, sides[1], sides[0])
    send[ROWS:, :] = other.astype(BF16)
    onward[ROWS:, :] = mine


def second(keep, got):
    return pl.pallas_call(
        second_kernel,
        out_shape=[shaped((288, 512), BF16), shaped((288, 512), F32)],
        in_specs=[VMEM] * 2,
        out_specs=[VMEM] * 2,
        compiler_params=params(8),
        cost_estimate=SMALL,
        name="second",
    )(keep, got)


def new_offset():
    return lax.axis_index("hid_1") * 128 + lax.axis_index("hid_0") * NEW


def rotate_kernel(keep, got, cosine, sine, queries, notes):
    for h in range(4):
        cols = slice(h * HD, (h + 1) * HD)
        u = keep[:ROWS, cols] + got[:ROWS, cols].astype(F32)
        turned = u * cosine[...] + pltpu.roll(u, HD // 2, 1) * sine[...]
        queries[:, cols] = turned.astype(BF16)
    low = keep[ROWS:, :] + got[ROWS:, :].astype(F32)
    low = jnp.concatenate([low[:, :PAIR], low[:, PAIR:]], axis=0)
    rows = pl.ds(pl.multiple_of(new_offset(), NEW), NEW)
    u = low[:, :HD]
    turned = u * cosine[rows, :] + pltpu.roll(u, HD // 2, 1) * sine[rows, :]
    for z in range(8):
        notes[z, :, :HD] = turned.astype(BF16)
        notes[z, :, HD:] = low[:, HD:].astype(BF16)


def rotated(keep, got, cosine, sine):
    return pl.pallas_call(
        rotate_kernel,
        out_shape=[shaped((ROWS, 512), BF16), shaped((8, NEW, PAIR), BF16)],
        in_specs=[VMEM] * 4,
        out_specs=[VMEM] * 2,
        compiler_params=params(8),
        cost_estimate=SMALL,
        name="rotated",
    )(keep, got, cosine, sine)


def gather_visible(mine, slabs, halves, new, keys, values, chunk):
    height = keys.shape[0]
    values[:, HD:] = jnp.ones((height, HD), BF16)
    n = jnp.int32(0)
    lane = lax.broadcasted_iota(jnp.int32, (16, HD), 1)
    marks = jnp.zeros((16, HD), jnp.int32)
    for i, load in enumerate(halves):
        codes = load[ROWS:, :HD].astype(F32)
        codes = jnp.where(lane == 0, 2.0, 1.0) * codes
        place = (codes + pltpu.roll(codes, HD - 1, 1)).astype(jnp.int32)
        marks = marks + jnp.where(place < mine, 1 << i, 0)
    mask = jnp.max(jnp.where(lane == 0, marks, 0))
    bit = 0
    for load in halves:
        seen = ((mask >> bit) & 1) == 1
        bit += 1

        @pl.when(seen)
        def _(load=load, n=n):
            at = pl.ds(pl.multiple_of(n * NEW, NEW), ROWS)
            keys[at, :] = load[:ROWS, :HD]
            values[at, :HD] = load[:ROWS, HD:]

        n = n + jnp.where(seen, ROWS // NEW, 0)
    if new is not None:
        for z in range(8):
            seen = slabs[z] < mine

            @pl.when(seen)
            def _(z=z, n=n):
                at = pl.ds(pl.multiple_of(n * NEW, NEW), NEW)
                keys[at, :] = new[z, :, :HD]
                values[at, :HD] = new[z, :, HD:]

            n = n + jnp.where(seen, 1, 0)
    per = chunk // NEW
    chunks = (n + per - 1) // per

    def pad(t, carry):
        at = pl.ds(pl.multiple_of(t * NEW, NEW), NEW)
        keys[at, :] = keys[:NEW, :]
        values[at, :] = jnp.zeros((NEW, PAIR), BF16)
        return carry

    lax.fori_loop(n, chunks * per, pad, 0)
    return chunks


def attend(q, peak_ref, chunks, keys, values, scores, chunk, acc_at, before):
    def peaks(i, carry):
        at = pl.ds(pl.multiple_of(i * chunk, chunk), chunk)
        s = lax.dot_general(q, keys[at, :], CONTRACT, preferred_element_type=F32)
        scores[i] = s
        best = peak_ref[...]
        for t in range(chunk // HD):
            best = jnp.maximum(best, s[:, t * HD : (t + 1) * HD])
        peak_ref[...] = best
        return carry

    lax.fori_loop(0, chunks, peaks, 0)
    peak = jnp.max(peak_ref[...], axis=1, keepdims=True)
    acc_at[...] = before(peak)

    def weigh(i, carry):
        at = pl.ds(pl.multiple_of(i * chunk, chunk), chunk)
        p = jnp.exp2((scores[i] - peak) * EXPONENT).astype(BF16)
        acc_at[...] += jnp.dot(p, values[at, :], preferred_element_type=F32)
        return carry

    lax.fori_loop(0, chunks, weigh, 0)
    return peak


def halves_of(buffers):
    halves = []
    for ref in buffers:
        for b in range(ref.shape[0] // HALF):
            halves.append(ref.at[b * HALF : (b + 1) * HALF, :])
    return halves


def near_kernel(slabs, near, far, notes, *refs, chunk, count):
    sources, (q_out, acc_out, peak_out) = refs[:count], refs[count : count + 3]
    refs = refs[count + 3 :]
    near_in, far_in, own, *loads = refs[: 3 + count]
    q_all, acc_all, peak_all, keys, values, scores, peak_ref, acc, sems = refs[3 + count :]
    pairs = [(sources[0].at[: 2 * HALF, :], loads[0])] + list(zip(sources[1:], loads[1:]))
    pairs += [(notes.at[0], own), (near, near_in), (far, far_in)]
    copies = fetch(pairs, sems.at[: count + 3])
    mine = slabs[lax.axis_index("key")]
    core = lax.axis_index("hid_1")
    x = lax.axis_index("hid_0")
    for copy in copies[:count]:
        copy.wait()
    chunks = gather_visible(mine, None, halves_of(loads), None, keys, values, chunk)
    for copy in copies[count:]:
        copy.wait()
    for j in range(4):
        half = x if j < 2 else 1 - x
        parity = core if j % 2 == 0 else 1 - core
        cols = pl.ds(pl.multiple_of(parity * PAIR, PAIR), PAIR)
        rows = [slice((2 * j + t) * ROWS, (2 * j + t + 1) * ROWS) for t in range(2)]

        @pl.when(half == core)
        def _(cols=cols, rows=rows):
            both = near_in[:, cols]
            q_all[rows[0], :] = both[:, :HD]
            q_all[rows[1], :] = both[:, HD:]

        @pl.when(half != core)
        def _(cols=cols, rows=rows):
            both = far_in[:, cols]
            q_all[rows[0], :] = both[:, :HD]
            q_all[rows[1], :] = both[:, HD:]

    out = fetch([(q_all, q_out)], sems.at[count + 3 : count + 4])
    zeros = jnp.zeros((NEW, HD), BF16)
    own_keys = jnp.concatenate([own[:, :HD], zeros], axis=0)
    own_values = jnp.concatenate([own[:, HD:], zeros], axis=0)
    own_values = jnp.concatenate([own_values, jnp.ones((HD, HD), BF16)], axis=1)
    row = lax.broadcasted_iota(jnp.int32, (TALL, HD), 0) % ROWS
    lane = lax.broadcasted_iota(jnp.int32, (TALL, HD), 1)
    visible = jnp.logical_and(lane < NEW, lane + new_offset() <= row)
    for step in range(8 * ROWS // TALL):
        at = pl.ds(step * TALL, TALL)
        q = q_all[at, :]
        s = lax.dot_general(q, own_keys, CONTRACT, preferred_element_type=F32)
        s = jnp.where(visible, s, NEGATIVE)
        peak_ref[...] = s

        def before(peak, s=s):
            p = jnp.where(visible, jnp.exp2((s - peak) * EXPONENT), 0.0)
            return jnp.dot(p.astype(BF16), own_values, preferred_element_type=F32)

        peak = attend(
            q, peak_ref, chunks, keys, values, scores, chunk, acc, before
        )
        acc_all[at, :] = acc[:, :HD]
        peak_all[at, :] = jnp.where(lane < HD // 2, peak, acc[:, HD:])
        first_sem = count + 4 + 2 * step
        out += fetch(
            [
                (acc_all.at[at, :], acc_out.at[at, :]),
                (peak_all.at[at, :], peak_out.at[at, :]),
            ],
            sems.at[first_sem : first_sem + 2],
        )
    for copy in out:
        copy.wait()


def attend_near(slabs, near, far, notes, loads):
    count, chunk = len(loads), 1280
    shapes = [(2 * HALF, PAIR)] + [a.shape for a in loads[1:]]
    height = sum(shape[0] // HALF * ROWS for shape in shapes)
    state = [((8 * ROWS, HD), BF16), ((8 * ROWS, HD), F32), ((8 * ROWS, HD), F32)]
    return pl.pallas_call(
        functools.partial(near_kernel, chunk=chunk, count=count),
        out_shape=[shaped(*s) for s in state],
        in_specs=[SMEM] + [HBM] * (3 + count),
        out_specs=[HBM] * 3,
        scratch_shapes=[
            pltpu.VMEM((ROWS, 4 * HD), BF16),
            pltpu.VMEM((ROWS, 4 * HD), BF16),
            pltpu.VMEM((NEW, PAIR), BF16),
            *[pltpu.VMEM(shape, BF16) for shape in shapes],
            *[pltpu.VMEM(*s) for s in state],
            pltpu.VMEM((height, HD), BF16),
            pltpu.VMEM((height, PAIR), BF16),
            pltpu.VMEM((height // chunk, TALL, chunk), F32),
            pltpu.VMEM((TALL, HD), F32),
            pltpu.VMEM((TALL, PAIR), F32),
            pltpu.SemaphoreType.DMA((count + 4 + 2 * (8 * ROWS // TALL),)),
        ],
        compiler_params=params(),
        cost_estimate=SMALL,
        name="near",
    )(slabs, near, far, notes, *loads)


def far_kernel(slabs, *refs, chunk, count):
    sources, outs = refs[: 4 + count], refs[4 + count : 7 + count]
    refs = refs[7 + count :]
    core = lax.axis_index("hid_1")
    outs = [outs[0].at[core], outs[0].at[1 - core], outs[1], outs[2]]
    buffers = refs[: 4 + count]
    queries, acc_in, peak_in, new, *loads = buffers
    keys, values, scores, peak_ref, acc, sems = refs[4 + count :]
    tall = 8 * ROWS
    copies = fetch(list(zip(sources, buffers))[::-1], sems)
    mine = slabs[lax.axis_index("key")]
    for copy in copies[: count + 1]:
        copy.wait()
    chunks = gather_visible(mine, slabs, halves_of(loads), new, keys, values, chunk)
    for copy in copies[count + 1 :]:
        copy.wait()
    peak_ref[...] = jnp.broadcast_to(peak_in[:, :1], (tall, HD))

    def before(peak):
        factor = jnp.exp2((peak_in[:, :1] - peak) * EXPONENT)
        total = jnp.broadcast_to(peak_in[:, HD // 2 : HD // 2 + 1], (tall, HD))
        return jnp.concatenate([acc_in[...], total], axis=1) * factor

    peak = attend(
        queries[...], peak_ref, chunks, keys, values, scores, chunk, acc, before
    )
    total = acc[:, HD:]
    heads = (acc[:, :HD] / jnp.where(total > 0.0, total, 1.0)).astype(BF16)
    lane = lax.broadcasted_iota(jnp.int32, (ROWS, HD), 1)
    totals = jnp.zeros((ROWS, HD), F32)
    peaks = jnp.zeros((ROWS, HD), F32)
    for h in range(tall // ROWS):
        rows = slice(h * ROWS, (h + 1) * ROWS)
        totals = jnp.where(lane == h, total[rows], totals)
        peaks = jnp.where(lane == h, peak[rows], peaks)
    some = totals > 0.0
    level = peaks * EXPONENT + jnp.log2(jnp.where(some, totals, 1.0))
    level = jnp.transpose(jnp.where(some, level, NEGATIVE))
    where = lax.broadcasted_iota(jnp.int32, (16, ROWS), 0)
    for t in range(tall // (2 * ROWS)):
        out = outs[t]
        table = jnp.zeros((16, ROWS), F32)
        for half in range(2):
            h = 2 * t + half
            cols = slice(half * HD, (half + 1) * HD)
            out[:ROWS, cols] = heads[h * ROWS : (h + 1) * ROWS]
            rest = level[h : h + 1, :]
            for k in range(3):
                coded = rest.astype(BF16).astype(F32)
                table = jnp.where(where == 3 * half + k, coded, table)
                rest = rest - coded
        out[ROWS:, :] = table.astype(BF16)


def attend_far(slabs, queries, acc, peak, new, loads):
    operands = [queries, acc, peak, new, *loads]
    count, chunk = len(loads), 1024
    height = sum(a.shape[0] // HALF * ROWS for a in loads) + 8 * NEW
    height = -(-height // chunk) * chunk
    tall = 8 * ROWS
    return pl.pallas_call(
        functools.partial(far_kernel, chunk=chunk, count=count),
        out_shape=[shaped((2, MSG, PAIR), BF16)] + [shaped((MSG, PAIR), BF16)] * 2,
        in_specs=[SMEM] + [HBM] * len(operands),
        out_specs=[VMEM] * 3,
        scratch_shapes=[
            *[pltpu.VMEM(a.shape, a.dtype) for a in operands],
            pltpu.VMEM((height, HD), BF16),
            pltpu.VMEM((height, PAIR), BF16),
            pltpu.VMEM((height // chunk, tall, chunk), F32),
            pltpu.VMEM((tall, HD), F32),
            pltpu.VMEM((tall, PAIR), F32),
            pltpu.SemaphoreType.DMA((len(operands),)),
        ],
        compiler_params=params(),
        cost_estimate=MEDIUM,
        name="far",
    )(slabs, *operands)


def merge_kernel(pair, straight, across, out):
    parts = [pair.at[0], pair.at[1], straight, across]
    levels = []
    for ref in parts:
        t = ref[ROWS:, :].astype(F32)
        levels.append([t[0:1] + t[1:2] + t[2:3], t[3:4] + t[4:5] + t[5:6]])
    rows = []
    for half in range(2):
        top = functools.reduce(jnp.maximum, [lv[half] for lv in levels])
        w = [jnp.exp2(lv[half] - top) for lv in levels]
        total = w[0] + w[1] + w[2] + w[3]
        rows.extend([x / total for x in w])
    table = jnp.concatenate(rows, axis=0)
    table = jnp.transpose(jnp.concatenate([table, jnp.zeros((HD - 8, ROWS), F32)], axis=0))
    for half in range(2):
        cols = slice(half * HD, (half + 1) * HD)
        so_far = None
        for t, ref in enumerate(parts):
            w = table[:, half * 4 + t : half * 4 + t + 1]
            term = ref[:ROWS, cols].astype(F32) * w
            so_far = term if so_far is None else so_far + term
        out[:, cols] = so_far.astype(BF16)


def merge(parts):
    return pl.pallas_call(
        merge_kernel,
        out_shape=shaped((ROWS, PAIR), BF16),
        in_specs=[VMEM] * 3,
        out_specs=VMEM,
        compiler_params=params(8),
        cost_estimate=SMALL,
        name="merge",
    )(*parts)


def project_kernel(*refs):
    heads, weights, send, keep = refs[:4], refs[4:8], refs[8], refs[9]
    core = lax.axis_index("hid_1")
    h = jnp.concatenate([ref[...] for ref in heads], axis=1)
    for out, side in ((send, 1 - core), (keep, core)):
        for t in range(4):
            cols = pl.ds(pl.multiple_of(t * 512 + side * ROWS, ROWS), ROWS)
            w = jnp.concatenate([ref[:, cols] for ref in weights], axis=0)
            total = jnp.dot(h, w, preferred_element_type=F32)
            out[:, t * ROWS : (t + 1) * ROWS] = total.astype(out.dtype)


def project(heads, weights):
    width = weights[0].shape[1]
    return pl.pallas_call(
        project_kernel,
        out_shape=[shaped((ROWS, width // 2), BF16), shaped((ROWS, width // 2), F32)],
        in_specs=[VMEM] * 8,
        out_specs=[VMEM] * 2,
        compiler_params=params(16),
        cost_estimate=SMALL,
        name="project",
    )(*heads, *weights)


def split_kernel(keep, got, own, *sends):
    spot = 2 * lax.axis_index("head_0") + lax.axis_index("hid_0")
    for by in range(4):
        cols = pl.ds(pl.multiple_of(lax.rem(spot + by, 4) * ROWS, ROWS), ROWS)
        total = keep[:, cols] + got[:, cols].astype(F32)
        if by == 0:
            own[...] = total
        else:
            sends[by - 1][...] = total.astype(BF16)


def split(keep, got):
    return pl.pallas_call(
        split_kernel,
        out_shape=[shaped((ROWS, ROWS), F32)] + [shaped((ROWS, ROWS), BF16)] * 3,
        in_specs=[VMEM] * 2,
        out_specs=[VMEM] * 4,
        compiler_params=params(8),
        cost_estimate=SMALL,
        name="split",
    )(keep, got)


def body(
    tokens,
    query_weight,
    key_weight,
    value_weight,
    output_weight,
    key_cache,
    value_cache,
    cache_places,
    slab_places,
):

    load, spots = pack(
        cache_places, slab_places, key_cache.reshape(-1, HD), value_cache.reshape(-1, HD)
    )

    def away(array, by):
        pairs = []
        for k in range(8):
            pairs.append((2 * k, 2 * ((k + by) % 8)))
            pairs.append((2 * k + 1, 2 * ((k - by) % 8) + 1))
        return lax.ppermute(array, ("key", "hid_1"), pairs)

    one = away(load, 1)

    pieces = columns(output_weight)

    send, keep = first(tokens, query_weight, key_weight, value_weight)
    one, keep, pieces = lax.optimization_barrier((one, keep, pieces))
    two = away(one, 1)
    send, keep = second(keep, swap(send, "hid_1"))
    got = swap(send, "hid_0")
    weights = [pieces[3]]
    for piece, by in zip(pieces, (2, 1, 3)):
        weights.append(lax.ppermute(piece, "head_1", shift(4, by)))

    middle = HD // 2
    index = np.arange(HD) % middle
    frequency = jnp.exp(jnp.asarray(index, F32) * (-2.0 * math.log(THETA) / HD))
    sign = np.where(np.arange(HD) < middle, -1.0, 1.0).astype(np.float32)
    angles = spots * frequency[None, :]
    cosine, sine = jnp.cos(angles), jnp.sin(angles) * sign[None, :]
    two, cosine, sine = lax.optimization_barrier((two, cosine, sine))
    three = away(two, 1)
    queries, notes = rotated(keep, got, cosine, sine)
    far = swap(queries, "hid_1")
    far, onward = lax.optimization_barrier((far, two[: 2 * HALF]))
    four = away(onward, 2)

    new = lax.all_to_all(notes, "key", split_axis=0, concat_axis=0, tiled=True)

    state = attend_near(slab_places, queries, far, notes, [load, one, two])
    pair, straight, across = attend_far(slab_places, *state, new, [three, four])
    parts = [
        lax.all_to_all(pair, "hid_1", split_axis=0, concat_axis=0, tiled=True),
        swap(straight, "hid_0"),
        lax.ppermute(across, HID, [(0, 3), (1, 2), (2, 1), (3, 0)]),
    ]
    parts, weights = lax.optimization_barrier((parts, weights))
    merged = merge(parts)

    heads = [merged] + [lax.ppermute(merged, "head_1", shift(4, by)) for by in (2, 1, 3)]
    send, keep = project(heads, weights)
    own, *blocks = split(keep, swap(send, "hid_1"))
    out = own
    for by in (2, 1, 3):
        out = out + lax.ppermute(blocks[by - 1], ALONG_X, shift(4, by)).astype(F32)
    return out.astype(BF16)


def solution(mesh):
    finer = Mesh(
        mesh.devices.reshape(2, 4, mesh.shape["key"], 2, 2),
        ("head_0", "head_1", "key", "hid_0", "hid_1"),
    )
    return jax.shard_map(
        body,
        mesh=finer,
        in_specs=(
            P("key", HID),
            P(HID, HEAD),
            P(HID, HEAD),
            P(HID, HEAD),
            P(HEAD_HID, None),
            P("key", HEAD, None),
            P("key", HEAD, None),
            P("key"),
            P(),
        ),
        out_specs=P("key", HEAD_HID),
        check_vma=False,
    )
```

```python
import functools
import math

import jax
import jax.numpy as jnp
import numpy as np
from jax import lax
from jax.experimental import pallas as pl
from jax.experimental.pallas import tpu as pltpu
from jax.sharding import Mesh
from jax.sharding import PartitionSpec as P

HID = ("hid_0", "hid_1")
HEAD = ("head_0", "head_1")
HEAD_HID = ("head_0", "head_1", "hid_0", "hid_1")
ALONG_X = ("head_0", "hid_0")

THETA = 500000.0
NEGATIVE = -1e30
BF16 = jnp.bfloat16
F32 = jnp.float32

ROWS = 256
HD = 128
PAIR = 2 * HD
NEW = 64
QUARTER = 512
HALF = ROWS + 16
LOAD = 4 * HALF
MSG = ROWS + 16
TALL = 2048
EXPONENT = math.log2(math.e) / math.sqrt(HD)
CONTRACT = (((1,), (1,)), ((), ()))

VMEM = pl.BlockSpec(memory_space=pltpu.VMEM)
SMEM = pl.BlockSpec(memory_space=pltpu.SMEM)
HBM = pl.BlockSpec(memory_space=pltpu.HBM)


def shaped(shape, dtype):
    return jax.ShapeDtypeStruct(shape, dtype)


def params(mib=60):
    return pltpu.CompilerParams(vmem_limit_bytes=mib * 2**20)


SMALL = pl.CostEstimate(flops=1, bytes_accessed=1, transcendentals=0)
MEDIUM = pl.CostEstimate(flops=2**30, bytes_accessed=2**18, transcendentals=2**10)


def shift(n, by):
    return [(i, (i + by) % n) for i in range(n)]


def swap(array, axis):
    return lax.ppermute(array, axis, shift(2, 1))


def hid_index():
    return 2 * lax.axis_index("hid_0") + lax.axis_index("hid_1")


def fetch(pairs, sems):
    copies = [
        pltpu.make_async_copy(source, target, sems.at[i])
        for i, (source, target) in enumerate(pairs)
    ]
    for copy in copies:
        copy.start()
    return copies


def pack_kernel(places, slabs, keys, values, out, spots, load, sems):
    core = lax.axis_index("hid_1")
    lane = lax.broadcasted_iota(jnp.int32, (16, PAIR), 1)
    pairs = []
    for i in range(4):
        block = 4 * lax.axis_index("hid_0") + lax.rem(2 * core + i, 4)
        rows = pl.ds(pl.multiple_of(block * ROWS, ROWS), ROWS)
        to = slice(i * HALF, i * HALF + ROWS)
        pairs.append((keys.at[rows, :], load.at[to, :HD]))
        pairs.append((values.at[rows, :], load.at[to, HD:]))
        place = places[block]
        table = jnp.where(lane == 0, place >> 1, jnp.where(lane == 1, place & 1, 0))
        load[i * HALF + ROWS : (i + 1) * HALF, :] = table.astype(F32).astype(BF16)
    copies = fetch(pairs, sems.at[:8])
    leaving = []
    for i in range(4):
        copies[2 * i].wait()
        copies[2 * i + 1].wait()
        to = slice(i * HALF, (i + 1) * HALF)
        leaving += fetch([(load.at[to, :], out.at[to, :])], sems.at[8 + i : 9 + i])
    row = lax.broadcasted_iota(jnp.int32, (ROWS, HD), 0)
    spots[...] = (slabs[lax.axis_index("key")] * ROWS + row).astype(F32)
    for copy in leaving:
        copy.wait()


def pack(places, slabs, keys, values):
    return pl.pallas_call(
        pack_kernel,
        out_shape=[shaped((LOAD, PAIR), BF16), shaped((ROWS, HD), F32)],
        in_specs=[SMEM, SMEM, HBM, HBM],
        out_specs=[HBM, VMEM],
        scratch_shapes=[pltpu.VMEM((LOAD, PAIR), BF16), pltpu.SemaphoreType.DMA((12,))],
        compiler_params=params(),
        cost_estimate=SMALL,
        name="pack",
    )(places, slabs, keys, values)


def columns_kernel(weight, *refs):
    outs, pieces, sems, out_sems = refs[:4], refs[4], refs[5], refs[6]
    y = lax.axis_index("head_1")
    pairs = []
    for t, by in enumerate((2, 1, 3, 0)):
        at = lax.rem(y + by, 4) * 1024
        for hi in range(2):
            source = pl.ds(pl.multiple_of(hi * 4096 + at, 1024), 1024)
            pairs.append((weight.at[:, source], pieces.at[t, :, hi * 1024 : (hi + 1) * 1024]))
    copies = fetch(pairs, sems)
    leaving = []
    for t in range(4):
        copies[2 * t].wait()
        copies[2 * t + 1].wait()
        leaving += fetch([(pieces.at[t], outs[t])], out_sems.at[t : t + 1])
    for copy in leaving:
        copy.wait()


def columns(weight):
    return pl.pallas_call(
        columns_kernel,
        out_shape=[shaped((ROWS, 2048), BF16)] * 4,
        in_specs=[HBM],
        out_specs=[HBM] * 4,
        scratch_shapes=[
            pltpu.VMEM((4, ROWS, 2048), BF16),
            pltpu.SemaphoreType.DMA((8,)),
            pltpu.SemaphoreType.DMA((4,)),
        ],
        compiler_params=params(),
        cost_estimate=SMALL,
        name="columns",
    )(weight)


def first_kernel(tokens, query, key, value, send, keep, tok, wide, kv, sent, fresh, sems):
    core = lax.axis_index("hid_1")
    deep = tok.shape[2]
    copies = []
    for t in range(4):
        part = slice(t * deep, (t + 1) * deep)
        pairs = [
            (tokens.at[:, part], tok.at[t]),
            (query.at[part, :], wide.at[t]),
            (key.at[part, :], kv.at[t, :, :HD]),
            (value.at[part, :], kv.at[t, :, HD:]),
        ]
        copies.append(fetch(pairs, sems.at[4 * t : 4 * t + 4]))
    far_cols = pl.ds(pl.multiple_of((1 - core) * 512, 512), 512)
    near_cols = pl.ds(pl.multiple_of(core * 512, 512), 512)
    for t in range(4):
        for copy in copies[t]:
            copy.wait()
        a = tok[t]
        far = jnp.dot(a, wide[t, :, far_cols], preferred_element_type=F32)
        near = jnp.dot(a, wide[t, :, near_cols], preferred_element_type=F32)
        new = jnp.dot(a, kv[t], preferred_element_type=F32)
        if t == 0:
            sent[...] = far
            keep[:ROWS, :] = near
            fresh[...] = new
        else:
            keep[:ROWS, :] += near
            fresh[...] += new
            if t == 3:
                send[:ROWS, :] = (sent[...] + far).astype(BF16)
            else:
                sent[...] += far
    for t in range(2):
        cols = slice(t * PAIR, (t + 1) * PAIR)
        far_rows = pl.ds(pl.multiple_of((1 - core) * 128 + t * NEW, NEW), NEW)
        near_rows = pl.ds(pl.multiple_of(core * 128 + t * NEW, NEW), NEW)
        send[ROWS:, cols] = fresh[far_rows, :].astype(BF16)
        keep[ROWS:, cols] = fresh[near_rows, :]


def first(tokens, query, key, value):
    deep = tokens.shape[1] // 4
    return pl.pallas_call(
        first_kernel,
        out_shape=[shaped((320, 512), BF16), shaped((320, 512), F32)],
        in_specs=[HBM] * 4,
        out_specs=[VMEM] * 2,
        scratch_shapes=[
            pltpu.VMEM((4, ROWS, deep), BF16),
            pltpu.VMEM((4, deep, query.shape[1]), BF16),
            pltpu.VMEM((4, deep, PAIR), BF16),
            pltpu.VMEM((ROWS, 512), F32),
            pltpu.VMEM((ROWS, PAIR), F32),
            pltpu.SemaphoreType.DMA((16,)),
        ],
        compiler_params=params(),
        cost_estimate=SMALL,
        name="first",
    )(tokens, query, key, value)


def second_kernel(keep, got, send, onward):
    x = lax.axis_index("hid_0")
    q = keep[:ROWS, :] + got[:ROWS, :].astype(F32)
    send[:ROWS, :] = q.astype(BF16)
    onward[:ROWS, :] = q
    low = keep[ROWS:, :] + got[ROWS:, :].astype(F32)
    sides = [low[:, :PAIR], low[:, PAIR:]]
    sides = [jnp.concatenate([s[:32], s[32:]], axis=1) for s in sides]
    mine = jnp.where(x == 0, sides[0], sides[1])
    other = jnp.where(x == 0, sides[1], sides[0])
    send[ROWS:, :] = other.astype(BF16)
    onward[ROWS:, :] = mine


def second(keep, got):
    return pl.pallas_call(
        second_kernel,
        out_shape=[shaped((288, 512), BF16), shaped((288, 512), F32)],
        in_specs=[VMEM] * 2,
        out_specs=[VMEM] * 2,
        compiler_params=params(8),
        cost_estimate=SMALL,
        name="second",
    )(keep, got)


def new_offset():
    return lax.axis_index("hid_1") * 128 + lax.axis_index("hid_0") * NEW


def rotate_kernel(keep, got, cosine, sine, queries, notes):
    for h in range(4):
        cols = slice(h * HD, (h + 1) * HD)
        u = keep[:ROWS, cols] + got[:ROWS, cols].astype(F32)
        turned = u * cosine[...] + pltpu.roll(u, HD // 2, 1) * sine[...]
        queries[:, cols] = turned.astype(BF16)
    low = keep[ROWS:, :] + got[ROWS:, :].astype(F32)
    low = jnp.concatenate([low[:, :PAIR], low[:, PAIR:]], axis=0)
    rows = pl.ds(pl.multiple_of(new_offset(), NEW), NEW)
    u = low[:, :HD]
    turned = u * cosine[rows, :] + pltpu.roll(u, HD // 2, 1) * sine[rows, :]
    for z in range(8):
        notes[z, :, :HD] = turned.astype(BF16)
        notes[z, :, HD:] = low[:, HD:].astype(BF16)


def rotated(keep, got, cosine, sine):
    return pl.pallas_call(
        rotate_kernel,
        out_shape=[shaped((ROWS, 512), BF16), shaped((8, NEW, PAIR), BF16)],
        in_specs=[VMEM] * 4,
        out_specs=[VMEM] * 2,
        compiler_params=params(8),
        cost_estimate=SMALL,
        name="rotated",
    )(keep, got, cosine, sine)


def gather_visible(mine, slabs, halves, new, keys, values, chunk):
    height = keys.shape[0]
    values[:, HD:] = jnp.ones((height, HD), BF16)
    n = jnp.int32(0)
    lane = lax.broadcasted_iota(jnp.int32, (16, HD), 1)
    marks = jnp.zeros((16, HD), jnp.int32)
    for i, load in enumerate(halves):
        codes = load[ROWS:, :HD].astype(F32)
        codes = jnp.where(lane == 0, 2.0, 1.0) * codes
        place = (codes + pltpu.roll(codes, HD - 1, 1)).astype(jnp.int32)
        marks = marks + jnp.where(place < mine, 1 << i, 0)
    mask = jnp.max(jnp.where(lane == 0, marks, 0))
    bit = 0
    for load in halves:
        seen = ((mask >> bit) & 1) == 1
        bit += 1

        @pl.when(seen)
        def _(load=load, n=n):
            at = pl.ds(pl.multiple_of(n * NEW, NEW), ROWS)
            keys[at, :] = load[:ROWS, :HD]
            values[at, :HD] = load[:ROWS, HD:]

        n = n + jnp.where(seen, ROWS // NEW, 0)
    if new is not None:
        for z in range(8):
            seen = slabs[z] < mine

            @pl.when(seen)
            def _(z=z, n=n):
                at = pl.ds(pl.multiple_of(n * NEW, NEW), NEW)
                keys[at, :] = new[z, :, :HD]
                values[at, :HD] = new[z, :, HD:]

            n = n + jnp.where(seen, 1, 0)
    per = chunk // NEW
    chunks = (n + per - 1) // per

    def pad(t, carry):
        at = pl.ds(pl.multiple_of(t * NEW, NEW), NEW)
        keys[at, :] = keys[:NEW, :]
        values[at, :] = jnp.zeros((NEW, PAIR), BF16)
        return carry

    lax.fori_loop(n, chunks * per, pad, 0)
    return chunks


def attend(q, peak_ref, chunks, keys, values, scores, chunk, acc_at, before):
    def peaks(i, carry):
        at = pl.ds(pl.multiple_of(i * chunk, chunk), chunk)
        s = lax.dot_general(q, keys[at, :], CONTRACT, preferred_element_type=F32)
        scores[i] = s
        best = peak_ref[...]
        for t in range(chunk // HD):
            best = jnp.maximum(best, s[:, t * HD : (t + 1) * HD])
        peak_ref[...] = best
        return carry

    lax.fori_loop(0, chunks, peaks, 0)
    peak = jnp.max(peak_ref[...], axis=1, keepdims=True)
    acc_at[...] = before(peak)

    def weigh(i, carry):
        at = pl.ds(pl.multiple_of(i * chunk, chunk), chunk)
        p = jnp.exp2((scores[i] - peak) * EXPONENT).astype(BF16)
        acc_at[...] += jnp.dot(p, values[at, :], preferred_element_type=F32)
        return carry

    lax.fori_loop(0, chunks, weigh, 0)
    return peak


def halves_of(buffers):
    halves = []
    for ref in buffers:
        for b in range(ref.shape[0] // HALF):
            halves.append(ref.at[b * HALF : (b + 1) * HALF, :])
    return halves


def near_kernel(slabs, near, far, notes, *refs, chunk, count):
    sources, (q_out, acc_out, peak_out) = refs[:count], refs[count : count + 3]
    refs = refs[count + 3 :]
    near_in, far_in, own, *loads = refs[: 3 + count]
    q_all, acc_all, peak_all, keys, values, scores, peak_ref, acc, sems = refs[3 + count :]
    pairs = [(sources[0].at[: 2 * HALF, :], loads[0])] + list(zip(sources[1:], loads[1:]))
    pairs += [(notes.at[0], own), (near, near_in), (far, far_in)]
    copies = fetch(pairs, sems.at[: count + 3])
    mine = slabs[lax.axis_index("key")]
    core = lax.axis_index("hid_1")
    x = lax.axis_index("hid_0")
    for copy in copies[:count]:
        copy.wait()
    chunks = gather_visible(mine, None, halves_of(loads), None, keys, values, chunk)
    for copy in copies[count:]:
        copy.wait()
    for j in range(4):
        half = x if j < 2 else 1 - x
        parity = core if j % 2 == 0 else 1 - core
        cols = pl.ds(pl.multiple_of(parity * PAIR, PAIR), PAIR)
        rows = [slice((2 * j + t) * ROWS, (2 * j + t + 1) * ROWS) for t in range(2)]

        @pl.when(half == core)
        def _(cols=cols, rows=rows):
            both = near_in[:, cols]
            q_all[rows[0], :] = both[:, :HD]
            q_all[rows[1], :] = both[:, HD:]

        @pl.when(half != core)
        def _(cols=cols, rows=rows):
            both = far_in[:, cols]
            q_all[rows[0], :] = both[:, :HD]
            q_all[rows[1], :] = both[:, HD:]

    out = fetch([(q_all, q_out)], sems.at[count + 3 : count + 4])
    zeros = jnp.zeros((NEW, HD), BF16)
    own_keys = jnp.concatenate([own[:, :HD], zeros], axis=0)
    own_values = jnp.concatenate([own[:, HD:], zeros], axis=0)
    own_values = jnp.concatenate([own_values, jnp.ones((HD, HD), BF16)], axis=1)
    row = lax.broadcasted_iota(jnp.int32, (TALL, HD), 0) % ROWS
    lane = lax.broadcasted_iota(jnp.int32, (TALL, HD), 1)
    visible = jnp.logical_and(lane < NEW, lane + new_offset() <= row)
    for step in range(8 * ROWS // TALL):
        at = pl.ds(step * TALL, TALL)
        q = q_all[at, :]
        s = lax.dot_general(q, own_keys, CONTRACT, preferred_element_type=F32)
        s = jnp.where(visible, s, NEGATIVE)
        peak_ref[...] = s

        def before(peak, s=s):
            p = jnp.where(visible, jnp.exp2((s - peak) * EXPONENT), 0.0)
            return jnp.dot(p.astype(BF16), own_values, preferred_element_type=F32)

        peak = attend(
            q, peak_ref, chunks, keys, values, scores, chunk, acc, before
        )
        acc_all[at, :] = acc[:, :HD]
        peak_all[at, :] = jnp.where(lane < HD // 2, peak, acc[:, HD:])
        first_sem = count + 4 + 2 * step
        out += fetch(
            [
                (acc_all.at[at, :], acc_out.at[at, :]),
                (peak_all.at[at, :], peak_out.at[at, :]),
            ],
            sems.at[first_sem : first_sem + 2],
        )
    for copy in out:
        copy.wait()


def attend_near(slabs, near, far, notes, loads):
    count, chunk = len(loads), 1280
    shapes = [(2 * HALF, PAIR)] + [a.shape for a in loads[1:]]
    height = sum(shape[0] // HALF * ROWS for shape in shapes)
    state = [((8 * ROWS, HD), BF16), ((8 * ROWS, HD), F32), ((8 * ROWS, HD), F32)]
    return pl.pallas_call(
        functools.partial(near_kernel, chunk=chunk, count=count),
        out_shape=[shaped(*s) for s in state],
        in_specs=[SMEM] + [HBM] * (3 + count),
        out_specs=[HBM] * 3,
        scratch_shapes=[
            pltpu.VMEM((ROWS, 4 * HD), BF16),
            pltpu.VMEM((ROWS, 4 * HD), BF16),
            pltpu.VMEM((NEW, PAIR), BF16),
            *[pltpu.VMEM(shape, BF16) for shape in shapes],
            *[pltpu.VMEM(*s) for s in state],
            pltpu.VMEM((height, HD), BF16),
            pltpu.VMEM((height, PAIR), BF16),
            pltpu.VMEM((height // chunk, TALL, chunk), F32),
            pltpu.VMEM((TALL, HD), F32),
            pltpu.VMEM((TALL, PAIR), F32),
            pltpu.SemaphoreType.DMA((count + 4 + 2 * (8 * ROWS // TALL),)),
        ],
        compiler_params=params(),
        cost_estimate=SMALL,
        name="near",
    )(slabs, near, far, notes, *loads)


def far_kernel(slabs, *refs, chunk, count):
    sources, outs = refs[: 4 + count], refs[4 + count : 7 + count]
    refs = refs[7 + count :]
    core = lax.axis_index("hid_1")
    outs = [outs[0].at[core], outs[0].at[1 - core], outs[1], outs[2]]
    buffers = refs[: 4 + count]
    queries, acc_in, peak_in, new, *loads = buffers
    keys, values, scores, peak_ref, acc, sems = refs[4 + count :]
    tall = 8 * ROWS
    copies = fetch(list(zip(sources, buffers))[::-1], sems)
    mine = slabs[lax.axis_index("key")]
    for copy in copies[: count + 1]:
        copy.wait()
    chunks = gather_visible(mine, slabs, halves_of(loads), new, keys, values, chunk)
    for copy in copies[count + 1 :]:
        copy.wait()
    peak_ref[...] = jnp.broadcast_to(peak_in[:, :1], (tall, HD))

    def before(peak):
        factor = jnp.exp2((peak_in[:, :1] - peak) * EXPONENT)
        total = jnp.broadcast_to(peak_in[:, HD // 2 : HD // 2 + 1], (tall, HD))
        return jnp.concatenate([acc_in[...], total], axis=1) * factor

    peak = attend(
        queries[...], peak_ref, chunks, keys, values, scores, chunk, acc, before
    )
    total = acc[:, HD:]
    heads = (acc[:, :HD] / jnp.where(total > 0.0, total, 1.0)).astype(BF16)
    lane = lax.broadcasted_iota(jnp.int32, (ROWS, HD), 1)
    totals = jnp.zeros((ROWS, HD), F32)
    peaks = jnp.zeros((ROWS, HD), F32)
    for h in range(tall // ROWS):
        rows = slice(h * ROWS, (h + 1) * ROWS)
        totals = jnp.where(lane == h, total[rows], totals)
        peaks = jnp.where(lane == h, peak[rows], peaks)
    some = totals > 0.0
    level = peaks * EXPONENT + jnp.log2(jnp.where(some, totals, 1.0))
    level = jnp.transpose(jnp.where(some, level, NEGATIVE))
    where = lax.broadcasted_iota(jnp.int32, (16, ROWS), 0)
    for t in range(tall // (2 * ROWS)):
        out = outs[t]
        table = jnp.zeros((16, ROWS), F32)
        for half in range(2):
            h = 2 * t + half
            cols = slice(half * HD, (half + 1) * HD)
            out[:ROWS, cols] = heads[h * ROWS : (h + 1) * ROWS]
            rest = level[h : h + 1, :]
            for k in range(3):
                coded = rest.astype(BF16).astype(F32)
                table = jnp.where(where == 3 * half + k, coded, table)
                rest = rest - coded
        out[ROWS:, :] = table.astype(BF16)


def attend_far(slabs, queries, acc, peak, new, loads):
    operands = [queries, acc, peak, new, *loads]
    count, chunk = len(loads), 1024
    height = sum(a.shape[0] // HALF * ROWS for a in loads) + 8 * NEW
    height = -(-height // chunk) * chunk
    tall = 8 * ROWS
    return pl.pallas_call(
        functools.partial(far_kernel, chunk=chunk, count=count),
        out_shape=[shaped((2, MSG, PAIR), BF16)] + [shaped((MSG, PAIR), BF16)] * 2,
        in_specs=[SMEM] + [HBM] * len(operands),
        out_specs=[VMEM] * 3,
        scratch_shapes=[
            *[pltpu.VMEM(a.shape, a.dtype) for a in operands],
            pltpu.VMEM((height, HD), BF16),
            pltpu.VMEM((height, PAIR), BF16),
            pltpu.VMEM((height // chunk, tall, chunk), F32),
            pltpu.VMEM((tall, HD), F32),
            pltpu.VMEM((tall, PAIR), F32),
            pltpu.SemaphoreType.DMA((len(operands),)),
        ],
        compiler_params=params(),
        cost_estimate=MEDIUM,
        name="far",
    )(slabs, *operands)


def merge_kernel(pair, straight, across, out):
    parts = [pair.at[0], pair.at[1], straight, across]
    levels = []
    for ref in parts:
        t = ref[ROWS:, :].astype(F32)
        levels.append([t[0:1] + t[1:2] + t[2:3], t[3:4] + t[4:5] + t[5:6]])
    rows = []
    for half in range(2):
        top = functools.reduce(jnp.maximum, [lv[half] for lv in levels])
        w = [jnp.exp2(lv[half] - top) for lv in levels]
        total = w[0] + w[1] + w[2] + w[3]
        rows.extend([x / total for x in w])
    table = jnp.concatenate(rows, axis=0)
    table = jnp.transpose(jnp.concatenate([table, jnp.zeros((HD - 8, ROWS), F32)], axis=0))
    for half in range(2):
        cols = slice(half * HD, (half + 1) * HD)
        so_far = None
        for t, ref in enumerate(parts):
            w = table[:, half * 4 + t : half * 4 + t + 1]
            term = ref[:ROWS, cols].astype(F32) * w
            so_far = term if so_far is None else so_far + term
        out[:, cols] = so_far.astype(BF16)


def merge(parts):
    return pl.pallas_call(
        merge_kernel,
        out_shape=shaped((ROWS, PAIR), BF16),
        in_specs=[VMEM] * 3,
        out_specs=VMEM,
        compiler_params=params(8),
        cost_estimate=SMALL,
        name="merge",
    )(*parts)


def project_kernel(*refs):
    heads, weights, send, keep = refs[:4], refs[4:8], refs[8], refs[9]
    core = lax.axis_index("hid_1")
    h = jnp.concatenate([ref[...] for ref in heads], axis=1)
    for out, side in ((send, 1 - core), (keep, core)):
        for t in range(4):
            cols = pl.ds(pl.multiple_of(t * 512 + side * ROWS, ROWS), ROWS)
            w = jnp.concatenate([ref[:, cols] for ref in weights], axis=0)
            total = jnp.dot(h, w, preferred_element_type=F32)
            out[:, t * ROWS : (t + 1) * ROWS] = total.astype(out.dtype)


def project(heads, weights):
    width = weights[0].shape[1]
    return pl.pallas_call(
        project_kernel,
        out_shape=[shaped((ROWS, width // 2), BF16), shaped((ROWS, width // 2), F32)],
        in_specs=[VMEM] * 8,
        out_specs=[VMEM] * 2,
        compiler_params=params(16),
        cost_estimate=SMALL,
        name="project",
    )(*heads, *weights)


def split_kernel(keep, got, own, *sends):
    spot = 2 * lax.axis_index("head_0") + lax.axis_index("hid_0")
    for by in range(4):
        cols = pl.ds(pl.multiple_of(lax.rem(spot + by, 4) * ROWS, ROWS), ROWS)
        total = keep[:, cols] + got[:, cols].astype(F32)
        if by == 0:
            own[...] = total
        else:
            sends[by - 1][...] = total.astype(BF16)


def split(keep, got):
    return pl.pallas_call(
        split_kernel,
        out_shape=[shaped((ROWS, ROWS), F32)] + [shaped((ROWS, ROWS), BF16)] * 3,
        in_specs=[VMEM] * 2,
        out_specs=[VMEM] * 4,
        compiler_params=params(8),
        cost_estimate=SMALL,
        name="split",
    )(keep, got)


def body(
    tokens,
    query_weight,
    key_weight,
    value_weight,
    output_weight,
    key_cache,
    value_cache,
    cache_places,
    slab_places,
):

    load, spots = pack(
        cache_places, slab_places, key_cache.reshape(-1, HD), value_cache.reshape(-1, HD)
    )

    def away(array, by):
        pairs = []
        for k in range(8):
            pairs.append((2 * k, 2 * ((k + by) % 8)))
            pairs.append((2 * k + 1, 2 * ((k - by) % 8) + 1))
        return lax.ppermute(array, ("key", "hid_1"), pairs)

    one = away(load, 1)

    pieces = columns(output_weight)

    send, keep = first(tokens, query_weight, key_weight, value_weight)
    one, keep, pieces = lax.optimization_barrier((one, keep, pieces))
    two = away(one, 1)
    send, keep = second(keep, swap(send, "hid_1"))
    keep, pieces = lax.optimization_barrier((keep, pieces))
    got = swap(send, "hid_0")
    weights = [pieces[3]]
    for piece, by in zip(pieces, (2, 1, 3)):
        weights.append(lax.ppermute(piece, "head_1", shift(4, by)))

    middle = HD // 2
    index = np.arange(HD) % middle
    frequency = jnp.exp(jnp.asarray(index, F32) * (-2.0 * math.log(THETA) / HD))
    sign = np.where(np.arange(HD) < middle, -1.0, 1.0).astype(np.float32)
    angles = spots * frequency[None, :]
    cosine, sine = jnp.cos(angles), jnp.sin(angles) * sign[None, :]
    queries, notes = rotated(keep, got, cosine, sine)
    two, queries = lax.optimization_barrier((two, queries))
    three = away(two, 1)
    far = swap(queries, "hid_1")
    far, onward = lax.optimization_barrier((far, two[: 2 * HALF]))
    four = away(onward, 2)

    new = lax.all_to_all(notes, "key", split_axis=0, concat_axis=0, tiled=True)

    state = attend_near(slab_places, queries, far, notes, [load, one, two])
    pair, straight, across = attend_far(slab_places, *state, new, [three, four])
    parts = [
        lax.all_to_all(pair, "hid_1", split_axis=0, concat_axis=0, tiled=True),
        swap(straight, "hid_0"),
        lax.ppermute(across, HID, [(0, 3), (1, 2), (2, 1), (3, 0)]),
    ]
    parts, weights = lax.optimization_barrier((parts, weights))
    merged = merge(parts)

    heads = [merged] + [lax.ppermute(merged, "head_1", shift(4, by)) for by in (2, 1, 3)]
    send, keep = project(heads, weights)
    own, *blocks = split(keep, swap(send, "hid_1"))
    out = own
    for by in (2, 1, 3):
        out = out + lax.ppermute(blocks[by - 1], ALONG_X, shift(4, by)).astype(F32)
    return out.astype(BF16)


def solution(mesh):
    finer = Mesh(
        mesh.devices.reshape(2, 4, mesh.shape["key"], 2, 2),
        ("head_0", "head_1", "key", "hid_0", "hid_1"),
    )
    return jax.shard_map(
        body,
        mesh=finer,
        in_specs=(
            P("key", HID),
            P(HID, HEAD),
            P(HID, HEAD),
            P(HID, HEAD),
            P(HEAD_HID, None),
            P("key", HEAD, None),
            P("key", HEAD, None),
            P("key"),
            P(),
        ),
        out_specs=P("key", HEAD_HID),
        check_vma=False,
    )
```

```python
import functools
import math

import jax
import jax.numpy as jnp
import numpy as np
from jax import lax
from jax.experimental import pallas as pl
from jax.experimental.pallas import tpu as pltpu
from jax.sharding import Mesh
from jax.sharding import PartitionSpec as P

HID = ("hid_0", "hid_1")
HEAD = ("head_0", "head_1")
HEAD_HID = ("head_0", "head_1", "hid_0", "hid_1")
ALONG_X = ("head_0", "hid_0")

THETA = 500000.0
NEGATIVE = -1e30
BF16 = jnp.bfloat16
F32 = jnp.float32

ROWS = 256
HD = 128
PAIR = 2 * HD
NEW = 64
QUARTER = 512
HALF = ROWS + 16
LOAD = 4 * HALF
MSG = ROWS + 16
TALL = 2048
EXPONENT = math.log2(math.e) / math.sqrt(HD)
CONTRACT = (((1,), (1,)), ((), ()))

VMEM = pl.BlockSpec(memory_space=pltpu.VMEM)
SMEM = pl.BlockSpec(memory_space=pltpu.SMEM)
HBM = pl.BlockSpec(memory_space=pltpu.HBM)


def shaped(shape, dtype):
    return jax.ShapeDtypeStruct(shape, dtype)


def params(mib=60):
    return pltpu.CompilerParams(vmem_limit_bytes=mib * 2**20)


SMALL = pl.CostEstimate(flops=1, bytes_accessed=1, transcendentals=0)
MEDIUM = pl.CostEstimate(flops=2**30, bytes_accessed=2**18, transcendentals=2**10)


def shift(n, by):
    return [(i, (i + by) % n) for i in range(n)]


def swap(array, axis):
    return lax.ppermute(array, axis, shift(2, 1))


def hid_index():
    return 2 * lax.axis_index("hid_0") + lax.axis_index("hid_1")


def fetch(pairs, sems):
    copies = [
        pltpu.make_async_copy(source, target, sems.at[i])
        for i, (source, target) in enumerate(pairs)
    ]
    for copy in copies:
        copy.start()
    return copies


def pack_kernel(places, slabs, keys, values, out, spots, load, sems):
    core = lax.axis_index("hid_1")
    lane = lax.broadcasted_iota(jnp.int32, (16, PAIR), 1)
    pairs = []
    for i in range(4):
        block = 4 * lax.axis_index("hid_0") + lax.rem(2 * core + i, 4)
        rows = pl.ds(pl.multiple_of(block * ROWS, ROWS), ROWS)
        to = slice(i * HALF, i * HALF + ROWS)
        pairs.append((keys.at[rows, :], load.at[to, :HD]))
        pairs.append((values.at[rows, :], load.at[to, HD:]))
        place = places[block]
        table = jnp.where(lane == 0, place >> 1, jnp.where(lane == 1, place & 1, 0))
        load[i * HALF + ROWS : (i + 1) * HALF, :] = table.astype(F32).astype(BF16)
    copies = fetch(pairs, sems.at[:8])
    leaving = []
    for i in range(4):
        copies[2 * i].wait()
        copies[2 * i + 1].wait()
        to = slice(i * HALF, (i + 1) * HALF)
        leaving += fetch([(load.at[to, :], out.at[to, :])], sems.at[8 + i : 9 + i])
    row = lax.broadcasted_iota(jnp.int32, (ROWS, HD), 0)
    spots[...] = (slabs[lax.axis_index("key")] * ROWS + row).astype(F32)
    for copy in leaving:
        copy.wait()


def pack(places, slabs, keys, values):
    return pl.pallas_call(
        pack_kernel,
        out_shape=[shaped((LOAD, PAIR), BF16), shaped((ROWS, HD), F32)],
        in_specs=[SMEM, SMEM, HBM, HBM],
        out_specs=[HBM, VMEM],
        scratch_shapes=[pltpu.VMEM((LOAD, PAIR), BF16), pltpu.SemaphoreType.DMA((12,))],
        compiler_params=params(),
        cost_estimate=SMALL,
        name="pack",
    )(places, slabs, keys, values)


def columns_kernel(weight, *refs):
    outs, pieces, sems, out_sems = refs[:4], refs[4], refs[5], refs[6]
    y = lax.axis_index("head_1")
    pairs = []
    for t, by in enumerate((2, 1, 3, 0)):
        at = lax.rem(y + by, 4) * 1024
        for hi in range(2):
            source = pl.ds(pl.multiple_of(hi * 4096 + at, 1024), 1024)
            pairs.append((weight.at[:, source], pieces.at[t, :, hi * 1024 : (hi + 1) * 1024]))
    copies = fetch(pairs, sems)
    leaving = []
    for t in range(4):
        copies[2 * t].wait()
        copies[2 * t + 1].wait()
        leaving += fetch([(pieces.at[t], outs[t])], out_sems.at[t : t + 1])
    for copy in leaving:
        copy.wait()


def columns(weight):
    return pl.pallas_call(
        columns_kernel,
        out_shape=[shaped((ROWS, 2048), BF16)] * 4,
        in_specs=[HBM],
        out_specs=[HBM] * 4,
        scratch_shapes=[
            pltpu.VMEM((4, ROWS, 2048), BF16),
            pltpu.SemaphoreType.DMA((8,)),
            pltpu.SemaphoreType.DMA((4,)),
        ],
        compiler_params=params(),
        cost_estimate=SMALL,
        name="columns",
    )(weight)


def first_kernel(tokens, query, key, value, send, keep, tok, wide, kv, sent, fresh, sems):
    core = lax.axis_index("hid_1")
    deep = tok.shape[2]
    copies = []
    for t in range(4):
        part = slice(t * deep, (t + 1) * deep)
        pairs = [
            (tokens.at[:, part], tok.at[t]),
            (query.at[part, :], wide.at[t]),
            (key.at[part, :], kv.at[t, :, :HD]),
            (value.at[part, :], kv.at[t, :, HD:]),
        ]
        copies.append(fetch(pairs, sems.at[4 * t : 4 * t + 4]))
    far_cols = pl.ds(pl.multiple_of((1 - core) * 512, 512), 512)
    near_cols = pl.ds(pl.multiple_of(core * 512, 512), 512)
    for t in range(4):
        for copy in copies[t]:
            copy.wait()
        a = tok[t]
        far = jnp.dot(a, wide[t, :, far_cols], preferred_element_type=F32)
        near = jnp.dot(a, wide[t, :, near_cols], preferred_element_type=F32)
        new = jnp.dot(a, kv[t], preferred_element_type=F32)
        if t == 0:
            sent[...] = far
            keep[:ROWS, :] = near
            fresh[...] = new
        else:
            keep[:ROWS, :] += near
            fresh[...] += new
            if t == 3:
                send[:ROWS, :] = (sent[...] + far).astype(BF16)
            else:
                sent[...] += far
    for t in range(2):
        cols = slice(t * PAIR, (t + 1) * PAIR)
        far_rows = pl.ds(pl.multiple_of((1 - core) * 128 + t * NEW, NEW), NEW)
        near_rows = pl.ds(pl.multiple_of(core * 128 + t * NEW, NEW), NEW)
        send[ROWS:, cols] = fresh[far_rows, :].astype(BF16)
        keep[ROWS:, cols] = fresh[near_rows, :]


def first(tokens, query, key, value):
    deep = tokens.shape[1] // 4
    return pl.pallas_call(
        first_kernel,
        out_shape=[shaped((320, 512), BF16), shaped((320, 512), F32)],
        in_specs=[HBM] * 4,
        out_specs=[VMEM] * 2,
        scratch_shapes=[
            pltpu.VMEM((4, ROWS, deep), BF16),
            pltpu.VMEM((4, deep, query.shape[1]), BF16),
            pltpu.VMEM((4, deep, PAIR), BF16),
            pltpu.VMEM((ROWS, 512), F32),
            pltpu.VMEM((ROWS, PAIR), F32),
            pltpu.SemaphoreType.DMA((16,)),
        ],
        compiler_params=params(),
        cost_estimate=SMALL,
        name="first",
    )(tokens, query, key, value)


def second_kernel(keep, got, send, onward):
    x = lax.axis_index("hid_0")
    q = keep[:ROWS, :] + got[:ROWS, :].astype(F32)
    send[:ROWS, :] = q.astype(BF16)
    onward[:ROWS, :] = q
    low = keep[ROWS:, :] + got[ROWS:, :].astype(F32)
    sides = [low[:, :PAIR], low[:, PAIR:]]
    sides = [jnp.concatenate([s[:32], s[32:]], axis=1) for s in sides]
    mine = jnp.where(x == 0, sides[0], sides[1])
    other = jnp.where(x == 0, sides[1], sides[0])
    send[ROWS:, :] = other.astype(BF16)
    onward[ROWS:, :] = mine


def second(keep, got):
    return pl.pallas_call(
        second_kernel,
        out_shape=[shaped((288, 512), BF16), shaped((288, 512), F32)],
        in_specs=[VMEM] * 2,
        out_specs=[VMEM] * 2,
        compiler_params=params(8),
        cost_estimate=SMALL,
        name="second",
    )(keep, got)


def new_offset():
    return lax.axis_index("hid_1") * 128 + lax.axis_index("hid_0") * NEW


def rotate_kernel(keep, got, cosine, sine, queries, notes):
    for h in range(4):
        cols = slice(h * HD, (h + 1) * HD)
        u = keep[:ROWS, cols] + got[:ROWS, cols].astype(F32)
        turned = u * cosine[...] + pltpu.roll(u, HD // 2, 1) * sine[...]
        queries[:, cols] = turned.astype(BF16)
    low = keep[ROWS:, :] + got[ROWS:, :].astype(F32)
    low = jnp.concatenate([low[:, :PAIR], low[:, PAIR:]], axis=0)
    rows = pl.ds(pl.multiple_of(new_offset(), NEW), NEW)
    u = low[:, :HD]
    turned = u * cosine[rows, :] + pltpu.roll(u, HD // 2, 1) * sine[rows, :]
    for z in range(8):
        notes[z, :, :HD] = turned.astype(BF16)
        notes[z, :, HD:] = low[:, HD:].astype(BF16)


def rotated(keep, got, cosine, sine):
    return pl.pallas_call(
        rotate_kernel,
        out_shape=[shaped((ROWS, 512), BF16), shaped((8, NEW, PAIR), BF16)],
        in_specs=[VMEM] * 4,
        out_specs=[VMEM] * 2,
        compiler_params=params(8),
        cost_estimate=SMALL,
        name="rotated",
    )(keep, got, cosine, sine)


def gather_visible(mine, slabs, halves, new, keys, values, chunk):
    height = keys.shape[0]
    values[:, HD:] = jnp.ones((height, HD), BF16)
    n = jnp.int32(0)
    lane = lax.broadcasted_iota(jnp.int32, (16, HD), 1)
    marks = jnp.zeros((16, HD), jnp.int32)
    for i, load in enumerate(halves):
        codes = load[ROWS:, :HD].astype(F32)
        codes = jnp.where(lane == 0, 2.0, 1.0) * codes
        place = (codes + pltpu.roll(codes, HD - 1, 1)).astype(jnp.int32)
        marks = marks + jnp.where(place < mine, 1 << i, 0)
    mask = jnp.max(jnp.where(lane == 0, marks, 0))
    bit = 0
    for load in halves:
        seen = ((mask >> bit) & 1) == 1
        bit += 1

        @pl.when(seen)
        def _(load=load, n=n):
            at = pl.ds(pl.multiple_of(n * NEW, NEW), ROWS)
            keys[at, :] = load[:ROWS, :HD]
            values[at, :HD] = load[:ROWS, HD:]

        n = n + jnp.where(seen, ROWS // NEW, 0)
    if new is not None:
        for z in range(8):
            seen = slabs[z] < mine

            @pl.when(seen)
            def _(z=z, n=n):
                at = pl.ds(pl.multiple_of(n * NEW, NEW), NEW)
                keys[at, :] = new[z, :, :HD]
                values[at, :HD] = new[z, :, HD:]

            n = n + jnp.where(seen, 1, 0)
    per = chunk // NEW
    chunks = (n + per - 1) // per

    def pad(t, carry):
        at = pl.ds(pl.multiple_of(t * NEW, NEW), NEW)
        keys[at, :] = keys[:NEW, :]
        values[at, :] = jnp.zeros((NEW, PAIR), BF16)
        return carry

    lax.fori_loop(n, chunks * per, pad, 0)
    return chunks


def attend(q, peak_ref, chunks, keys, values, scores, chunk, acc_at, before):
    def peaks(i, carry):
        at = pl.ds(pl.multiple_of(i * chunk, chunk), chunk)
        s = lax.dot_general(q, keys[at, :], CONTRACT, preferred_element_type=F32)
        scores[i] = s
        best = peak_ref[...]
        for t in range(chunk // HD):
            best = jnp.maximum(best, s[:, t * HD : (t + 1) * HD])
        peak_ref[...] = best
        return carry

    lax.fori_loop(0, chunks, peaks, 0)
    peak = jnp.max(peak_ref[...], axis=1, keepdims=True)
    acc_at[...] = before(peak)

    def weigh(i, carry):
        at = pl.ds(pl.multiple_of(i * chunk, chunk), chunk)
        p = jnp.exp2((scores[i] - peak) * EXPONENT).astype(BF16)
        acc_at[...] += jnp.dot(p, values[at, :], preferred_element_type=F32)
        return carry

    lax.fori_loop(0, chunks, weigh, 0)
    return peak


def halves_of(buffers):
    halves = []
    for ref in buffers:
        for b in range(ref.shape[0] // HALF):
            halves.append(ref.at[b * HALF : (b + 1) * HALF, :])
    return halves


def near_kernel(slabs, near, far, notes, *refs, chunk, count):
    sources, (q_out, acc_out, peak_out) = refs[:count], refs[count : count + 3]
    refs = refs[count + 3 :]
    near_in, far_in, own, *loads = refs[: 3 + count]
    q_all, acc_all, peak_all, keys, values, scores, peak_ref, acc, sems = refs[3 + count :]
    pairs = [(sources[0].at[: 2 * HALF, :], loads[0])] + list(zip(sources[1:], loads[1:]))
    pairs += [(notes.at[0], own), (near, near_in), (far, far_in)]
    copies = fetch(pairs, sems.at[: count + 3])
    mine = slabs[lax.axis_index("key")]
    core = lax.axis_index("hid_1")
    x = lax.axis_index("hid_0")
    for copy in copies[:count]:
        copy.wait()
    chunks = gather_visible(mine, None, halves_of(loads), None, keys, values, chunk)
    for copy in copies[count:]:
        copy.wait()
    for j in range(4):
        half = x if j < 2 else 1 - x
        parity = core if j % 2 == 0 else 1 - core
        cols = pl.ds(pl.multiple_of(parity * PAIR, PAIR), PAIR)
        rows = [slice((2 * j + t) * ROWS, (2 * j + t + 1) * ROWS) for t in range(2)]

        @pl.when(half == core)
        def _(cols=cols, rows=rows):
            both = near_in[:, cols]
            q_all[rows[0], :] = both[:, :HD]
            q_all[rows[1], :] = both[:, HD:]

        @pl.when(half != core)
        def _(cols=cols, rows=rows):
            both = far_in[:, cols]
            q_all[rows[0], :] = both[:, :HD]
            q_all[rows[1], :] = both[:, HD:]

    out = fetch([(q_all, q_out)], sems.at[count + 3 : count + 4])
    zeros = jnp.zeros((NEW, HD), BF16)
    own_keys = jnp.concatenate([own[:, :HD], zeros], axis=0)
    own_values = jnp.concatenate([own[:, HD:], zeros], axis=0)
    own_values = jnp.concatenate([own_values, jnp.ones((HD, HD), BF16)], axis=1)
    row = lax.broadcasted_iota(jnp.int32, (TALL, HD), 0) % ROWS
    lane = lax.broadcasted_iota(jnp.int32, (TALL, HD), 1)
    visible = jnp.logical_and(lane < NEW, lane + new_offset() <= row)
    for step in range(8 * ROWS // TALL):
        at = pl.ds(step * TALL, TALL)
        q = q_all[at, :]
        s = lax.dot_general(q, own_keys, CONTRACT, preferred_element_type=F32)
        s = jnp.where(visible, s, NEGATIVE)
        peak_ref[...] = s

        def before(peak, s=s):
            p = jnp.where(visible, jnp.exp2((s - peak) * EXPONENT), 0.0)
            return jnp.dot(p.astype(BF16), own_values, preferred_element_type=F32)

        peak = attend(
            q, peak_ref, chunks, keys, values, scores, chunk, acc, before
        )
        acc_all[at, :] = acc[:, :HD]
        peak_all[at, :] = jnp.where(lane < HD // 2, peak, acc[:, HD:])
        first_sem = count + 4 + 2 * step
        out += fetch(
            [
                (acc_all.at[at, :], acc_out.at[at, :]),
                (peak_all.at[at, :], peak_out.at[at, :]),
            ],
            sems.at[first_sem : first_sem + 2],
        )
    for copy in out:
        copy.wait()


def attend_near(slabs, near, far, notes, loads):
    count, chunk = len(loads), 1280
    shapes = [(2 * HALF, PAIR)] + [a.shape for a in loads[1:]]
    height = sum(shape[0] // HALF * ROWS for shape in shapes)
    state = [((8 * ROWS, HD), BF16), ((8 * ROWS, HD), F32), ((8 * ROWS, HD), F32)]
    return pl.pallas_call(
        functools.partial(near_kernel, chunk=chunk, count=count),
        out_shape=[shaped(*s) for s in state],
        in_specs=[SMEM] + [HBM] * (3 + count),
        out_specs=[HBM] * 3,
        scratch_shapes=[
            pltpu.VMEM((ROWS, 4 * HD), BF16),
            pltpu.VMEM((ROWS, 4 * HD), BF16),
            pltpu.VMEM((NEW, PAIR), BF16),
            *[pltpu.VMEM(shape, BF16) for shape in shapes],
            *[pltpu.VMEM(*s) for s in state],
            pltpu.VMEM((height, HD), BF16),
            pltpu.VMEM((height, PAIR), BF16),
            pltpu.VMEM((height // chunk, TALL, chunk), F32),
            pltpu.VMEM((TALL, HD), F32),
            pltpu.VMEM((TALL, PAIR), F32),
            pltpu.SemaphoreType.DMA((count + 4 + 2 * (8 * ROWS // TALL),)),
        ],
        compiler_params=params(),
        cost_estimate=SMALL,
        name="near",
    )(slabs, near, far, notes, *loads)


def far_kernel(slabs, *refs, chunk, count):
    sources, outs = refs[: 4 + count], refs[4 + count : 7 + count]
    refs = refs[7 + count :]
    core = lax.axis_index("hid_1")
    outs = [outs[0].at[core], outs[0].at[1 - core], outs[1], outs[2]]
    buffers = refs[: 4 + count]
    queries, acc_in, peak_in, new, *loads = buffers
    keys, values, scores, peak_ref, acc, sems = refs[4 + count :]
    tall = 8 * ROWS
    copies = fetch(list(zip(sources, buffers))[::-1], sems)
    mine = slabs[lax.axis_index("key")]
    for copy in copies[: count + 1]:
        copy.wait()
    chunks = gather_visible(mine, slabs, halves_of(loads), new, keys, values, chunk)
    for copy in copies[count + 1 :]:
        copy.wait()
    peak_ref[...] = jnp.broadcast_to(peak_in[:, :1], (tall, HD))

    def before(peak):
        factor = jnp.exp2((peak_in[:, :1] - peak) * EXPONENT)
        total = jnp.broadcast_to(peak_in[:, HD // 2 : HD // 2 + 1], (tall, HD))
        return jnp.concatenate([acc_in[...], total], axis=1) * factor

    peak = attend(
        queries[...], peak_ref, chunks, keys, values, scores, chunk, acc, before
    )
    total = acc[:, HD:]
    heads = (acc[:, :HD] / jnp.where(total > 0.0, total, 1.0)).astype(BF16)
    lane = lax.broadcasted_iota(jnp.int32, (ROWS, HD), 1)
    totals = jnp.zeros((ROWS, HD), F32)
    peaks = jnp.zeros((ROWS, HD), F32)
    for h in range(tall // ROWS):
        rows = slice(h * ROWS, (h + 1) * ROWS)
        totals = jnp.where(lane == h, total[rows], totals)
        peaks = jnp.where(lane == h, peak[rows], peaks)
    some = totals > 0.0
    level = peaks * EXPONENT + jnp.log2(jnp.where(some, totals, 1.0))
    level = jnp.transpose(jnp.where(some, level, NEGATIVE))
    where = lax.broadcasted_iota(jnp.int32, (16, ROWS), 0)
    for t in range(tall // (2 * ROWS)):
        out = outs[t]
        table = jnp.zeros((16, ROWS), F32)
        for half in range(2):
            h = 2 * t + half
            cols = slice(half * HD, (half + 1) * HD)
            out[:ROWS, cols] = heads[h * ROWS : (h + 1) * ROWS]
            rest = level[h : h + 1, :]
            for k in range(3):
                coded = rest.astype(BF16).astype(F32)
                table = jnp.where(where == 3 * half + k, coded, table)
                rest = rest - coded
        out[ROWS:, :] = table.astype(BF16)


def attend_far(slabs, queries, acc, peak, new, loads):
    operands = [queries, acc, peak, new, *loads]
    count, chunk = len(loads), 1024
    height = sum(a.shape[0] // HALF * ROWS for a in loads) + 8 * NEW
    height = -(-height // chunk) * chunk
    tall = 8 * ROWS
    return pl.pallas_call(
        functools.partial(far_kernel, chunk=chunk, count=count),
        out_shape=[shaped((2, MSG, PAIR), BF16)] + [shaped((MSG, PAIR), BF16)] * 2,
        in_specs=[SMEM] + [HBM] * len(operands),
        out_specs=[VMEM] * 3,
        scratch_shapes=[
            *[pltpu.VMEM(a.shape, a.dtype) for a in operands],
            pltpu.VMEM((height, HD), BF16),
            pltpu.VMEM((height, PAIR), BF16),
            pltpu.VMEM((height // chunk, tall, chunk), F32),
            pltpu.VMEM((tall, HD), F32),
            pltpu.VMEM((tall, PAIR), F32),
            pltpu.SemaphoreType.DMA((len(operands),)),
        ],
        compiler_params=params(),
        cost_estimate=MEDIUM,
        name="far",
    )(slabs, *operands)


def merge_kernel(pair, straight, across, out):
    parts = [pair.at[0], pair.at[1], straight, across]
    levels = []
    for ref in parts:
        t = ref[ROWS:, :].astype(F32)
        levels.append([t[0:1] + t[1:2] + t[2:3], t[3:4] + t[4:5] + t[5:6]])
    rows = []
    for half in range(2):
        top = functools.reduce(jnp.maximum, [lv[half] for lv in levels])
        w = [jnp.exp2(lv[half] - top) for lv in levels]
        total = w[0] + w[1] + w[2] + w[3]
        rows.extend([x / total for x in w])
    table = jnp.concatenate(rows, axis=0)
    table = jnp.transpose(jnp.concatenate([table, jnp.zeros((HD - 8, ROWS), F32)], axis=0))
    for half in range(2):
        cols = slice(half * HD, (half + 1) * HD)
        so_far = None
        for t, ref in enumerate(parts):
            w = table[:, half * 4 + t : half * 4 + t + 1]
            term = ref[:ROWS, cols].astype(F32) * w
            so_far = term if so_far is None else so_far + term
        out[:, cols] = so_far.astype(BF16)


def merge(parts):
    return pl.pallas_call(
        merge_kernel,
        out_shape=shaped((ROWS, PAIR), BF16),
        in_specs=[VMEM] * 3,
        out_specs=VMEM,
        compiler_params=params(8),
        cost_estimate=SMALL,
        name="merge",
    )(*parts)


def project_kernel(*refs):
    heads, weights, send, keep = refs[:4], refs[4:8], refs[8], refs[9]
    core = lax.axis_index("hid_1")
    h = jnp.concatenate([ref[...] for ref in heads], axis=1)
    for out, side in ((send, 1 - core), (keep, core)):
        for t in range(4):
            cols = pl.ds(pl.multiple_of(t * 512 + side * ROWS, ROWS), ROWS)
            w = jnp.concatenate([ref[:, cols] for ref in weights], axis=0)
            total = jnp.dot(h, w, preferred_element_type=F32)
            out[:, t * ROWS : (t + 1) * ROWS] = total.astype(out.dtype)


def project(heads, weights):
    width = weights[0].shape[1]
    return pl.pallas_call(
        project_kernel,
        out_shape=[shaped((ROWS, width // 2), BF16), shaped((ROWS, width // 2), F32)],
        in_specs=[VMEM] * 8,
        out_specs=[VMEM] * 2,
        compiler_params=params(16),
        cost_estimate=SMALL,
        name="project",
    )(*heads, *weights)


def split_kernel(keep, got, own, *sends):
    spot = 2 * lax.axis_index("head_0") + lax.axis_index("hid_0")
    for by in range(4):
        cols = pl.ds(pl.multiple_of(lax.rem(spot + by, 4) * ROWS, ROWS), ROWS)
        total = keep[:, cols] + got[:, cols].astype(F32)
        if by == 0:
            own[...] = total
        else:
            sends[by - 1][...] = total.astype(BF16)


def split(keep, got):
    return pl.pallas_call(
        split_kernel,
        out_shape=[shaped((ROWS, ROWS), F32)] + [shaped((ROWS, ROWS), BF16)] * 3,
        in_specs=[VMEM] * 2,
        out_specs=[VMEM] * 4,
        compiler_params=params(8),
        cost_estimate=SMALL,
        name="split",
    )(keep, got)


def body(
    tokens,
    query_weight,
    key_weight,
    value_weight,
    output_weight,
    key_cache,
    value_cache,
    cache_places,
    slab_places,
):

    load, spots = pack(
        cache_places, slab_places, key_cache.reshape(-1, HD), value_cache.reshape(-1, HD)
    )

    def away(array, by):
        pairs = []
        for k in range(8):
            pairs.append((2 * k, 2 * ((k + by) % 8)))
            pairs.append((2 * k + 1, 2 * ((k - by) % 8) + 1))
        return lax.ppermute(array, ("key", "hid_1"), pairs)

    one = away(load, 1)

    pieces = columns(output_weight)

    send, keep = first(tokens, query_weight, key_weight, value_weight)
    one, keep, pieces = lax.optimization_barrier((one, keep, pieces))
    two = away(one, 1)
    send, keep = second(keep, swap(send, "hid_1"))
    keep, pieces = lax.optimization_barrier((keep, pieces))
    got = swap(send, "hid_0")
    weights = [pieces[3]]
    for piece, by in zip(pieces, (2, 1, 3)):
        weights.append(lax.ppermute(piece, "head_1", shift(4, by)))

    middle = HD // 2
    index = np.arange(HD) % middle
    frequency = jnp.exp(jnp.asarray(index, F32) * (-2.0 * math.log(THETA) / HD))
    sign = np.where(np.arange(HD) < middle, -1.0, 1.0).astype(np.float32)
    angles = spots * frequency[None, :]
    cosine, sine = jnp.cos(angles), jnp.sin(angles) * sign[None, :]
    queries, notes = rotated(keep, got, cosine, sine)
    two, queries = lax.optimization_barrier((two, queries))
    three = away(two, 1)
    far = swap(queries, "hid_1")
    far, onward = lax.optimization_barrier((far, two[: 2 * HALF]))
    four = away(onward, 2)

    new = lax.all_to_all(notes, "key", split_axis=0, concat_axis=0, tiled=True)

    state = attend_near(slab_places, queries, far, notes, [load, one, two])
    pair, straight, across = attend_far(slab_places, *state, new, [three, four])
    parts = [
        lax.all_to_all(pair, "hid_1", split_axis=0, concat_axis=0, tiled=True),
        swap(straight, "hid_0"),
        lax.ppermute(across, HID, [(0, 3), (1, 2), (2, 1), (3, 0)]),
    ]
    parts, weights[2:] = lax.optimization_barrier((parts, weights[2:]))
    merged = merge(parts)

    heads = [merged] + [lax.ppermute(merged, "head_1", shift(4, by)) for by in (2, 1, 3)]
    send, keep = project(heads, weights)
    own, *blocks = split(keep, swap(send, "hid_1"))
    out = own
    for by in (2, 1, 3):
        out = out + lax.ppermute(blocks[by - 1], ALONG_X, shift(4, by)).astype(F32)
    return out.astype(BF16)


def solution(mesh):
    finer = Mesh(
        mesh.devices.reshape(2, 4, mesh.shape["key"], 2, 2),
        ("head_0", "head_1", "key", "hid_0", "hid_1"),
    )
    return jax.shard_map(
        body,
        mesh=finer,
        in_specs=(
            P("key", HID),
            P(HID, HEAD),
            P(HID, HEAD),
            P(HID, HEAD),
            P(HEAD_HID, None),
            P("key", HEAD, None),
            P("key", HEAD, None),
            P("key"),
            P(),
        ),
        out_specs=P("key", HEAD_HID),
        check_vma=False,
    )
```

```python
import functools
import math

import jax
import jax.numpy as jnp
import numpy as np
from jax import lax
from jax.experimental import pallas as pl
from jax.experimental.pallas import tpu as pltpu
from jax.sharding import Mesh
from jax.sharding import PartitionSpec as P

HID = ("hid_0", "hid_1")
HEAD = ("head_0", "head_1")
HEAD_HID = ("head_0", "head_1", "hid_0", "hid_1")
ALONG_X = ("head_0", "hid_0")

THETA = 500000.0
NEGATIVE = -1e30
BF16 = jnp.bfloat16
F32 = jnp.float32

ROWS = 256
HD = 128
PAIR = 2 * HD
NEW = 64
QUARTER = 512
HALF = ROWS + 16
LOAD = 4 * HALF
MSG = ROWS + 16
TALL = 2048
EXPONENT = math.log2(math.e) / math.sqrt(HD)
CONTRACT = (((1,), (1,)), ((), ()))

VMEM = pl.BlockSpec(memory_space=pltpu.VMEM)
SMEM = pl.BlockSpec(memory_space=pltpu.SMEM)
HBM = pl.BlockSpec(memory_space=pltpu.HBM)


def shaped(shape, dtype):
    return jax.ShapeDtypeStruct(shape, dtype)


def params(mib=60):
    return pltpu.CompilerParams(vmem_limit_bytes=mib * 2**20)


SMALL = pl.CostEstimate(flops=1, bytes_accessed=1, transcendentals=0)
MEDIUM = pl.CostEstimate(flops=2**30, bytes_accessed=2**18, transcendentals=2**10)


def shift(n, by):
    return [(i, (i + by) % n) for i in range(n)]


def swap(array, axis):
    return lax.ppermute(array, axis, shift(2, 1))


def hid_index():
    return 2 * lax.axis_index("hid_0") + lax.axis_index("hid_1")


def fetch(pairs, sems):
    copies = [
        pltpu.make_async_copy(source, target, sems.at[i])
        for i, (source, target) in enumerate(pairs)
    ]
    for copy in copies:
        copy.start()
    return copies


def pack_kernel(places, slabs, keys, values, out, spots, load, sems):
    core = lax.axis_index("hid_1")
    lane = lax.broadcasted_iota(jnp.int32, (16, PAIR), 1)
    pairs = []
    for i in range(4):
        block = 4 * lax.axis_index("hid_0") + lax.rem(2 * core + i, 4)
        rows = pl.ds(pl.multiple_of(block * ROWS, ROWS), ROWS)
        to = slice(i * HALF, i * HALF + ROWS)
        pairs.append((keys.at[rows, :], load.at[to, :HD]))
        pairs.append((values.at[rows, :], load.at[to, HD:]))
        place = places[block]
        table = jnp.where(lane == 0, place >> 1, jnp.where(lane == 1, place & 1, 0))
        load[i * HALF + ROWS : (i + 1) * HALF, :] = table.astype(F32).astype(BF16)
    copies = fetch(pairs, sems.at[:8])
    leaving = []
    for i in range(4):
        copies[2 * i].wait()
        copies[2 * i + 1].wait()
        to = slice(i * HALF, (i + 1) * HALF)
        leaving += fetch([(load.at[to, :], out.at[to, :])], sems.at[8 + i : 9 + i])
    row = lax.broadcasted_iota(jnp.int32, (ROWS, HD), 0)
    spots[...] = (slabs[lax.axis_index("key")] * ROWS + row).astype(F32)
    for copy in leaving:
        copy.wait()


def pack(places, slabs, keys, values):
    return pl.pallas_call(
        pack_kernel,
        out_shape=[shaped((LOAD, PAIR), BF16), shaped((ROWS, HD), F32)],
        in_specs=[SMEM, SMEM, HBM, HBM],
        out_specs=[HBM, VMEM],
        scratch_shapes=[pltpu.VMEM((LOAD, PAIR), BF16), pltpu.SemaphoreType.DMA((12,))],
        compiler_params=params(),
        cost_estimate=SMALL,
        name="pack",
    )(places, slabs, keys, values)


def columns_kernel(weight, *refs):
    outs, pieces, sems, out_sems = refs[:4], refs[4], refs[5], refs[6]
    y = lax.axis_index("head_1")
    pairs = []
    for t, by in enumerate((2, 1, 3, 0)):
        at = lax.rem(y + by, 4) * 1024
        for hi in range(2):
            source = pl.ds(pl.multiple_of(hi * 4096 + at, 1024), 1024)
            pairs.append((weight.at[:, source], pieces.at[t, :, hi * 1024 : (hi + 1) * 1024]))
    copies = fetch(pairs, sems)
    leaving = []
    for t in range(4):
        copies[2 * t].wait()
        copies[2 * t + 1].wait()
        leaving += fetch([(pieces.at[t], outs[t])], out_sems.at[t : t + 1])
    for copy in leaving:
        copy.wait()


def columns(weight):
    return pl.pallas_call(
        columns_kernel,
        out_shape=[shaped((ROWS, 2048), BF16)] * 4,
        in_specs=[HBM],
        out_specs=[HBM] * 4,
        scratch_shapes=[
            pltpu.VMEM((4, ROWS, 2048), BF16),
            pltpu.SemaphoreType.DMA((8,)),
            pltpu.SemaphoreType.DMA((4,)),
        ],
        compiler_params=params(),
        cost_estimate=SMALL,
        name="columns",
    )(weight)


def first_kernel(tokens, query, key, value, send, keep, tok, wide, kv, sent, fresh, sems):
    core = lax.axis_index("hid_1")
    deep = tok.shape[2]
    copies = []
    for t in range(4):
        part = slice(t * deep, (t + 1) * deep)
        pairs = [
            (tokens.at[:, part], tok.at[t]),
            (query.at[part, :], wide.at[t]),
            (key.at[part, :], kv.at[t, :, :HD]),
            (value.at[part, :], kv.at[t, :, HD:]),
        ]
        copies.append(fetch(pairs, sems.at[4 * t : 4 * t + 4]))
    far_cols = pl.ds(pl.multiple_of((1 - core) * 512, 512), 512)
    near_cols = pl.ds(pl.multiple_of(core * 512, 512), 512)
    for t in range(4):
        for copy in copies[t]:
            copy.wait()
        a = tok[t]
        far = jnp.dot(a, wide[t, :, far_cols], preferred_element_type=F32)
        near = jnp.dot(a, wide[t, :, near_cols], preferred_element_type=F32)
        new = jnp.dot(a, kv[t], preferred_element_type=F32)
        if t == 0:
            sent[...] = far
            keep[:ROWS, :] = near
            fresh[...] = new
        else:
            keep[:ROWS, :] += near
            fresh[...] += new
            if t == 3:
                send[:ROWS, :] = (sent[...] + far).astype(BF16)
            else:
                sent[...] += far
    for t in range(2):
        cols = slice(t * PAIR, (t + 1) * PAIR)
        far_rows = pl.ds(pl.multiple_of((1 - core) * 128 + t * NEW, NEW), NEW)
        near_rows = pl.ds(pl.multiple_of(core * 128 + t * NEW, NEW), NEW)
        send[ROWS:, cols] = fresh[far_rows, :].astype(BF16)
        keep[ROWS:, cols] = fresh[near_rows, :]


def first(tokens, query, key, value):
    deep = tokens.shape[1] // 4
    return pl.pallas_call(
        first_kernel,
        out_shape=[shaped((320, 512), BF16), shaped((320, 512), F32)],
        in_specs=[HBM] * 4,
        out_specs=[VMEM] * 2,
        scratch_shapes=[
            pltpu.VMEM((4, ROWS, deep), BF16),
            pltpu.VMEM((4, deep, query.shape[1]), BF16),
            pltpu.VMEM((4, deep, PAIR), BF16),
            pltpu.VMEM((ROWS, 512), F32),
            pltpu.VMEM((ROWS, PAIR), F32),
            pltpu.SemaphoreType.DMA((16,)),
        ],
        compiler_params=params(),
        cost_estimate=SMALL,
        name="first",
    )(tokens, query, key, value)


def second_kernel(keep, got, send, onward):
    x = lax.axis_index("hid_0")
    q = keep[:ROWS, :] + got[:ROWS, :].astype(F32)
    send[:ROWS, :] = q.astype(BF16)
    onward[:ROWS, :] = q
    low = keep[ROWS:, :] + got[ROWS:, :].astype(F32)
    sides = [low[:, :PAIR], low[:, PAIR:]]
    sides = [jnp.concatenate([s[:32], s[32:]], axis=1) for s in sides]
    mine = jnp.where(x == 0, sides[0], sides[1])
    other = jnp.where(x == 0, sides[1], sides[0])
    send[ROWS:, :] = other.astype(BF16)
    onward[ROWS:, :] = mine


def second(keep, got):
    return pl.pallas_call(
        second_kernel,
        out_shape=[shaped((288, 512), BF16), shaped((288, 512), F32)],
        in_specs=[VMEM] * 2,
        out_specs=[VMEM] * 2,
        compiler_params=params(8),
        cost_estimate=SMALL,
        name="second",
    )(keep, got)


def new_offset():
    return lax.axis_index("hid_1") * 128 + lax.axis_index("hid_0") * NEW


def rotate_kernel(keep, got, cosine, sine, queries, notes):
    for h in range(4):
        cols = slice(h * HD, (h + 1) * HD)
        u = keep[:ROWS, cols] + got[:ROWS, cols].astype(F32)
        turned = u * cosine[...] + pltpu.roll(u, HD // 2, 1) * sine[...]
        queries[:, cols] = turned.astype(BF16)
    low = keep[ROWS:, :] + got[ROWS:, :].astype(F32)
    low = jnp.concatenate([low[:, :PAIR], low[:, PAIR:]], axis=0)
    rows = pl.ds(pl.multiple_of(new_offset(), NEW), NEW)
    u = low[:, :HD]
    turned = u * cosine[rows, :] + pltpu.roll(u, HD // 2, 1) * sine[rows, :]
    for z in range(8):
        notes[z, :, :HD] = turned.astype(BF16)
        notes[z, :, HD:] = low[:, HD:].astype(BF16)


def rotated(keep, got, cosine, sine):
    return pl.pallas_call(
        rotate_kernel,
        out_shape=[shaped((ROWS, 512), BF16), shaped((8, NEW, PAIR), BF16)],
        in_specs=[VMEM] * 4,
        out_specs=[VMEM] * 2,
        compiler_params=params(8),
        cost_estimate=SMALL,
        name="rotated",
    )(keep, got, cosine, sine)


def gather_visible(mine, slabs, halves, new, keys, values, chunk):
    height = keys.shape[0]
    values[:, HD:] = jnp.ones((height, HD), BF16)
    n = jnp.int32(0)
    lane = lax.broadcasted_iota(jnp.int32, (16, HD), 1)
    marks = jnp.zeros((16, HD), jnp.int32)
    for i, load in enumerate(halves):
        codes = load[ROWS:, :HD].astype(F32)
        codes = jnp.where(lane == 0, 2.0, 1.0) * codes
        place = (codes + pltpu.roll(codes, HD - 1, 1)).astype(jnp.int32)
        marks = marks + jnp.where(place < mine, 1 << i, 0)
    mask = jnp.max(jnp.where(lane == 0, marks, 0))
    bit = 0
    for load in halves:
        seen = ((mask >> bit) & 1) == 1
        bit += 1

        @pl.when(seen)
        def _(load=load, n=n):
            at = pl.ds(pl.multiple_of(n * NEW, NEW), ROWS)
            keys[at, :] = load[:ROWS, :HD]
            values[at, :HD] = load[:ROWS, HD:]

        n = n + jnp.where(seen, ROWS // NEW, 0)
    if new is not None:
        for z in range(8):
            seen = slabs[z] < mine

            @pl.when(seen)
            def _(z=z, n=n):
                at = pl.ds(pl.multiple_of(n * NEW, NEW), NEW)
                keys[at, :] = new[z, :, :HD]
                values[at, :HD] = new[z, :, HD:]

            n = n + jnp.where(seen, 1, 0)
    per = chunk // NEW
    chunks = (n + per - 1) // per

    def pad(t, carry):
        at = pl.ds(pl.multiple_of(t * NEW, NEW), NEW)
        keys[at, :] = keys[:NEW, :]
        values[at, :] = jnp.zeros((NEW, PAIR), BF16)
        return carry

    lax.fori_loop(n, chunks * per, pad, 0)
    return chunks


def attend(q, peak_ref, chunks, keys, values, scores, chunk, acc_at, before):
    def peaks(i, carry):
        at = pl.ds(pl.multiple_of(i * chunk, chunk), chunk)
        s = lax.dot_general(q, keys[at, :], CONTRACT, preferred_element_type=F32)
        scores[i] = s
        best = peak_ref[...]
        for t in range(chunk // HD):
            best = jnp.maximum(best, s[:, t * HD : (t + 1) * HD])
        peak_ref[...] = best
        return carry

    lax.fori_loop(0, chunks, peaks, 0)
    peak = jnp.max(peak_ref[...], axis=1, keepdims=True)
    acc_at[...] = before(peak)

    def weigh(i, carry):
        at = pl.ds(pl.multiple_of(i * chunk, chunk), chunk)
        p = jnp.exp2((scores[i] - peak) * EXPONENT).astype(BF16)
        acc_at[...] += jnp.dot(p, values[at, :], preferred_element_type=F32)
        return carry

    lax.fori_loop(0, chunks, weigh, 0)
    return peak


def halves_of(buffers):
    halves = []
    for ref in buffers:
        for b in range(ref.shape[0] // HALF):
            halves.append(ref.at[b * HALF : (b + 1) * HALF, :])
    return halves


def near_kernel(slabs, near, far, notes, *refs, chunk, count):
    sources, (q_out, acc_out, peak_out) = refs[:count], refs[count : count + 3]
    refs = refs[count + 3 :]
    near_in, far_in, own, *loads = refs[: 3 + count]
    q_all, acc_all, peak_all, keys, values, scores, peak_ref, acc, sems = refs[3 + count :]
    pairs = [(sources[0].at[: 2 * HALF, :], loads[0])] + list(zip(sources[1:], loads[1:]))
    pairs += [(notes.at[0], own), (near, near_in), (far, far_in)]
    copies = fetch(pairs, sems.at[: count + 3])
    mine = slabs[lax.axis_index("key")]
    core = lax.axis_index("hid_1")
    x = lax.axis_index("hid_0")
    for copy in copies[:count]:
        copy.wait()
    chunks = gather_visible(mine, None, halves_of(loads), None, keys, values, chunk)
    for copy in copies[count:]:
        copy.wait()
    for j in range(4):
        half = x if j < 2 else 1 - x
        parity = core if j % 2 == 0 else 1 - core
        cols = pl.ds(pl.multiple_of(parity * PAIR, PAIR), PAIR)
        rows = [slice((2 * j + t) * ROWS, (2 * j + t + 1) * ROWS) for t in range(2)]

        @pl.when(half == core)
        def _(cols=cols, rows=rows):
            both = near_in[:, cols]
            q_all[rows[0], :] = both[:, :HD]
            q_all[rows[1], :] = both[:, HD:]

        @pl.when(half != core)
        def _(cols=cols, rows=rows):
            both = far_in[:, cols]
            q_all[rows[0], :] = both[:, :HD]
            q_all[rows[1], :] = both[:, HD:]

    out = fetch([(q_all, q_out)], sems.at[count + 3 : count + 4])
    zeros = jnp.zeros((NEW, HD), BF16)
    own_keys = jnp.concatenate([own[:, :HD], zeros], axis=0)
    own_values = jnp.concatenate([own[:, HD:], zeros], axis=0)
    own_values = jnp.concatenate([own_values, jnp.ones((HD, HD), BF16)], axis=1)
    row = lax.broadcasted_iota(jnp.int32, (TALL, HD), 0) % ROWS
    lane = lax.broadcasted_iota(jnp.int32, (TALL, HD), 1)
    visible = jnp.logical_and(lane < NEW, lane + new_offset() <= row)
    for step in range(8 * ROWS // TALL):
        at = pl.ds(step * TALL, TALL)
        q = q_all[at, :]
        s = lax.dot_general(q, own_keys, CONTRACT, preferred_element_type=F32)
        s = jnp.where(visible, s, NEGATIVE)
        peak_ref[...] = s

        def before(peak, s=s):
            p = jnp.where(visible, jnp.exp2((s - peak) * EXPONENT), 0.0)
            return jnp.dot(p.astype(BF16), own_values, preferred_element_type=F32)

        peak = attend(
            q, peak_ref, chunks, keys, values, scores, chunk, acc, before
        )
        acc_all[at, :] = acc[:, :HD]
        peak_all[at, :] = jnp.where(lane < HD // 2, peak, acc[:, HD:])
        first_sem = count + 4 + 2 * step
        out += fetch(
            [
                (acc_all.at[at, :], acc_out.at[at, :]),
                (peak_all.at[at, :], peak_out.at[at, :]),
            ],
            sems.at[first_sem : first_sem + 2],
        )
    for copy in out:
        copy.wait()


def attend_near(slabs, near, far, notes, loads):
    count, chunk = len(loads), 1280
    shapes = [(2 * HALF, PAIR)] + [a.shape for a in loads[1:]]
    height = sum(shape[0] // HALF * ROWS for shape in shapes)
    state = [((8 * ROWS, HD), BF16), ((8 * ROWS, HD), F32), ((8 * ROWS, HD), F32)]
    return pl.pallas_call(
        functools.partial(near_kernel, chunk=chunk, count=count),
        out_shape=[shaped(*s) for s in state],
        in_specs=[SMEM] + [HBM] * (3 + count),
        out_specs=[HBM] * 3,
        scratch_shapes=[
            pltpu.VMEM((ROWS, 4 * HD), BF16),
            pltpu.VMEM((ROWS, 4 * HD), BF16),
            pltpu.VMEM((NEW, PAIR), BF16),
            *[pltpu.VMEM(shape, BF16) for shape in shapes],
            *[pltpu.VMEM(*s) for s in state],
            pltpu.VMEM((height, HD), BF16),
            pltpu.VMEM((height, PAIR), BF16),
            pltpu.VMEM((height // chunk, TALL, chunk), F32),
            pltpu.VMEM((TALL, HD), F32),
            pltpu.VMEM((TALL, PAIR), F32),
            pltpu.SemaphoreType.DMA((count + 4 + 2 * (8 * ROWS // TALL),)),
        ],
        compiler_params=params(),
        cost_estimate=SMALL,
        name="near",
    )(slabs, near, far, notes, *loads)


def far_kernel(slabs, *refs, chunk, count):
    sources, outs = refs[: 4 + count], refs[4 + count : 7 + count]
    refs = refs[7 + count :]
    core = lax.axis_index("hid_1")
    outs = [outs[0].at[core], outs[0].at[1 - core], outs[1], outs[2]]
    buffers = refs[: 4 + count]
    queries, acc_in, peak_in, new, *loads = buffers
    keys, values, scores, peak_ref, acc, sems = refs[4 + count :]
    tall = 8 * ROWS
    copies = fetch(list(zip(sources, buffers))[::-1], sems)
    mine = slabs[lax.axis_index("key")]
    for copy in copies[: count + 1]:
        copy.wait()
    chunks = gather_visible(mine, slabs, halves_of(loads), new, keys, values, chunk)
    for copy in copies[count + 1 :]:
        copy.wait()
    peak_ref[...] = jnp.broadcast_to(peak_in[:, :1], (tall, HD))

    def before(peak):
        factor = jnp.exp2((peak_in[:, :1] - peak) * EXPONENT)
        total = jnp.broadcast_to(peak_in[:, HD // 2 : HD // 2 + 1], (tall, HD))
        return jnp.concatenate([acc_in[...], total], axis=1) * factor

    peak = attend(
        queries[...], peak_ref, chunks, keys, values, scores, chunk, acc, before
    )
    total = acc[:, HD:]
    heads = (acc[:, :HD] / jnp.where(total > 0.0, total, 1.0)).astype(BF16)
    lane = lax.broadcasted_iota(jnp.int32, (ROWS, HD), 1)
    totals = jnp.zeros((ROWS, HD), F32)
    peaks = jnp.zeros((ROWS, HD), F32)
    for h in range(tall // ROWS):
        rows = slice(h * ROWS, (h + 1) * ROWS)
        totals = jnp.where(lane == h, total[rows], totals)
        peaks = jnp.where(lane == h, peak[rows], peaks)
    some = totals > 0.0
    level = peaks * EXPONENT + jnp.log2(jnp.where(some, totals, 1.0))
    level = jnp.transpose(jnp.where(some, level, NEGATIVE))
    where = lax.broadcasted_iota(jnp.int32, (16, ROWS), 0)
    for t in range(tall // (2 * ROWS)):
        out = outs[t]
        table = jnp.zeros((16, ROWS), F32)
        for half in range(2):
            h = 2 * t + half
            cols = slice(half * HD, (half + 1) * HD)
            out[:ROWS, cols] = heads[h * ROWS : (h + 1) * ROWS]
            rest = level[h : h + 1, :]
            for k in range(3):
                coded = rest.astype(BF16).astype(F32)
                table = jnp.where(where == 3 * half + k, coded, table)
                rest = rest - coded
        out[ROWS:, :] = table.astype(BF16)


def attend_far(slabs, queries, acc, peak, new, loads):
    operands = [queries, acc, peak, new, *loads]
    count, chunk = len(loads), 1024
    height = sum(a.shape[0] // HALF * ROWS for a in loads) + 8 * NEW
    height = -(-height // chunk) * chunk
    tall = 8 * ROWS
    return pl.pallas_call(
        functools.partial(far_kernel, chunk=chunk, count=count),
        out_shape=[shaped((2, MSG, PAIR), BF16)] + [shaped((MSG, PAIR), BF16)] * 2,
        in_specs=[SMEM] + [HBM] * len(operands),
        out_specs=[VMEM] * 3,
        scratch_shapes=[
            *[pltpu.VMEM(a.shape, a.dtype) for a in operands],
            pltpu.VMEM((height, HD), BF16),
            pltpu.VMEM((height, PAIR), BF16),
            pltpu.VMEM((height // chunk, tall, chunk), F32),
            pltpu.VMEM((tall, HD), F32),
            pltpu.VMEM((tall, PAIR), F32),
            pltpu.SemaphoreType.DMA((len(operands),)),
        ],
        compiler_params=params(),
        cost_estimate=MEDIUM,
        name="far",
    )(slabs, *operands)


def merge_kernel(pair, straight, across, out):
    parts = [pair.at[0], pair.at[1], straight, across]
    levels = []
    for ref in parts:
        t = ref[ROWS:, :].astype(F32)
        levels.append([t[0:1] + t[1:2] + t[2:3], t[3:4] + t[4:5] + t[5:6]])
    rows = []
    for half in range(2):
        top = functools.reduce(jnp.maximum, [lv[half] for lv in levels])
        w = [jnp.exp2(lv[half] - top) for lv in levels]
        total = w[0] + w[1] + w[2] + w[3]
        rows.extend([x / total for x in w])
    table = jnp.concatenate(rows, axis=0)
    table = jnp.transpose(jnp.concatenate([table, jnp.zeros((HD - 8, ROWS), F32)], axis=0))
    for half in range(2):
        cols = slice(half * HD, (half + 1) * HD)
        so_far = None
        for t, ref in enumerate(parts):
            w = table[:, half * 4 + t : half * 4 + t + 1]
            term = ref[:ROWS, cols].astype(F32) * w
            so_far = term if so_far is None else so_far + term
        out[:, cols] = so_far.astype(BF16)


def merge(parts):
    return pl.pallas_call(
        merge_kernel,
        out_shape=shaped((ROWS, PAIR), BF16),
        in_specs=[VMEM] * 3,
        out_specs=VMEM,
        compiler_params=params(8),
        cost_estimate=SMALL,
        name="merge",
    )(*parts)


def project_kernel(*refs):
    heads, weights, send, keep = refs[:4], refs[4:8], refs[8], refs[9]
    core = lax.axis_index("hid_1")
    h = jnp.concatenate([ref[...] for ref in heads], axis=1)
    for out, side in ((send, 1 - core), (keep, core)):
        for t in range(4):
            cols = pl.ds(pl.multiple_of(t * 512 + side * ROWS, ROWS), ROWS)
            w = jnp.concatenate([ref[:, cols] for ref in weights], axis=0)
            total = jnp.dot(h, w, preferred_element_type=F32)
            out[:, t * ROWS : (t + 1) * ROWS] = total.astype(out.dtype)


def project(heads, weights):
    width = weights[0].shape[1]
    return pl.pallas_call(
        project_kernel,
        out_shape=[shaped((ROWS, width // 2), BF16), shaped((ROWS, width // 2), F32)],
        in_specs=[VMEM] * 8,
        out_specs=[VMEM] * 2,
        compiler_params=params(16),
        cost_estimate=SMALL,
        name="project",
    )(*heads, *weights)


def split_kernel(keep, got, own, *sends):
    spot = 2 * lax.axis_index("head_0") + lax.axis_index("hid_0")
    for by in range(4):
        cols = pl.ds(pl.multiple_of(lax.rem(spot + by, 4) * ROWS, ROWS), ROWS)
        total = keep[:, cols] + got[:, cols].astype(F32)
        if by == 0:
            own[...] = total
        else:
            sends[by - 1][...] = total.astype(BF16)


def split(keep, got):
    return pl.pallas_call(
        split_kernel,
        out_shape=[shaped((ROWS, ROWS), F32)] + [shaped((ROWS, ROWS), BF16)] * 3,
        in_specs=[VMEM] * 2,
        out_specs=[VMEM] * 4,
        compiler_params=params(8),
        cost_estimate=SMALL,
        name="split",
    )(keep, got)


def body(
    tokens,
    query_weight,
    key_weight,
    value_weight,
    output_weight,
    key_cache,
    value_cache,
    cache_places,
    slab_places,
):

    load, spots = pack(
        cache_places, slab_places, key_cache.reshape(-1, HD), value_cache.reshape(-1, HD)
    )

    def away(array, by):
        pairs = []
        for k in range(8):
            pairs.append((2 * k, 2 * ((k + by) % 8)))
            pairs.append((2 * k + 1, 2 * ((k - by) % 8) + 1))
        return lax.ppermute(array, ("key", "hid_1"), pairs)

    one = away(load, 1)

    pieces = columns(output_weight)

    send, keep = first(tokens, query_weight, key_weight, value_weight)
    one, keep, pieces = lax.optimization_barrier((one, keep, pieces))
    two = away(one, 1)
    send, keep = second(keep, swap(send, "hid_1"))
    keep, pieces = lax.optimization_barrier((keep, pieces))
    got = swap(send, "hid_0")
    weights = [pieces[3]]
    for piece, by in zip(pieces, (2, 1, 3)):
        weights.append(lax.ppermute(piece, "head_1", shift(4, by)))

    middle = HD // 2
    index = np.arange(HD) % middle
    frequency = jnp.exp(jnp.asarray(index, F32) * (-2.0 * math.log(THETA) / HD))
    sign = np.where(np.arange(HD) < middle, -1.0, 1.0).astype(np.float32)
    angles = spots * frequency[None, :]
    cosine, sine = jnp.cos(angles), jnp.sin(angles) * sign[None, :]
    queries, notes = rotated(keep, got, cosine, sine)
    two, queries = lax.optimization_barrier((two, queries))
    three = away(two, 1)
    far = swap(queries, "hid_1")
    far, onward = lax.optimization_barrier((far, two[: 2 * HALF]))
    four = away(onward, 2)

    new = lax.all_to_all(notes, "key", split_axis=0, concat_axis=0, tiled=True)

    state = attend_near(slab_places, queries, far, notes, [load, one, two])
    pair, straight, across = attend_far(slab_places, *state, new, [three, four])
    parts = [
        lax.all_to_all(pair, "hid_1", split_axis=0, concat_axis=0, tiled=True),
        swap(straight, "hid_0"),
        lax.ppermute(across, HID, [(0, 3), (1, 2), (2, 1), (3, 0)]),
    ]
    parts, weights[3] = lax.optimization_barrier((parts, weights[3]))
    merged = merge(parts)

    heads = [merged] + [lax.ppermute(merged, "head_1", shift(4, by)) for by in (2, 1, 3)]
    send, keep = project(heads, weights)
    own, *blocks = split(keep, swap(send, "hid_1"))
    out = own
    for by in (2, 1, 3):
        out = out + lax.ppermute(blocks[by - 1], ALONG_X, shift(4, by)).astype(F32)
    return out.astype(BF16)


def solution(mesh):
    finer = Mesh(
        mesh.devices.reshape(2, 4, mesh.shape["key"], 2, 2),
        ("head_0", "head_1", "key", "hid_0", "hid_1"),
    )
    return jax.shard_map(
        body,
        mesh=finer,
        in_specs=(
            P("key", HID),
            P(HID, HEAD),
            P(HID, HEAD),
            P(HID, HEAD),
            P(HEAD_HID, None),
            P("key", HEAD, None),
            P("key", HEAD, None),
            P("key"),
            P(),
        ),
        out_specs=P("key", HEAD_HID),
        check_vma=False,
    )
```
